32 devices in a mesh: dp: 8 (over z, core), expert: 4 (over y, x).
Axes of the slice: x: 2, y: 2, z: 4, core: 2. Of those that a mesh axis runs over, the one named last changes fastest.
Arguments:
- inputs: bfloat16 [8, 1024, 1536], P('dp', 'expert'), may hold values from -6 to 6
- routes: int32 [2, 4, 8, 256, 8], P(None, 'expert', 'dp'), may hold values from 0 to 19, all different within a row; in each aligned block of 256 rows (0 to 255, 256 to 511, ..., all dimensions but the last counted through in order) at most 192 rows name the same one
- cotangent: bfloat16 [8, 1024, 1536], P('dp', 'expert'), may hold values from -6 to 6
- query_weight: bfloat16 [2, 1536, 1536], P(None, ('dp', 'expert')), may hold values from -0.15625 to 0.15625
- key_projection_weight: bfloat16 [2, 1536, 512], P(None, ('dp', 'expert')), may hold values from -0.15625 to 0.15625
- value_projection_weight: bfloat16 [2, 1536, 512], P(None, ('dp', 'expert')), may hold values from -0.15625 to 0.15625
- output_weight: bfloat16 [2, 1536, 1536], P(None, None, ('dp', 'expert')), may hold values from -0.625 to 0.625
- attention_gain: bfloat16 [2, 1536], P(None, ('dp', 'expert')), may hold values from 0.5 to 1.5
- expert_gain: bfloat16 [2, 1536], P(None, ('dp', 'expert')), may hold values from 0.5 to 1.5
- router_weight: bfloat16 [2, 1536, 20], P(None, ('dp', 'expert')), may hold values from -0.078125 to 0.078125
- gate_weight: bfloat16 [2, 20, 1536, 512], P(None, 'expert', 'dp'), may hold values from -0.15625 to 0.15625
- up_weight: bfloat16 [2, 20, 1536, 512], P(None, 'expert', 'dp'), may hold values from -0.15625 to 0.15625
- down_weight: bfloat16 [2, 20, 512, 1536], P(None, 'expert', None, 'dp'), may hold values from -0.75 to 0.75
Outputs:
- result: bfloat16 [8, 1024, 1536], P('dp', 'expert')
- grad_inputs: float32 [8, 1024, 1536], P('dp', 'expert')
- grad_query_weight: float32 [2, 1536, 1536], P(None, ('dp', 'expert'))
- grad_key_weight: float32 [2, 1536, 512], P(None, ('dp', 'expert'))
- grad_value_weight: float32 [2, 1536, 512], P(None, ('dp', 'expert'))
- grad_output_weight: float32 [2, 1536, 1536], P(None, None, ('dp', 'expert'))
- grad_attention_gain: float32 [2, 1536], P(None, ('dp', 'expert'))
- grad_expert_gain: float32 [2, 1536], P(None, ('dp', 'expert'))
- grad_router_weight: float32 [2, 1536, 20], P(None, ('dp', 'expert'))
- grad_gate_weight: float32 [2, 20, 1536, 512], P(None, 'expert', 'dp')
- grad_up_weight: float32 [2, 20, 1536, 512], P(None, 'expert', 'dp')
- grad_down_weight: float32 [2, 20, 512, 1536], P(None, 'expert', None, 'dp')
The draws below stay inside these ranges and needn't reach their ends.
Inputs may be any that keep to these rules, and one draw needn't show every extreme that they name: `routes`: each row names 8 different experts. Over the 256 rows of one device of one layer (one block of positions, the sequences of one dp index), no expert is named more than 192 times, a bound that some block reaches.
All inputs are finite; a program needn't handle non-finite values.
Results may differ from the reference program's by a relative error of at most 0.03.
Values may be sent and summed in bfloat16 or wider, within the bound.
No kernel may reach another device: no remote copies, remote signals or barrier semaphores. Data moves between devices by JAX's collectives and lax.ppermute only.
A program may use at most 448 MiB of HBM per device.

```python
import math
import jax
import jax.numpy as jnp
import numpy as np
from jax import lax

MODEL_DIM = 1536
QUERY_HEADS = 24
KEY_VALUE_HEADS = 8
HEAD_SIZE = 64
FF = 512
TOP = 8
LAYER_COUNT = 2
SEQUENCE_LENGTH = 1024
SEQUENCE_COUNT = 8
BLOCK_LEN = 256
TOK_DEV = 256
EXPERTS = 20
CAP = 192
N_DP = 8
N_EXPERT = 4


def shard_levels(stream_key, extent, split, least, top_value):
    def one(dim, blocks):
        draws = jax.random.uniform(jax.random.fold_in(jax.random.fold_in(stream_key, 6), dim), (blocks,), jnp.float32, least / len(split), top_value / len(split))
        return jnp.repeat(jnp.exp(draws), extent[dim] // blocks).reshape((-1,) + (1,) * (len(extent) - dim - 1))

    level = one(*split[0])
    for cut in split[1:]:
        level = level * one(*cut)
    return level


def assign_block(rng, own, number, rows, amount, top, bound, skew):
    sequence = jax.random.permutation(rng, amount)
    crowded, common = portions_of(amount, rows * top, bound, skew, True), portions_of(amount, rows * top, bound, skew, False)
    places = jnp.arange(amount)

    def named(lengths, offset_by):
        used = int((lengths > 0).sum())
        fixed = max(1, used // 4)
        passed = fixed + (places - fixed + offset_by * (used - fixed)) % max(1, amount - fixed)
        return jnp.zeros((amount,), jnp.int32).at[sequence[jnp.where(places < fixed, places, passed)]].set(jnp.asarray(lengths, jnp.int32))

    lengths = jnp.where(number % 4 == 0, named(crowded, number // 4), named(common, number - number // 4 - 1))
    mixed = jax.random.permutation(jax.random.fold_in(own, 3), amount)
    source_of, sink = mixed[0:amount // 2 * 2:2], mixed[1:amount // 2 * 2:2]
    slack = jnp.minimum(lengths[source_of] - 1, bound - lengths[sink]) // 2
    slack = jnp.where((source_of == sequence[0]) | (sink == sequence[0]) | (lengths[sink] == 0), 0, jnp.maximum(slack, 0))
    passed = jax.random.randint(jax.random.fold_in(own, 4), (amount // 2,), 0, 1 << 20) % (slack + 1)
    lengths = lengths.at[source_of].add(-passed).at[sink].add(passed)
    labels = jnp.searchsorted(jnp.cumsum(lengths), jnp.arange(rows * top), side="right").astype(jnp.int32)
    listing = labels.reshape(top, rows).T
    listing = listing[jax.random.permutation(jax.random.fold_in(own, 1), rows)]
    offset_by = jax.random.randint(jax.random.fold_in(own, 2), (rows, 1), 0, top)
    return jnp.take_along_axis(listing, (jnp.arange(top)[None, :] + offset_by) % top, axis=1)


def portions_of(amount, total, most, slope, full):
    portions = [(1 << 20) // math.isqrt(grade ** slope) + 1 for grade in range(1, amount + 1)]
    largest = most if full else min(most, max(-(-total // amount), total * portions[0] // sum(portions)))
    least = 1 if total - largest >= amount - 1 else 0
    given, spare = [largest] + [least] * (amount - 1), total - largest - least * (amount - 1)
    while spare > 0:
        candidates = [i for i in range(1, amount) if given[i] < largest] or [i for i in range(1, amount) if given[i] < most]
        mass, budget = sum([portions[i] for i in candidates]), spare
        for i in candidates:
            addition = min(most - given[i], max(1, budget * portions[i] // mass), spare)
            given[i] = given[i] + addition
            spare = spare - addition
    return np.array(given)


def scatter_about(stream_key, dims, width, limit, cuts=(), kind=jnp.bfloat16):
    drawn = width * jax.random.normal(stream_key, dims, jnp.float32)
    if cuts:
        drawn = drawn * shard_levels(stream_key, dims, cuts, -0.22, 0.18)
    return jnp.clip(drawn, -limit, limit).astype(kind)


def setup_inputs(seed: int = 0) -> dict:
    key_list = jax.random.split(jax.random.key(seed), 14)
    inputs = scatter_about(key_list[0], (SEQUENCE_COUNT, SEQUENCE_LENGTH, MODEL_DIM), 1.0, 6.0, ((0, 8), (1, 4)))
    routes_keys = jax.random.split(jax.random.fold_in(key_list[1], 1), LAYER_COUNT * (SEQUENCE_LENGTH // BLOCK_LEN) * SEQUENCE_COUNT * BLOCK_LEN // TOK_DEV)
    routes_turns = jax.random.permutation(jax.random.fold_in(key_list[1], 3), LAYER_COUNT * (SEQUENCE_LENGTH // BLOCK_LEN) * SEQUENCE_COUNT * BLOCK_LEN // TOK_DEV)
    routes = jax.vmap(lambda own, number: assign_block(jax.random.fold_in(key_list[1], 2), own, number, TOK_DEV, EXPERTS, TOP, CAP, 1))(routes_keys, routes_turns).reshape((LAYER_COUNT, SEQUENCE_LENGTH // BLOCK_LEN, SEQUENCE_COUNT, BLOCK_LEN, TOP))
    cotangent = scatter_about(key_list[2], (SEQUENCE_COUNT, SEQUENCE_LENGTH, MODEL_DIM), 1.0, 6.0, ((0, 8), (1, 4)))
    query_weight = scatter_about(key_list[3], (LAYER_COUNT, MODEL_DIM, QUERY_HEADS * HEAD_SIZE), MODEL_DIM ** -0.5, 0.15625, ((1, 32),))
    key_projection_weight = scatter_about(key_list[4], (LAYER_COUNT, MODEL_DIM, KEY_VALUE_HEADS * HEAD_SIZE), MODEL_DIM ** -0.5, 0.15625, ((1, 32),))
    value_projection_weight = scatter_about(key_list[5], (LAYER_COUNT, MODEL_DIM, KEY_VALUE_HEADS * HEAD_SIZE), MODEL_DIM ** -0.5, 0.15625, ((1, 32),))
    output_weight = scatter_about(key_list[6], (LAYER_COUNT, QUERY_HEADS * HEAD_SIZE, MODEL_DIM), (QUERY_HEADS * HEAD_SIZE // 16) ** -0.5, 0.625, ((2, 32),))
    attention_gain = jnp.clip(1.0 + 0.1 * jax.random.normal(key_list[7], (LAYER_COUNT, MODEL_DIM), jnp.float32), 0.5, 1.5).astype(jnp.bfloat16)
    expert_gain = jnp.clip(1.0 + 0.1 * jax.random.normal(key_list[8], (LAYER_COUNT, MODEL_DIM), jnp.float32), 0.5, 1.5).astype(jnp.bfloat16)
    router_weight = scatter_about(key_list[9], (LAYER_COUNT, MODEL_DIM, EXPERTS), (4 * MODEL_DIM) ** -0.5, 0.078125, ((1, 32),))
    gate_weight = scatter_about(key_list[10], (LAYER_COUNT, EXPERTS, MODEL_DIM, FF), MODEL_DIM ** -0.5, 0.15625, ((1, 4), (2, 8)))
    up_weight = scatter_about(key_list[11], (LAYER_COUNT, EXPERTS, MODEL_DIM, FF), MODEL_DIM ** -0.5, 0.15625, ((1, 4), (2, 8)))
    down_weight = scatter_about(key_list[12], (LAYER_COUNT, EXPERTS, FF, MODEL_DIM), (FF // 8) ** -0.5, 0.75, ((1, 4), (3, 8)))
    return dict(inputs=inputs, routes=routes, cotangent=cotangent, query_weight=query_weight, key_projection_weight=key_projection_weight, value_projection_weight=value_projection_weight, output_weight=output_weight, attention_gain=attention_gain, expert_gain=expert_gain, router_weight=router_weight, gate_weight=gate_weight, up_weight=up_weight, down_weight=down_weight)


@jax.custom_vjp
def reduced_precision(v):
    return lax.optimization_barrier(v.astype(jnp.bfloat16)).astype(jnp.float32)

@jax.custom_vjp
def reduced_backward(v):
    return v

def low_keep(v):
    return (reduced_precision(v), None)

def low_pass(kept, grad):
    return (grad,)

def back_keep(v):
    return (v, None)

def back_low(kept, grad):
    return (reduced_precision(grad),)
reduced_precision.defvjp(low_keep, low_pass)
reduced_backward.defvjp(back_keep, back_low)
eps_norm = 1e-06
highest_precision = lax.Precision.HIGHEST

def rotary_tables(positions, half_dim):
    frequency = jnp.exp(-math.log(10000.0) * jnp.arange(half_dim, dtype=jnp.float32) / half_dim)
    angles = positions.astype(jnp.float32)[:, None] * frequency[None, :]
    return (jnp.cos(angles), jnp.sin(angles))

def rotate_features(values, cosine_table, sine_table):
    half_dim = values.shape[-1] // 2
    first_half = values[..., :half_dim]
    second_half = values[..., half_dim:]
    cos_part = cosine_table[:, None, :]
    sin_part = sine_table[:, None, :]
    return jnp.concatenate([first_half * cos_part - second_half * sin_part, second_half * cos_part + first_half * sin_part], axis=-1)

def rms_norm(values, gain_vec):
    inv_rms = lax.rsqrt(lax.optimization_barrier(jnp.mean(values * values, axis=-1, keepdims=True)) + eps_norm)
    return values * inv_rms * gain_vec

def attend_sequence(operands):
    query_seq, key_seq, value_seq = operands
    seq_len = query_seq.shape[0]
    raw_scores = jnp.einsum('qhgd,khd->hgqk', query_seq, key_seq, precision=highest_precision) * HEAD_SIZE ** (-0.5)
    scores = reduced_backward(raw_scores)
    causal = jnp.arange(seq_len, dtype=jnp.int32)[:, None] >= jnp.arange(seq_len, dtype=jnp.int32)[None, :]
    masked = jnp.where(causal, scores, -1e+30)
    row_max = lax.optimization_barrier(jnp.max(masked, axis=-1, keepdims=True))
    exp_scores = jnp.exp(masked - row_max)
    prob_low = reduced_precision(exp_scores / lax.optimization_barrier(jnp.sum(exp_scores, axis=-1, keepdims=True)))
    return jnp.einsum('hgqk,khd->qhgd', prob_low, value_seq, precision=highest_precision)

def layer_forward(hidden, layer_routes, weights):
    query_w, key_matrix, value_matrix, output_w, gain_one, gain_two, router_w, gate_w, up_w, down_w = weights
    cosine_table, sine_table = rotary_tables(jnp.arange(SEQUENCE_LENGTH, dtype=jnp.int32), HEAD_SIZE // 2)
    first_normalized = reduced_precision(rms_norm(hidden, gain_one)).reshape(-1, MODEL_DIM)
    query_linear = reduced_backward(jnp.dot(first_normalized, query_w, precision=highest_precision)).reshape(SEQUENCE_COUNT, SEQUENCE_LENGTH, QUERY_HEADS, HEAD_SIZE)
    key_linear = reduced_backward(jnp.dot(first_normalized, key_matrix, precision=highest_precision)).reshape(SEQUENCE_COUNT, SEQUENCE_LENGTH, KEY_VALUE_HEADS, HEAD_SIZE)
    value_everything = reduced_precision(reduced_backward(jnp.dot(first_normalized, value_matrix, precision=highest_precision))).reshape(SEQUENCE_COUNT, SEQUENCE_LENGTH, KEY_VALUE_HEADS, HEAD_SIZE)
    query_rotated = reduced_precision(rotate_features(query_linear, cosine_table, sine_table)).reshape(SEQUENCE_COUNT, SEQUENCE_LENGTH, KEY_VALUE_HEADS, QUERY_HEADS // KEY_VALUE_HEADS, HEAD_SIZE)
    key_rot = reduced_precision(rotate_features(key_linear, cosine_table, sine_table))
    attended = lax.map(jax.checkpoint(attend_sequence), (query_rotated, key_rot, value_everything))
    attended = reduced_precision(reduced_backward(attended.reshape(-1, QUERY_HEADS * HEAD_SIZE)))
    branch = reduced_backward(jnp.dot(attended, output_w, precision=highest_precision))
    middle = hidden.reshape(-1, MODEL_DIM) + branch
    normed_two = reduced_precision(rms_norm(middle, gain_two))
    logits = reduced_backward(jnp.dot(normed_two, router_w, precision=highest_precision))
    token_routes = layer_routes.transpose(1, 0, 2, 3).reshape(-1, TOP)
    chosen = jnp.take_along_axis(logits, token_routes, axis=1)
    gate_share = jax.nn.softmax(chosen, axis=-1)
    pair_total = token_routes.shape[0] * TOP
    flat_expert = token_routes.reshape(-1)
    pair_hot = (flat_expert[:, None] == jnp.arange(EXPERTS, dtype=jnp.int32)[None, :]).astype(jnp.int32)
    slot_rank = lax.optimization_barrier(jnp.sum((jnp.cumsum(pair_hot, axis=0) - 1) * pair_hot, axis=1)).astype(jnp.int32)
    slot_table = jnp.full((EXPERTS, N_DP * N_EXPERT * CAP), pair_total, jnp.int32)
    slot_table = slot_table.at[flat_expert, slot_rank].set(jnp.arange(pair_total, dtype=jnp.int32))
    gate_flat = gate_share.reshape(-1)

    def expert_rows(gate_e, up_e, down_e, table_row):
        is_valid = table_row < pair_total
        safe_pair = jnp.minimum(table_row, pair_total - 1)
        token_rows = reduced_backward(normed_two[safe_pair // TOP])
        gate_val = reduced_backward(jnp.dot(token_rows, gate_e, precision=highest_precision))
        up_val = reduced_backward(jnp.dot(token_rows, up_e, precision=highest_precision))
        inner_act = reduced_precision(jax.nn.silu(gate_val) * up_val)
        out_rows = reduced_precision(reduced_backward(jnp.dot(inner_act, down_e, precision=highest_precision)))
        weight = jnp.where(is_valid, gate_flat[safe_pair], 0.0)
        return out_rows * weight[:, None]
    checked = jax.checkpoint(expert_rows)

    def expert_step(running, operands):
        gate_e, up_e, down_e, table_row = operands
        token_ids = jnp.minimum(table_row, pair_total - 1) // TOP
        return (running.at[token_ids].add(checked(gate_e, up_e, down_e, table_row)), None)
    expert_sum, unused = lax.scan(expert_step, jnp.zeros((SEQUENCE_COUNT * SEQUENCE_LENGTH, MODEL_DIM), jnp.float32), (gate_w, up_w, down_w, slot_table))
    return (middle + expert_sum).reshape(SEQUENCE_COUNT, SEQUENCE_LENGTH, MODEL_DIM)

def reference(inputs, routes, cotangent, query_weight, key_projection_weight, value_projection_weight, output_weight, attention_gain, expert_gain, router_weight, gate_weight, up_weight, down_weight):
    params = tuple((stacked.astype(jnp.float32) for stacked in (query_weight, key_projection_weight, value_projection_weight, output_weight, attention_gain, expert_gain, router_weight, gate_weight, up_weight, down_weight)))

    def forward(hidden, weights):
        for layer_index in range(LAYER_COUNT):
            hidden = layer_forward(hidden, routes[layer_index], tuple((stacked[layer_index] for stacked in weights)))
        return hidden
    output, pullback = jax.vjp(forward, inputs.astype(jnp.float32), params)
    grad_inputs, grad_params = pullback(cotangent.astype(jnp.float32))
    return (output.astype(jnp.bfloat16), grad_inputs, grad_params[0], grad_params[1], grad_params[2], grad_params[3], grad_params[4], grad_params[5], grad_params[6], grad_params[7], grad_params[8], grad_params[9])
```

```python
import math

import jax
import jax.numpy as jnp
from jax import lax
from jax.sharding import PartitionSpec as P

QUERY_HEADS = 24
KEY_VALUE_HEADS = 8
HEAD_SIZE = 64
LAYER_COUNT = 2


eps_norm = 1e-06
highest_precision = lax.Precision.HIGHEST


def rotary_tables(positions, half_dim):
    frequency = jnp.exp(-math.log(10000.0) * jnp.arange(half_dim, dtype=jnp.float32) / half_dim)
    angles = positions.astype(jnp.float32)[:, None] * frequency[None, :]
    return (jnp.cos(angles), jnp.sin(angles))


def rotate_features(values, cosine_table, sine_table):
    half_dim = values.shape[-1] // 2
    first_half = values[..., :half_dim]
    second_half = values[..., half_dim:]
    cos_part = cosine_table[:, None, :]
    sin_part = sine_table[:, None, :]
    return jnp.concatenate(
        [
            first_half * cos_part - second_half * sin_part,
            second_half * cos_part + first_half * sin_part,
        ],
        axis=-1,
    )


def norm_forward(values, gain_vec):
    inv_rms = lax.rsqrt(jnp.mean(values * values, axis=-1, keepdims=True) + eps_norm)
    return (values * inv_rms * gain_vec, inv_rms)


def norm_backward(values, inv_rms, gain_vec, upstream):
    scaled = upstream * gain_vec
    grad_gain = jnp.sum(upstream * values * inv_rms, axis=0)
    grad_values = inv_rms * (
        scaled - values * inv_rms * inv_rms * jnp.mean(scaled * values, axis=-1, keepdims=True)
    )
    return (grad_values, grad_gain)


def stack_member(layer_list, member):
    return jnp.stack([layer_parts[member] for layer_parts in layer_list], axis=0)


def exchange(blocks):
    return lax.all_to_all(blocks, "expert", split_axis=0, concat_axis=0, tiled=True)


def gather_rows(rows):
    groups = lax.axis_size("expert")
    blocks = exchange(jnp.broadcast_to(rows[None], (groups,) + rows.shape))
    return blocks.reshape((groups * rows.shape[0],) + rows.shape[1:])


def sum_rows(partial_rows):
    groups = lax.axis_size("expert")
    blocks = partial_rows.reshape((groups, -1) + partial_rows.shape[1:])
    return jnp.sum(exchange(blocks).astype(jnp.float32), axis=0)


def dot_f32(left, right, left_dims, right_dims):
    return lax.dot_general(
        left, right, ((left_dims, right_dims), ((), ())), preferred_element_type=jnp.float32
    )


def body(
    inputs,
    routes,
    cotangent,
    query_weight,
    key_projection_weight,
    value_projection_weight,
    output_weight,
    attention_gain,
    expert_gain,
    router_weight,
    gate_weight,
    up_weight,
    down_weight,
):
    sequences_per_device, block_length, model_width = inputs.shape
    token_total = sequences_per_device * block_length
    exp_dev = gate_weight.shape[1]
    groups = lax.axis_size("expert")
    expert_total = exp_dev * groups
    all_rows = token_total * groups
    query_width = query_weight.shape[2]
    key_width = key_projection_weight.shape[2]
    query_head_group = QUERY_HEADS // KEY_VALUE_HEADS
    score_scale = HEAD_SIZE ** (-0.5)
    my_group = lax.axis_index("expert")
    positions = my_group * block_length + jnp.arange(block_length, dtype=jnp.int32)
    cosine_table, sine_table = rotary_tables(positions, HEAD_SIZE // 2)
    causal = positions[:, None] >= jnp.arange(block_length * groups, dtype=jnp.int32)[None, :]
    expert_ids = jnp.arange(expert_total, dtype=jnp.int32)
    small_width = -(-(expert_total + 2) // 128) * 128
    gate_width = -(-(2 * expert_total) // 128) * 128
    edges = (
        query_width,
        query_width + key_width,
        query_width + 2 * key_width,
        query_width + 2 * key_width + model_width,
        query_width + 2 * key_width + model_width + expert_total,
        query_width + 2 * key_width + model_width + expert_total + 1,
    )

    def pack_attention(query_part, key_part, value_part, output_part, router_part, one, two):
        rows = query_part.shape[0]
        fill = jnp.zeros((rows, small_width - expert_total - 2), query_part.dtype)
        return jnp.concatenate(
            [
                query_part,
                key_part,
                value_part,
                output_part,
                router_part,
                one[:, None],
                two[:, None],
                fill,
            ],
            axis=1,
        )

    chosen_hot = jnp.any(
        routes.reshape(LAYER_COUNT, token_total, -1)[:, :, :, None] == expert_ids, axis=2
    )
    chosen_all = gather_rows(
        jnp.moveaxis(chosen_hot, 0, 1).reshape(token_total, -1).astype(jnp.bfloat16)
    ).reshape(all_rows, LAYER_COUNT, expert_total)

    packed = [
        lax.all_gather(
            pack_attention(
                query_weight[layer],
                key_projection_weight[layer],
                value_projection_weight[layer],
                output_weight[layer].T,
                router_weight[layer],
                attention_gain[layer],
                expert_gain[layer],
            ),
            ("dp", "expert"),
            axis=0,
            tiled=True,
        )
        for layer in range(LAYER_COUNT)
    ]
    gathered = [
        (
            lax.all_gather(gate_weight[layer], "dp", axis=1, tiled=True),
            lax.all_gather(up_weight[layer], "dp", axis=1, tiled=True),
            lax.all_gather(down_weight[layer], "dp", axis=2, tiled=True),
        )
        for layer in range(LAYER_COUNT)
    ]

    def shares_of(rows, router_full, hot):
        logits = jnp.dot(rows, router_full, preferred_element_type=jnp.float32)
        masked = jnp.where(hot, logits, -1e30)
        exps = jnp.where(hot, jnp.exp(masked - jnp.max(masked, axis=1, keepdims=True)), 0.0)
        return exps / jnp.sum(exps, axis=1, keepdims=True)

    def layer_forward(hidden, layer):
        full = packed[layer]
        qkv_full = full[:, : edges[2]]
        output_full = full[:, edges[2] : edges[3]]
        router_full = full[:, edges[3] : edges[4]]
        gain_one = full[:, edges[4]].astype(jnp.float32)
        gain_two = full[:, edges[5]].astype(jnp.float32)
        gate_full, up_full, down_full = gathered[layer]
        first_normalized, inv_one = norm_forward(hidden, gain_one)
        first_normalized = first_normalized.astype(jnp.bfloat16)
        linear = jnp.dot(first_normalized, qkv_full, preferred_element_type=jnp.float32)
        query_rotated = rotate_features(
            linear[:, : edges[0]].reshape(token_total, QUERY_HEADS, HEAD_SIZE),
            cosine_table,
            sine_table,
        ).astype(jnp.bfloat16)
        query_grouped = query_rotated.reshape(
            token_total, KEY_VALUE_HEADS, query_head_group, HEAD_SIZE
        )
        key_rot = rotate_features(
            linear[:, edges[0] : edges[1]].reshape(token_total, KEY_VALUE_HEADS, HEAD_SIZE),
            cosine_table,
            sine_table,
        ).astype(jnp.bfloat16)
        key_value = jnp.concatenate(
            [
                key_rot.reshape(token_total, key_width),
                linear[:, edges[1] :].astype(jnp.bfloat16),
            ],
            axis=1,
        )
        key_value_all = gather_rows(key_value).reshape(all_rows, 2, KEY_VALUE_HEADS, HEAD_SIZE)
        key_all, value_all = key_value_all[:, 0], key_value_all[:, 1]
        scores = (
            jnp.einsum("qhgd,khd->hgqk", query_grouped, key_all, preferred_element_type=jnp.float32)
            * score_scale
        )
        masked = jnp.where(causal, scores, -1e30)
        row_max = jnp.max(masked, axis=-1, keepdims=True)
        exp_scores = jnp.exp(masked - row_max)
        row_total = jnp.sum(exp_scores, axis=-1, keepdims=True)
        log_total = row_max + jnp.log(row_total)
        prob_low = (exp_scores / row_total).astype(jnp.bfloat16)
        attended = jnp.einsum(
            "hgqk,khd->qhgd", prob_low, value_all, preferred_element_type=jnp.float32
        )
        attended = attended.reshape(token_total, query_width).astype(jnp.bfloat16)
        middle = hidden + dot_f32(attended, output_full, (1,), (1,))
        normed_two, inv_two = norm_forward(middle, gain_two)
        normed_two = normed_two.astype(jnp.bfloat16)
        arrived = gather_rows(normed_two)
        share_all = shares_of(arrived, router_full, chosen_all[:, layer] > 0)
        share_own = shares_of(normed_two, router_full, chosen_hot[layer])
        share_local = lax.dynamic_slice_in_dim(share_all, my_group * exp_dev, exp_dev, axis=1)
        gate_val = jnp.einsum("td,edf->tef", arrived, gate_full, preferred_element_type=jnp.float32)
        up_val = jnp.einsum("td,edf->tef", arrived, up_full, preferred_element_type=jnp.float32)
        scaled_act = (jax.nn.silu(gate_val) * up_val * share_local[:, :, None]).astype(jnp.bfloat16)
        out_rows = jnp.einsum(
            "tef,efd->td", scaled_act, down_full, preferred_element_type=jnp.float32
        ).astype(jnp.bfloat16)
        output = middle + sum_rows(out_rows)
        kept_state = (
            hidden,
            inv_one,
            first_normalized,
            query_grouped,
            key_all,
            value_all,
            log_total,
            attended,
            middle,
            inv_two,
            normed_two,
            share_own,
            share_local,
            arrived,
            gate_val.astype(jnp.bfloat16),
            up_val.astype(jnp.bfloat16),
            scaled_act,
            qkv_full,
            output_full,
            gain_one,
            gain_two,
            router_full,
            gate_full,
            up_full,
            down_full,
        )
        return (output, kept_state)

    hidden = inputs.astype(jnp.float32).reshape(token_total, model_width)
    kept_states = []
    for layer in range(LAYER_COUNT):
        hidden, kept_state = layer_forward(hidden, layer)
        kept_states.append(kept_state)
    output = hidden.astype(jnp.bfloat16).reshape(sequences_per_device, block_length, model_width)
    grad_hidden = cotangent.astype(jnp.float32).reshape(token_total, model_width)
    attention_list = [None] * LAYER_COUNT
    expert_list = [None] * LAYER_COUNT
    for layer in range(LAYER_COUNT - 1, -1, -1):
        (
            layer_hidden,
            inv_one,
            first_normalized,
            query_grouped,
            key_all,
            value_all,
            log_total,
            attended,
            middle,
            inv_two,
            normed_two,
            share_own,
            share_local,
            arrived,
            gate_low,
            up_low,
            scaled_act,
            qkv_full,
            output_full,
            gain_one,
            gain_two,
            router_full,
            gate_full,
            up_full,
            down_full,
        ) = kept_states[layer]
        grad_all = gather_rows(grad_hidden.astype(jnp.bfloat16))
        grad_down = jnp.einsum(
            "tef,td->efd", scaled_act, grad_all, preferred_element_type=jnp.float32
        ).astype(jnp.bfloat16)
        grad_scaled = jnp.einsum(
            "td,efd->tef", grad_all, down_full, preferred_element_type=jnp.float32
        )
        gate_val = gate_low.astype(jnp.float32)
        up_val = up_low.astype(jnp.float32)
        sigmoid_val = jax.nn.sigmoid(gate_val)
        silu_val = gate_val * sigmoid_val
        grad_gates = jnp.sum(grad_scaled * silu_val * up_val, axis=2)
        grad_inner = grad_scaled * share_local[:, :, None]
        grad_gate_val = (
            grad_inner * up_val * sigmoid_val * (1.0 + gate_val * (1.0 - sigmoid_val))
        ).astype(jnp.bfloat16)
        grad_up_val = (grad_inner * silu_val).astype(jnp.bfloat16)
        grad_gate_w = jnp.einsum(
            "td,tef->edf", arrived, grad_gate_val, preferred_element_type=jnp.float32
        ).astype(jnp.bfloat16)
        grad_up_w = jnp.einsum(
            "td,tef->edf", arrived, grad_up_val, preferred_element_type=jnp.float32
        ).astype(jnp.bfloat16)
        grad_rows = jnp.einsum(
            "tef,edf->td", grad_gate_val, gate_full, preferred_element_type=jnp.float32
        ) + jnp.einsum("tef,edf->td", grad_up_val, up_full, preferred_element_type=jnp.float32)
        gates_high = grad_gates.astype(jnp.bfloat16)
        gates_low = (grad_gates - gates_high.astype(jnp.float32)).astype(jnp.bfloat16)
        gate_columns = jnp.zeros((all_rows, gate_width), jnp.bfloat16)
        gate_columns = lax.dynamic_update_slice_in_dim(
            gate_columns, gates_high, my_group * exp_dev, axis=1
        )
        gate_columns = lax.dynamic_update_slice_in_dim(
            gate_columns, gates_low, expert_total + my_group * exp_dev, axis=1
        )
        back = sum_rows(
            jnp.concatenate([grad_rows.astype(jnp.bfloat16), gate_columns], axis=1)
        )
        grad_gates_own = (
            back[:, model_width : model_width + expert_total]
            + back[:, model_width + expert_total : model_width + 2 * expert_total]
        )
        grad_logits = (
            share_own
            * (grad_gates_own - jnp.sum(share_own * grad_gates_own, axis=-1, keepdims=True))
        ).astype(jnp.bfloat16)
        grad_router = dot_f32(normed_two, grad_logits, (0,), (0,))
        grad_normed_two = back[:, :model_width] + dot_f32(grad_logits, router_full, (1,), (1,))
        grad_norm_mid, grad_gain_two = norm_backward(middle, inv_two, gain_two, grad_normed_two)
        grad_middle = grad_hidden + grad_norm_mid
        grad_branch = grad_middle.astype(jnp.bfloat16)
        grad_output_w = dot_f32(grad_branch, attended, (0,), (0,))
        grad_attended = (
            dot_f32(grad_branch, output_full, (1,), (0,))
            .astype(jnp.bfloat16)
            .reshape(token_total, KEY_VALUE_HEADS, query_head_group, HEAD_SIZE)
        )
        layer_scores = (
            jnp.einsum("qhgd,khd->hgqk", query_grouped, key_all, preferred_element_type=jnp.float32)
            * score_scale
        )
        softmax_probs = jnp.exp(jnp.where(causal, layer_scores, -1e30) - log_total)
        grad_probs = jnp.einsum(
            "qhgd,khd->hgqk", grad_attended, value_all, preferred_element_type=jnp.float32
        )
        grad_scores = (
            softmax_probs
            * (grad_probs - jnp.sum(softmax_probs * grad_probs, axis=-1, keepdims=True))
        ).astype(jnp.bfloat16)
        grad_query = (
            jnp.einsum("hgqk,khd->qhgd", grad_scores, key_all, preferred_element_type=jnp.float32)
            * score_scale
        )
        grad_key_all = (
            jnp.einsum(
                "hgqk,qhgd->khd", grad_scores, query_grouped, preferred_element_type=jnp.float32
            )
            * score_scale
        )
        grad_value_all = jnp.einsum(
            "hgqk,qhgd->khd",
            softmax_probs.astype(jnp.bfloat16),
            grad_attended,
            preferred_element_type=jnp.float32,
        )
        grad_kv = sum_rows(
            jnp.concatenate(
                [
                    grad_key_all.reshape(all_rows, key_width).astype(jnp.bfloat16),
                    grad_value_all.reshape(all_rows, key_width).astype(jnp.bfloat16),
                ],
                axis=1,
            )
        )
        grad_query_lin = (
            rotate_features(
                grad_query.reshape(token_total, QUERY_HEADS, HEAD_SIZE), cosine_table, -sine_table
            )
            .astype(jnp.bfloat16)
            .reshape(token_total, query_width)
        )
        grad_key_lin = (
            rotate_features(
                grad_kv[:, :key_width].reshape(token_total, KEY_VALUE_HEADS, HEAD_SIZE),
                cosine_table,
                -sine_table,
            )
            .astype(jnp.bfloat16)
            .reshape(token_total, key_width)
        )
        grad_linear = jnp.concatenate(
            [grad_query_lin, grad_key_lin, grad_kv[:, key_width:].astype(jnp.bfloat16)], axis=1
        )
        grad_qkv_w = dot_f32(first_normalized, grad_linear, (0,), (0,))
        grad_normed_one = dot_f32(grad_linear, qkv_full, (1,), (1,))
        grad_norm_in, grad_gain_one = norm_backward(
            layer_hidden, inv_one, gain_one, grad_normed_one
        )
        fill = jnp.zeros((model_width, small_width - expert_total - 2), jnp.bfloat16)
        small_part = jnp.concatenate(
            [
                grad_router.astype(jnp.bfloat16),
                grad_gain_one[:, None].astype(jnp.bfloat16),
                grad_gain_two[:, None].astype(jnp.bfloat16),
                fill,
            ],
            axis=1,
        )
        attention_list[layer] = lax.psum_scatter(
            jnp.concatenate(
                [
                    grad_qkv_w.astype(jnp.bfloat16),
                    grad_output_w.astype(jnp.bfloat16),
                    small_part,
                ],
                axis=1,
            ),
            ("dp", "expert"),
            scatter_dimension=0,
            tiled=True,
        ).astype(jnp.float32)
        expert_list[layer] = (
            lax.psum_scatter(grad_gate_w, "dp", scatter_dimension=1, tiled=True),
            lax.psum_scatter(grad_up_w, "dp", scatter_dimension=1, tiled=True),
            lax.psum_scatter(grad_down, "dp", scatter_dimension=2, tiled=True),
        )
        grad_hidden = grad_middle + grad_norm_in
    stacked = jnp.stack(attention_list)
    return (
        output,
        grad_hidden.reshape(sequences_per_device, block_length, model_width),
        stacked[:, :, : edges[0]],
        stacked[:, :, edges[0] : edges[1]],
        stacked[:, :, edges[1] : edges[2]],
        jnp.swapaxes(stacked[:, :, edges[2] : edges[3]], 1, 2),
        stacked[:, :, edges[4]],
        stacked[:, :, edges[5]],
        stacked[:, :, edges[3] : edges[4]],
        stack_member(expert_list, 0).astype(jnp.float32),
        stack_member(expert_list, 1).astype(jnp.float32),
        stack_member(expert_list, 2).astype(jnp.float32),
    )


def solution(mesh):
    in_specs = (
        P("dp", "expert", None),
        P(None, "expert", "dp", None, None),
        P("dp", "expert", None),
        P(None, ("dp", "expert"), None),
        P(None, ("dp", "expert"), None),
        P(None, ("dp", "expert"), None),
        P(None, None, ("dp", "expert")),
        P(None, ("dp", "expert")),
        P(None, ("dp", "expert")),
        P(None, ("dp", "expert"), None),
        P(None, "expert", "dp", None),
        P(None, "expert", "dp", None),
        P(None, "expert", None, "dp"),
    )
    out_specs = (
        P("dp", "expert", None),
        P("dp", "expert", None),
        P(None, ("dp", "expert"), None),
        P(None, ("dp", "expert"), None),
        P(None, ("dp", "expert"), None),
        P(None, None, ("dp", "expert")),
        P(None, ("dp", "expert")),
        P(None, ("dp", "expert")),
        P(None, ("dp", "expert"), None),
        P(None, "expert", "dp", None),
        P(None, "expert", "dp", None),
        P(None, "expert", None, "dp"),
    )
    return jax.shard_map(body, mesh=mesh, in_specs=in_specs, out_specs=out_specs, check_vma=False)
```

```python
import math

import jax
import jax.numpy as jnp
from jax import lax
from jax.sharding import PartitionSpec as P

QUERY_HEADS = 24
KEY_VALUE_HEADS = 8
HEAD_SIZE = 64
LAYER_COUNT = 2


eps_norm = 1e-06
highest_precision = lax.Precision.HIGHEST


def rotary_tables(positions, half_dim):
    frequency = jnp.exp(-math.log(10000.0) * jnp.arange(half_dim, dtype=jnp.float32) / half_dim)
    angles = positions.astype(jnp.float32)[:, None] * frequency[None, :]
    return (jnp.cos(angles), jnp.sin(angles))


def rotate_features(values, cosine_table, sine_table):
    half_dim = values.shape[-1] // 2
    first_half = values[..., :half_dim]
    second_half = values[..., half_dim:]
    cos_part = cosine_table[:, None, :]
    sin_part = sine_table[:, None, :]
    return jnp.concatenate(
        [
            first_half * cos_part - second_half * sin_part,
            second_half * cos_part + first_half * sin_part,
        ],
        axis=-1,
    )


def norm_forward(values, gain_vec):
    inv_rms = lax.rsqrt(jnp.mean(values * values, axis=-1, keepdims=True) + eps_norm)
    return (values * inv_rms * gain_vec, inv_rms)


def norm_backward(values, inv_rms, gain_vec, upstream):
    scaled = upstream * gain_vec
    grad_gain = jnp.sum(upstream * values * inv_rms, axis=0)
    grad_values = inv_rms * (
        scaled - values * inv_rms * inv_rms * jnp.mean(scaled * values, axis=-1, keepdims=True)
    )
    return (grad_values, grad_gain)


def stack_member(layer_list, member):
    return jnp.stack([layer_parts[member] for layer_parts in layer_list], axis=0)


def exchange(blocks):
    return lax.all_to_all(blocks, "expert", split_axis=0, concat_axis=0, tiled=True)


def gather_rows(rows):
    groups = lax.axis_size("expert")
    blocks = exchange(jnp.broadcast_to(rows[None], (groups,) + rows.shape))
    return blocks.reshape((groups * rows.shape[0],) + rows.shape[1:])


def sum_rows(partial_rows):
    groups = lax.axis_size("expert")
    blocks = partial_rows.reshape((groups, -1) + partial_rows.shape[1:])
    return jnp.sum(exchange(blocks).astype(jnp.float32), axis=0)


def same_core():
    members = range(lax.axis_size("dp"))
    return [[i for i in members if i % 2 == core] for core in range(2)]


def swap_cores(values):
    return lax.ppermute(values, "dp", [(i, i ^ 1) for i in range(lax.axis_size("dp"))])


def exchange_chips(blocks):
    return lax.all_to_all(
        blocks, "dp", split_axis=0, concat_axis=0, axis_index_groups=same_core(), tiled=True
    )


def gather_staged(shard):
    chips = lax.axis_size("dp") // 2
    groups = lax.axis_size("expert")
    rows, width = shard.shape
    chip_rows = exchange_chips(jnp.broadcast_to(shard[None], (chips, rows, width)))
    own = exchange(jnp.broadcast_to(chip_rows[None], (groups, chips, rows, width)))
    other = swap_cores(own)
    first = lax.axis_index("dp") % 2 == 0
    both = jnp.stack([jnp.where(first, own, other), jnp.where(first, other, own)])
    return both.transpose(2, 0, 1, 3, 4).reshape(-1, width)


def core_major(columns):
    chips = lax.axis_size("dp") // 2
    groups = lax.axis_size("expert")
    split = columns.reshape(columns.shape[0], chips, 2, groups, -1)
    halves = split.transpose(2, 0, 3, 1, 4).reshape(2, columns.shape[0], -1)
    core = lax.axis_index("dp") % 2
    mine = lax.dynamic_index_in_dim(halves, core, 0, keepdims=False)
    theirs = lax.dynamic_index_in_dim(halves, 1 - core, 0, keepdims=False)
    return jnp.concatenate([mine, swap_cores(theirs)], axis=0)


def both_cores(rows):
    return jnp.concatenate([rows, swap_cores(rows)], axis=0)


def scatter_staged(partial):
    chips = lax.axis_size("dp") // 2
    groups = lax.axis_size("expert")
    width = partial.shape[1]
    blocks = exchange(partial.reshape(groups, -1, width))
    chip_blocks = jnp.sum(blocks.astype(jnp.float32), axis=0).astype(jnp.bfloat16)
    arrived = exchange_chips(chip_blocks.reshape(chips, -1, width))
    return jnp.sum(arrived.astype(jnp.float32), axis=0)


def dot_f32(left, right, left_dims, right_dims):
    return lax.dot_general(
        left, right, ((left_dims, right_dims), ((), ())), preferred_element_type=jnp.float32
    )


def body(
    inputs,
    routes,
    cotangent,
    query_weight,
    key_projection_weight,
    value_projection_weight,
    output_weight,
    attention_gain,
    expert_gain,
    router_weight,
    gate_weight,
    up_weight,
    down_weight,
):
    sequences_per_device, block_length, model_width = inputs.shape
    token_total = sequences_per_device * block_length
    exp_dev = gate_weight.shape[1]
    groups = lax.axis_size("expert")
    expert_total = exp_dev * groups
    all_rows = token_total * groups
    query_width = query_weight.shape[2]
    key_width = key_projection_weight.shape[2]
    query_head_group = QUERY_HEADS // KEY_VALUE_HEADS
    score_scale = HEAD_SIZE ** (-0.5)
    my_group = lax.axis_index("expert")
    positions = my_group * block_length + jnp.arange(block_length, dtype=jnp.int32)
    cosine_table, sine_table = rotary_tables(positions, HEAD_SIZE // 2)
    causal = positions[:, None] >= jnp.arange(block_length * groups, dtype=jnp.int32)[None, :]
    expert_ids = jnp.arange(expert_total, dtype=jnp.int32)
    small_width = -(-(expert_total + 2) // 128) * 128
    gate_width = -(-(2 * expert_total) // 128) * 128
    edges = (
        query_width,
        query_width + key_width,
        query_width + 2 * key_width,
        query_width + 2 * key_width + model_width,
        query_width + 2 * key_width + model_width + expert_total,
        query_width + 2 * key_width + model_width + expert_total + 1,
    )

    def pack_attention(query_part, key_part, value_part, output_part, router_part, one, two):
        rows = query_part.shape[0]
        fill = jnp.zeros((rows, small_width - expert_total - 2), query_part.dtype)
        return jnp.concatenate(
            [
                query_part,
                key_part,
                value_part,
                output_part,
                router_part,
                one[:, None],
                two[:, None],
                fill,
            ],
            axis=1,
        )

    chosen_hot = jnp.any(
        routes.reshape(LAYER_COUNT, token_total, -1)[:, :, :, None] == expert_ids, axis=2
    )
    chosen_all = gather_rows(
        jnp.moveaxis(chosen_hot, 0, 1).reshape(token_total, -1).astype(jnp.bfloat16)
    ).reshape(all_rows, LAYER_COUNT, expert_total)

    shards = [
        pack_attention(
            query_weight[layer],
            key_projection_weight[layer],
            value_projection_weight[layer],
            output_weight[layer].T,
            router_weight[layer],
            attention_gain[layer],
            expert_gain[layer],
        )
        for layer in range(LAYER_COUNT)
    ]
    packed = [lax.all_gather(shards[0], ("dp", "expert"), axis=0, tiled=True)]
    packed += [gather_staged(shard) for shard in shards[1:]]
    ff_width = gate_weight.shape[3]
    hidden_width = exp_dev * ff_width
    gathered = [
        tuple(
            lax.all_gather(rows.reshape(-1, hidden_width), "dp", axis=0, tiled=True)
            for rows in (
                gate_weight[layer].transpose(1, 0, 2),
                up_weight[layer].transpose(1, 0, 2),
                down_weight[layer].transpose(2, 0, 1),
            )
        )
        for layer in range(LAYER_COUNT)
    ]

    def spread(columns):
        return jnp.broadcast_to(
            columns[:, :, None], columns.shape + (ff_width,)
        ).reshape(columns.shape[0], hidden_width)

    def shares_of(rows, router_full, hot):
        logits = jnp.dot(rows, router_full, preferred_element_type=jnp.float32)
        masked = jnp.where(hot, logits, -1e30)
        exps = jnp.where(hot, jnp.exp(masked - jnp.max(masked, axis=1, keepdims=True)), 0.0)
        return exps / jnp.sum(exps, axis=1, keepdims=True)

    def layer_forward(hidden, layer):
        full = packed[layer]
        qkv_full = full[:, : edges[2]]
        output_full = full[:, edges[2] : edges[3]]
        router_full = full[:, edges[3] : edges[4]]
        gain_one = full[:, edges[4]].astype(jnp.float32)
        gain_two = full[:, edges[5]].astype(jnp.float32)
        gate_full, up_full, down_full = gathered[layer]
        first_normalized, inv_one = norm_forward(hidden, gain_one)
        first_normalized = first_normalized.astype(jnp.bfloat16)
        linear = jnp.dot(first_normalized, qkv_full, preferred_element_type=jnp.float32)
        query_rotated = rotate_features(
            linear[:, : edges[0]].reshape(token_total, QUERY_HEADS, HEAD_SIZE),
            cosine_table,
            sine_table,
        ).astype(jnp.bfloat16)
        query_grouped = query_rotated.reshape(
            token_total, KEY_VALUE_HEADS, query_head_group, HEAD_SIZE
        )
        key_rot = rotate_features(
            linear[:, edges[0] : edges[1]].reshape(token_total, KEY_VALUE_HEADS, HEAD_SIZE),
            cosine_table,
            sine_table,
        ).astype(jnp.bfloat16)
        key_value = jnp.concatenate(
            [
                key_rot.reshape(token_total, key_width),
                linear[:, edges[1] :].astype(jnp.bfloat16),
            ],
            axis=1,
        )
        key_value_all = gather_rows(key_value).reshape(all_rows, 2, KEY_VALUE_HEADS, HEAD_SIZE)
        key_all, value_all = key_value_all[:, 0], key_value_all[:, 1]
        scores = (
            jnp.einsum("qhgd,khd->hgqk", query_grouped, key_all, preferred_element_type=jnp.float32)
            * score_scale
        )
        masked = jnp.where(causal, scores, -1e30)
        row_max = jnp.max(masked, axis=-1, keepdims=True)
        exp_scores = jnp.exp(masked - row_max)
        row_total = jnp.sum(exp_scores, axis=-1, keepdims=True)
        log_total = row_max + jnp.log(row_total)
        prob_low = (exp_scores / row_total).astype(jnp.bfloat16)
        attended = jnp.einsum(
            "hgqk,khd->qhgd", prob_low, value_all, preferred_element_type=jnp.float32
        )
        attended = attended.reshape(token_total, query_width).astype(jnp.bfloat16)
        middle = hidden + dot_f32(attended, output_full, (1,), (1,))
        normed_two, inv_two = norm_forward(middle, gain_two)
        normed_two = normed_two.astype(jnp.bfloat16)
        arrived = gather_rows(normed_two)
        share_all = shares_of(arrived, router_full, chosen_all[:, layer] > 0)
        share_own = shares_of(normed_two, router_full, chosen_hot[layer])
        share_local = lax.dynamic_slice_in_dim(share_all, my_group * exp_dev, exp_dev, axis=1)
        gate_val = jnp.dot(arrived, gate_full, preferred_element_type=jnp.float32)
        up_val = jnp.dot(arrived, up_full, preferred_element_type=jnp.float32)
        scaled_act = (jax.nn.silu(gate_val) * up_val * spread(share_local)).astype(jnp.bfloat16)
        out_rows = dot_f32(scaled_act, down_full, (1,), (1,)).astype(jnp.bfloat16)
        output = middle + sum_rows(out_rows)
        kept_state = (
            hidden,
            inv_one,
            first_normalized,
            query_grouped,
            key_all,
            value_all,
            log_total,
            attended,
            middle,
            inv_two,
            normed_two,
            share_own,
            share_local,
            arrived,
            gate_val.astype(jnp.bfloat16),
            up_val.astype(jnp.bfloat16),
            scaled_act,
            qkv_full,
            output_full,
            gain_one,
            gain_two,
            router_full,
            gate_full,
            up_full,
            down_full,
        )
        return (output, kept_state)

    hidden = inputs.astype(jnp.float32).reshape(token_total, model_width)
    kept_states = []
    for layer in range(LAYER_COUNT):
        hidden, kept_state = layer_forward(hidden, layer)
        kept_states.append(kept_state)
    output = hidden.astype(jnp.bfloat16).reshape(sequences_per_device, block_length, model_width)
    grad_hidden = cotangent.astype(jnp.float32).reshape(token_total, model_width)
    attention_list = [None] * LAYER_COUNT
    expert_list = [None] * LAYER_COUNT
    for layer in range(LAYER_COUNT - 1, -1, -1):
        (
            layer_hidden,
            inv_one,
            first_normalized,
            query_grouped,
            key_all,
            value_all,
            log_total,
            attended,
            middle,
            inv_two,
            normed_two,
            share_own,
            share_local,
            arrived,
            gate_low,
            up_low,
            scaled_act,
            qkv_full,
            output_full,
            gain_one,
            gain_two,
            router_full,
            gate_full,
            up_full,
            down_full,
        ) = kept_states[layer]
        grad_all = gather_rows(grad_hidden.astype(jnp.bfloat16))
        grad_down = dot_f32(grad_all, scaled_act, (0,), (0,)).astype(jnp.bfloat16)
        grad_all, grad_down = lax.optimization_barrier((grad_all, grad_down))
        expert_parts = [lax.psum_scatter(grad_down, "dp", scatter_dimension=0, tiled=True)]
        grad_scaled = jnp.dot(grad_all, down_full, preferred_element_type=jnp.float32)
        gate_val = gate_low.astype(jnp.float32)
        up_val = up_low.astype(jnp.float32)
        sigmoid_val = jax.nn.sigmoid(gate_val)
        silu_val = gate_val * sigmoid_val
        grad_gates = jnp.sum(
            (grad_scaled * silu_val * up_val).reshape(all_rows, exp_dev, ff_width), axis=2
        )
        grad_inner = grad_scaled * spread(share_local)
        grad_gate_val = (
            grad_inner * up_val * sigmoid_val * (1.0 + gate_val * (1.0 - sigmoid_val))
        ).astype(jnp.bfloat16)
        grad_up_val = (grad_inner * silu_val).astype(jnp.bfloat16)
        grad_rows = (
            dot_f32(grad_gate_val, gate_full, (1,), (1,))
            + dot_f32(grad_up_val, up_full, (1,), (1,))
        ).astype(jnp.bfloat16)
        grad_rows, grad_gate_val, grad_up_val = lax.optimization_barrier(
            (grad_rows, grad_gate_val, grad_up_val)
        )
        grad_gate_w = dot_f32(arrived, grad_gate_val, (0,), (0,)).astype(jnp.bfloat16)
        grad_up_w = dot_f32(arrived, grad_up_val, (0,), (0,)).astype(jnp.bfloat16)
        gates_high = grad_gates.astype(jnp.bfloat16)
        gates_low = (grad_gates - gates_high.astype(jnp.float32)).astype(jnp.bfloat16)
        gate_columns = jnp.zeros((all_rows, gate_width), jnp.bfloat16)
        gate_columns = lax.dynamic_update_slice_in_dim(
            gate_columns, gates_high, my_group * exp_dev, axis=1
        )
        gate_columns = lax.dynamic_update_slice_in_dim(
            gate_columns, gates_low, expert_total + my_group * exp_dev, axis=1
        )
        back = sum_rows(
            jnp.concatenate([grad_rows, gate_columns], axis=1)
        )
        back, grad_gate_w, grad_up_w = lax.optimization_barrier((back, grad_gate_w, grad_up_w))
        expert_parts += [
            lax.psum_scatter(grad_gate_w, "dp", scatter_dimension=0, tiled=True),
            lax.psum_scatter(grad_up_w, "dp", scatter_dimension=0, tiled=True),
        ]
        grad_gates_own = (
            back[:, model_width : model_width + expert_total]
            + back[:, model_width + expert_total : model_width + 2 * expert_total]
        )
        grad_logits = (
            share_own
            * (grad_gates_own - jnp.sum(share_own * grad_gates_own, axis=-1, keepdims=True))
        ).astype(jnp.bfloat16)
        grad_router = dot_f32(normed_two, grad_logits, (0,), (0,))
        grad_normed_two = back[:, :model_width] + dot_f32(grad_logits, router_full, (1,), (1,))
        grad_norm_mid, grad_gain_two = norm_backward(middle, inv_two, gain_two, grad_normed_two)
        grad_middle = grad_hidden + grad_norm_mid
        grad_branch = grad_middle.astype(jnp.bfloat16)
        grad_output_w = dot_f32(core_major(grad_branch), both_cores(attended), (0,), (0,))
        grad_attended = (
            dot_f32(grad_branch, output_full, (1,), (0,))
            .astype(jnp.bfloat16)
            .reshape(token_total, KEY_VALUE_HEADS, query_head_group, HEAD_SIZE)
        )
        layer_scores = (
            jnp.einsum("qhgd,khd->hgqk", query_grouped, key_all, preferred_element_type=jnp.float32)
            * score_scale
        )
        softmax_probs = jnp.exp(jnp.where(causal, layer_scores, -1e30) - log_total)
        grad_probs = jnp.einsum(
            "qhgd,khd->hgqk", grad_attended, value_all, preferred_element_type=jnp.float32
        )
        grad_scores = (
            softmax_probs
            * (grad_probs - jnp.sum(softmax_probs * grad_probs, axis=-1, keepdims=True))
        ).astype(jnp.bfloat16)
        grad_query = (
            jnp.einsum("hgqk,khd->qhgd", grad_scores, key_all, preferred_element_type=jnp.float32)
            * score_scale
        )
        grad_key_all = (
            jnp.einsum(
                "hgqk,qhgd->khd", grad_scores, query_grouped, preferred_element_type=jnp.float32
            )
            * score_scale
        )
        grad_value_all = jnp.einsum(
            "hgqk,qhgd->khd",
            softmax_probs.astype(jnp.bfloat16),
            grad_attended,
            preferred_element_type=jnp.float32,
        )
        grad_kv = sum_rows(
            jnp.concatenate(
                [
                    grad_key_all.reshape(all_rows, key_width).astype(jnp.bfloat16),
                    grad_value_all.reshape(all_rows, key_width).astype(jnp.bfloat16),
                ],
                axis=1,
            )
        )
        grad_query_lin = (
            rotate_features(
                grad_query.reshape(token_total, QUERY_HEADS, HEAD_SIZE), cosine_table, -sine_table
            )
            .astype(jnp.bfloat16)
            .reshape(token_total, query_width)
        )
        grad_key_lin = (
            rotate_features(
                grad_kv[:, :key_width].reshape(token_total, KEY_VALUE_HEADS, HEAD_SIZE),
                cosine_table,
                -sine_table,
            )
            .astype(jnp.bfloat16)
            .reshape(token_total, key_width)
        )
        grad_kv_lin = jnp.concatenate(
            [grad_key_lin, grad_kv[:, key_width:].astype(jnp.bfloat16)], axis=1
        )
        normed_split = core_major(first_normalized)
        grad_query_w = dot_f32(normed_split, both_cores(grad_query_lin), (0,), (0,))
        grad_kv_w = dot_f32(normed_split, both_cores(grad_kv_lin), (0,), (0,))
        grad_normed_one = dot_f32(grad_query_lin, qkv_full[:, : edges[0]], (1,), (1,)) + dot_f32(
            grad_kv_lin, qkv_full[:, edges[0] :], (1,), (1,)
        )
        grad_norm_in, grad_gain_one = norm_backward(
            layer_hidden, inv_one, gain_one, grad_normed_one
        )
        fill = jnp.zeros((model_width, small_width - expert_total - 2), jnp.bfloat16)
        small_part = jnp.concatenate(
            [
                grad_router.astype(jnp.bfloat16),
                grad_gain_one[:, None].astype(jnp.bfloat16),
                grad_gain_two[:, None].astype(jnp.bfloat16),
                fill,
            ],
            axis=1,
        )
        small_split = core_major(small_part.T).reshape(2, small_width, -1)
        small_half = jnp.sum(small_split.astype(jnp.float32), axis=0).T
        attention_list[layer] = (
            scatter_staged(grad_query_w.astype(jnp.bfloat16)),
            scatter_staged(grad_output_w.astype(jnp.bfloat16)),
            scatter_staged(
                jnp.concatenate([grad_kv_w, small_half], axis=1).astype(jnp.bfloat16)
            ),
        )
        expert_list[layer] = [
            part.reshape(-1, exp_dev, ff_width) for part in expert_parts
        ]
        grad_hidden = grad_middle + grad_norm_in
    query_grads, output_grads, other_grads = (
        stack_member(attention_list, member) for member in range(3)
    )
    down_grads, gate_grads, up_grads = (
        stack_member(expert_list, member).astype(jnp.float32) for member in range(3)
    )
    small_grads = other_grads[:, :, 2 * key_width :]
    return (
        output,
        grad_hidden.reshape(sequences_per_device, block_length, model_width),
        query_grads,
        other_grads[:, :, :key_width],
        other_grads[:, :, key_width : 2 * key_width],
        jnp.swapaxes(output_grads, 1, 2),
        small_grads[:, :, expert_total],
        small_grads[:, :, expert_total + 1],
        small_grads[:, :, :expert_total],
        gate_grads.transpose(0, 2, 1, 3),
        up_grads.transpose(0, 2, 1, 3),
        down_grads.transpose(0, 2, 3, 1),
    )


def solution(mesh):
    in_specs = (
        P("dp", "expert", None),
        P(None, "expert", "dp", None, None),
        P("dp", "expert", None),
        P(None, ("dp", "expert"), None),
        P(None, ("dp", "expert"), None),
        P(None, ("dp", "expert"), None),
        P(None, None, ("dp", "expert")),
        P(None, ("dp", "expert")),
        P(None, ("dp", "expert")),
        P(None, ("dp", "expert"), None),
        P(None, "expert", "dp", None),
        P(None, "expert", "dp", None),
        P(None, "expert", None, "dp"),
    )
    out_specs = (
        P("dp", "expert", None),
        P("dp", "expert", None),
        P(None, ("dp", "expert"), None),
        P(None, ("dp", "expert"), None),
        P(None, ("dp", "expert"), None),
        P(None, None, ("dp", "expert")),
        P(None, ("dp", "expert")),
        P(None, ("dp", "expert")),
        P(None, ("dp", "expert"), None),
        P(None, "expert", "dp", None),
        P(None, "expert", "dp", None),
        P(None, "expert", None, "dp"),
    )
    return jax.shard_map(body, mesh=mesh, in_specs=in_specs, out_specs=out_specs, check_vma=False)
```

```python
import math

import jax
import jax.numpy as jnp
from jax import lax
from jax.experimental import pallas as pl
from jax.experimental.pallas import tpu as pltpu
from jax.sharding import PartitionSpec as P

QUERY_HEADS = 24
KEY_VALUE_HEADS = 8
HEAD_SIZE = 64
LAYER_COUNT = 2


eps_norm = 1e-06
highest_precision = lax.Precision.HIGHEST


def rotary_tables(positions, half_dim):
    frequency = jnp.exp(-math.log(10000.0) * jnp.arange(half_dim, dtype=jnp.float32) / half_dim)
    angles = positions.astype(jnp.float32)[:, None] * frequency[None, :]
    return (jnp.cos(angles), jnp.sin(angles))


def rotate_features(values, cosine_table, sine_table):
    half_dim = values.shape[-1] // 2
    first_half = values[..., :half_dim]
    second_half = values[..., half_dim:]
    cos_part = cosine_table[:, None, :]
    sin_part = sine_table[:, None, :]
    return jnp.concatenate(
        [
            first_half * cos_part - second_half * sin_part,
            second_half * cos_part + first_half * sin_part,
        ],
        axis=-1,
    )


def norm_forward(values, gain_vec):
    inv_rms = lax.rsqrt(jnp.mean(values * values, axis=-1, keepdims=True) + eps_norm)
    return (values * inv_rms * gain_vec, inv_rms)


def norm_backward(values, inv_rms, gain_vec, upstream):
    scaled = upstream * gain_vec
    grad_gain = jnp.sum(upstream * values * inv_rms, axis=0)
    grad_values = inv_rms * (
        scaled - values * inv_rms * inv_rms * jnp.mean(scaled * values, axis=-1, keepdims=True)
    )
    return (grad_values, grad_gain)


def stack_member(layer_list, member):
    return jnp.stack([layer_parts[member] for layer_parts in layer_list], axis=0)


def exchange(blocks):
    return lax.all_to_all(blocks, "expert", split_axis=0, concat_axis=0, tiled=True)


def gather_rows(rows):
    groups = lax.axis_size("expert")
    blocks = exchange(jnp.broadcast_to(rows[None], (groups,) + rows.shape))
    return blocks.reshape((groups * rows.shape[0],) + rows.shape[1:])


def sum_rows(partial_rows):
    groups = lax.axis_size("expert")
    blocks = partial_rows.reshape((groups, -1) + partial_rows.shape[1:])
    return jnp.sum(exchange(blocks).astype(jnp.float32), axis=0)


def same_core():
    members = range(lax.axis_size("dp"))
    return [[i for i in members if i % 2 == core] for core in range(2)]


def swap_cores(values):
    return lax.ppermute(values, "dp", [(i, i ^ 1) for i in range(lax.axis_size("dp"))])


def exchange_chips(blocks):
    return lax.all_to_all(
        blocks, "dp", split_axis=0, concat_axis=0, axis_index_groups=same_core(), tiled=True
    )


def gather_staged(shard):
    chips = lax.axis_size("dp") // 2
    groups = lax.axis_size("expert")
    rows, width = shard.shape
    chip_rows = exchange_chips(jnp.broadcast_to(shard[None], (chips, rows, width)))
    return exchange(jnp.broadcast_to(chip_rows[None], (groups, chips, rows, width)))


def join_cores(own):
    width = own.shape[-1]
    other = swap_cores(own)
    first = lax.axis_index("dp") % 2 == 0
    both = jnp.stack([jnp.where(first, own, other), jnp.where(first, other, own)])
    return both.transpose(2, 0, 1, 3, 4).reshape(-1, width)


def core_major(columns):
    chips = lax.axis_size("dp") // 2
    groups = lax.axis_size("expert")
    split = columns.reshape(columns.shape[0], chips, 2, groups, -1)
    halves = split.transpose(2, 0, 3, 1, 4).reshape(2, columns.shape[0], -1)
    core = lax.axis_index("dp") % 2
    mine = lax.dynamic_index_in_dim(halves, core, 0, keepdims=False)
    theirs = lax.dynamic_index_in_dim(halves, 1 - core, 0, keepdims=False)
    return jnp.concatenate([mine, swap_cores(theirs)], axis=0)


def both_cores(rows):
    return jnp.concatenate([rows, swap_cores(rows)], axis=0)


def sum_groups(partial):
    blocks = exchange(partial.reshape(lax.axis_size("expert"), -1, partial.shape[1]))
    return jnp.sum(blocks.astype(jnp.float32), axis=0).astype(jnp.bfloat16)


def sum_chips(partial):
    blocks = exchange_chips(
        partial.reshape(lax.axis_size("dp") // 2, -1, partial.shape[1])
    )
    return jnp.sum(blocks.astype(jnp.float32), axis=0)


def dot_f32(left, right, left_dims, right_dims):
    return lax.dot_general(
        left, right, ((left_dims, right_dims), ((), ())), preferred_element_type=jnp.float32
    )


def contract(left, right, left_dim, right_dim):
    return lax.dot_general(
        left,
        right,
        (((left_dim,), (right_dim,)), ((), ())),
        preferred_element_type=jnp.float32,
    )


def pick_column(table, column):
    lanes = lax.broadcasted_iota(jnp.int32, table.shape, 1)
    return jnp.sum(jnp.where(lanes == column, table, 0.0), axis=1, keepdims=True)


def expert_forward_kernel(rows_ref, gate_ref, up_ref, share_ref, gate_out, up_out, act_out):
    rows = rows_ref[...]
    gate_val = contract(rows, gate_ref[...], 1, 0)
    up_val = contract(rows, up_ref[...], 1, 0)
    share = pick_column(share_ref[...], pl.program_id(0))
    gate_out[...] = gate_val.astype(jnp.bfloat16)
    up_out[...] = up_val.astype(jnp.bfloat16)
    act_out[...] = (gate_val * jax.nn.sigmoid(gate_val) * up_val * share).astype(jnp.bfloat16)


def expert_forward(rows, gate, up, share):
    row_total, width = rows.shape
    experts = share.shape[1]
    hidden = gate.shape[1] // experts
    tile = row_total // 2
    row_block = pl.BlockSpec((tile, width), lambda e, r: (r, 0))
    weight_block = pl.BlockSpec((width, hidden), lambda e, r: (0, e))
    hidden_block = pl.BlockSpec((tile, hidden), lambda e, r: (r, e))
    return pl.pallas_call(
        expert_forward_kernel,
        grid=(experts, 2),
        in_specs=[
            row_block,
            weight_block,
            weight_block,
            pl.BlockSpec((tile, experts), lambda e, r: (r, 0)),
        ],
        out_specs=[hidden_block] * 3,
        out_shape=[jax.ShapeDtypeStruct((row_total, gate.shape[1]), jnp.bfloat16)] * 3,
        cost_estimate=pl.CostEstimate(
            flops=4 * row_total * width * gate.shape[1],
            transcendentals=row_total * gate.shape[1],
            bytes_accessed=4 * width * gate.shape[1] + 6 * row_total * gate.shape[1],
        ),
    )(rows, gate, up, share)


def expert_backward_kernel(
    grad_ref,
    down_ref,
    gate_ref,
    up_ref,
    gate_val_ref,
    up_val_ref,
    share_ref,
    grad_gate_out,
    grad_up_out,
    rows_out,
    sums_out,
    rows_acc,
    sums_acc,
):
    expert = pl.program_id(0)
    tile = grad_ref.shape[0]
    window = pl.ds(pl.multiple_of(pl.program_id(1) * tile, tile), tile)
    grad_scaled = contract(grad_ref[...], down_ref[...], 1, 0)
    gate_val = gate_val_ref[...].astype(jnp.float32)
    up_val = up_val_ref[...].astype(jnp.float32)
    sigmoid_val = jax.nn.sigmoid(gate_val)
    silu_val = gate_val * sigmoid_val
    grad_sum = jnp.sum(grad_scaled * silu_val * up_val, axis=1, keepdims=True)
    grad_inner = grad_scaled * pick_column(share_ref[...], expert)
    grad_gate = (
        grad_inner * up_val * sigmoid_val * (1.0 + gate_val * (1.0 - sigmoid_val))
    ).astype(jnp.bfloat16)
    grad_up = (grad_inner * silu_val).astype(jnp.bfloat16)
    grad_gate_out[...] = grad_gate
    grad_up_out[...] = grad_up
    grad_rows = contract(grad_gate, gate_ref[...], 1, 1) + contract(
        grad_up, up_ref[...], 1, 1
    )
    lanes = lax.broadcasted_iota(jnp.int32, (tile, sums_acc.shape[1]), 1)
    grad_sums = jnp.where(lanes == expert, grad_sum, 0.0)

    @pl.when(expert == 0)
    def _():
        rows_acc[window, :] = grad_rows
        sums_acc[window, :] = grad_sums

    @pl.when(expert > 0)
    def _():
        rows_acc[window, :] += grad_rows
        sums_acc[window, :] += grad_sums

    @pl.when(expert == pl.num_programs(0) - 1)
    def _():
        rows_out[...] = rows_acc[window, :].astype(jnp.bfloat16)
        sums_out[...] = sums_acc[window, :]


def expert_backward(grad, down, gate, up, gate_val, up_val, share):
    row_total, width = grad.shape
    experts = share.shape[1]
    hidden = gate.shape[1] // experts
    tile = row_total // 2
    row_block = pl.BlockSpec((tile, width), lambda e, r: (r, 0))
    weight_block = pl.BlockSpec((width, hidden), lambda e, r: (0, e))
    hidden_block = pl.BlockSpec((tile, hidden), lambda e, r: (r, e))
    hidden_shape = jax.ShapeDtypeStruct((row_total, gate.shape[1]), jnp.bfloat16)

    def last_block(e, r):
        return (jnp.where(e == experts - 1, r, 0), 0)

    return pl.pallas_call(
        expert_backward_kernel,
        grid=(experts, 2),
        in_specs=[
            row_block,
            weight_block,
            weight_block,
            weight_block,
            hidden_block,
            hidden_block,
            pl.BlockSpec((tile, experts), lambda e, r: (r, 0)),
        ],
        out_specs=[
            hidden_block,
            hidden_block,
            pl.BlockSpec((tile, width), last_block),
            pl.BlockSpec((tile, 128), last_block),
        ],
        out_shape=[
            hidden_shape,
            hidden_shape,
            jax.ShapeDtypeStruct((row_total, width), jnp.bfloat16),
            jax.ShapeDtypeStruct((row_total, 128), jnp.float32),
        ],
        scratch_shapes=[
            pltpu.VMEM((row_total, width), jnp.float32),
            pltpu.VMEM((row_total, 128), jnp.float32),
        ],
        cost_estimate=pl.CostEstimate(
            flops=6 * row_total * width * gate.shape[1],
            transcendentals=row_total * gate.shape[1],
            bytes_accessed=6 * width * gate.shape[1] + 8 * row_total * gate.shape[1],
        ),
    )(grad, down, gate, up, gate_val, up_val, share)


def attention_probs(block_ref, query, key):
    scores = contract(key, query, 1, 1) * HEAD_SIZE ** (-0.5)
    key_at = lax.broadcasted_iota(jnp.int32, scores.shape, 0)
    query_at = lax.broadcasted_iota(jnp.int32, scores.shape, 1)
    offset = block_ref[0] * query.shape[0]
    masked = jnp.where(key_at <= query_at + offset, scores, -1e30)
    exp_scores = jnp.exp(masked - jnp.max(masked, axis=0, keepdims=True))
    return exp_scores / jnp.sum(exp_scores, axis=0, keepdims=True)


def head(values, index):
    return values[:, index * HEAD_SIZE : (index + 1) * HEAD_SIZE]


def attention_forward_kernel(block_ref, query_ref, key_ref, value_ref, out_ref):
    query, key, value = query_ref[...], key_ref[...], value_ref[...]
    group = QUERY_HEADS // KEY_VALUE_HEADS
    outs = []
    for index in range(2 * group):
        shared = index // group
        probs = attention_probs(block_ref, head(query, index), head(key, shared))
        outs.append(contract(head(value, shared), probs.astype(jnp.bfloat16), 0, 0))
    out_ref[...] = jnp.concatenate(outs, axis=0).T.astype(jnp.bfloat16)


def attention_specs(tokens, keys):
    pairs = KEY_VALUE_HEADS // 2
    query_block = pl.BlockSpec((tokens, QUERY_HEADS // pairs * HEAD_SIZE), lambda i, b: (0, i))
    key_block = pl.BlockSpec((keys, 2 * HEAD_SIZE), lambda i, b: (0, i))
    value_block = pl.BlockSpec((keys, 2 * HEAD_SIZE), lambda i, b: (0, i + pairs))
    return (pairs, query_block, key_block, value_block)


def attention_forward(block, query, key_value):
    tokens, width = query.shape
    keys = key_value.shape[0]
    pairs, query_block, key_block, value_block = attention_specs(tokens, keys)
    return pl.pallas_call(
        attention_forward_kernel,
        grid_spec=pltpu.PrefetchScalarGridSpec(
            num_scalar_prefetch=1,
            grid=(pairs,),
            in_specs=[query_block, key_block, value_block],
            out_specs=query_block,
        ),
        out_shape=jax.ShapeDtypeStruct((tokens, width), jnp.bfloat16),
        cost_estimate=pl.CostEstimate(
            flops=16 * tokens * width * keys,
            transcendentals=QUERY_HEADS * tokens * keys,
            bytes_accessed=4 * tokens * width + 2 * key_value.size,
        ),
    )(block, query, key_value, key_value)


def attention_backward_kernel(
    block_ref, query_ref, grad_ref, key_ref, value_ref, grad_query_out, grad_key_value_out
):
    query, grad, key, value = query_ref[...], grad_ref[...], key_ref[...], value_ref[...]
    group = QUERY_HEADS // KEY_VALUE_HEADS
    scale = HEAD_SIZE ** (-0.5)
    grad_queries, grad_keys, grad_values = [], [], []
    for shared in range(2):
        grad_key, grad_value = 0.0, 0.0
        for index in range(shared * group, (shared + 1) * group):
            query_one, grad_one = head(query, index), head(grad, index)
            probs = attention_probs(block_ref, query_one, head(key, shared))
            grad_probs = contract(head(value, shared), grad_one, 1, 1)
            centre = jnp.sum(probs * grad_probs, axis=0, keepdims=True)
            grad_scores = (probs * (grad_probs - centre)).astype(jnp.bfloat16)
            grad_queries.append(contract(head(key, shared), grad_scores, 0, 0) * scale)
            grad_key += contract(grad_scores, query_one, 1, 0)
            grad_value += contract(probs.astype(jnp.bfloat16), grad_one, 1, 0)
        grad_keys.append(grad_key * scale)
        grad_values.append(grad_value)
    grad_query_out[...] = jnp.concatenate(grad_queries, axis=0).T
    grad_key_value_out[...] = jnp.concatenate(grad_keys + grad_values, axis=1).astype(
        jnp.bfloat16
    )


def attention_backward(block, query, grad, key_value):
    tokens, width = query.shape
    keys = key_value.shape[0]
    pairs, query_block, key_block, value_block = attention_specs(tokens, keys)
    return pl.pallas_call(
        attention_backward_kernel,
        grid_spec=pltpu.PrefetchScalarGridSpec(
            num_scalar_prefetch=1,
            grid=(pairs,),
            in_specs=[query_block, query_block, key_block, value_block],
            out_specs=[
                query_block,
                pl.BlockSpec((keys, 4 * HEAD_SIZE), lambda i, b: (0, i)),
            ],
        ),
        out_shape=[
            jax.ShapeDtypeStruct((tokens, width), jnp.float32),
            jax.ShapeDtypeStruct(key_value.shape, jnp.bfloat16),
        ],
        cost_estimate=pl.CostEstimate(
            flops=40 * tokens * width * keys,
            transcendentals=QUERY_HEADS * tokens * keys,
            bytes_accessed=8 * tokens * width + 4 * key_value.size,
        ),
    )(block, query, grad, key_value, key_value)


def place_kernel(part_ref, held_ref, out_ref):
    del held_ref
    out_ref[0, 0] = part_ref[...].astype(jnp.float32)


def place_first_kernel(part_ref, out_ref):
    out_ref[0, 0] = part_ref[...].astype(jnp.float32)


def place_turned_kernel(part_ref, held_ref, out_ref):
    del held_ref
    out_ref[0, 0] = part_ref[...].astype(jnp.float32).T


def place_turned_first_kernel(part_ref, out_ref):
    out_ref[0, 0] = part_ref[...].astype(jnp.float32).T


def place(part, held, layer, experts, turned):
    rows = part.shape[0]
    hidden = part.shape[1] // experts
    block = (hidden, rows) if turned else (rows, hidden)
    kernels = (
        (place_turned_first_kernel, place_turned_kernel)
        if turned
        else (place_first_kernel, place_kernel)
    )
    in_specs = [pl.BlockSpec((rows, hidden), lambda e: (0, e))]
    operands = [part]
    if held is not None:
        in_specs.append(pl.BlockSpec(memory_space=pl.ANY))
        operands.append(held)
    return pl.pallas_call(
        kernels[held is not None],
        grid=(experts,),
        in_specs=in_specs,
        out_specs=pl.BlockSpec((1, 1) + block, lambda e: (layer, e, 0, 0)),
        out_shape=jax.ShapeDtypeStruct((LAYER_COUNT, experts) + block, jnp.float32),
        input_output_aliases={} if held is None else {1: 0},
    )(*operands)


def body(
    inputs,
    routes,
    cotangent,
    query_weight,
    key_projection_weight,
    value_projection_weight,
    output_weight,
    attention_gain,
    expert_gain,
    router_weight,
    gate_weight,
    up_weight,
    down_weight,
):
    sequences_per_device, block_length, model_width = inputs.shape
    token_total = sequences_per_device * block_length
    exp_dev = gate_weight.shape[1]
    groups = lax.axis_size("expert")
    expert_total = exp_dev * groups
    all_rows = token_total * groups
    query_width = query_weight.shape[2]
    key_width = key_projection_weight.shape[2]
    my_group = lax.axis_index("expert")
    positions = my_group * block_length + jnp.arange(block_length, dtype=jnp.int32)
    cosine_table, sine_table = rotary_tables(positions, HEAD_SIZE // 2)
    block_at = my_group.astype(jnp.int32).reshape(1)
    expert_ids = jnp.arange(expert_total, dtype=jnp.int32)
    small_width = -(-(expert_total + 2) // 128) * 128
    gate_width = -(-(2 * expert_total) // 128) * 128
    edges = (
        query_width,
        query_width + key_width,
        query_width + 2 * key_width,
        query_width + 2 * key_width + model_width,
        query_width + 2 * key_width + model_width + expert_total,
        query_width + 2 * key_width + model_width + expert_total + 1,
    )

    def pack_attention(query_part, key_part, value_part, output_part, router_part, one, two):
        rows = query_part.shape[0]
        fill = jnp.zeros((rows, small_width - expert_total - 2), query_part.dtype)
        return jnp.concatenate(
            [
                query_part,
                key_part,
                value_part,
                output_part,
                router_part,
                one[:, None],
                two[:, None],
                fill,
            ],
            axis=1,
        )

    chosen_hot = jnp.any(
        routes.reshape(LAYER_COUNT, token_total, -1)[:, :, :, None] == expert_ids, axis=2
    )
    chosen_all = gather_rows(
        jnp.moveaxis(chosen_hot, 0, 1).reshape(token_total, -1).astype(jnp.bfloat16)
    ).reshape(all_rows, LAYER_COUNT, expert_total)

    shards = [
        pack_attention(
            query_weight[layer],
            key_projection_weight[layer],
            value_projection_weight[layer],
            output_weight[layer].T,
            router_weight[layer],
            attention_gain[layer],
            expert_gain[layer],
        )
        for layer in range(LAYER_COUNT)
    ]
    packed = [lax.all_gather(shards[0], ("dp", "expert"), axis=0, tiled=True)]
    staged = [gather_staged(shard) for shard in shards[1:]]
    inputs, staged = lax.optimization_barrier((inputs, staged))
    packed += [join_cores(own) for own in staged]
    ff_width = gate_weight.shape[3]
    hidden_width = exp_dev * ff_width
    gathered = [
        tuple(
            lax.all_gather(rows.reshape(-1, hidden_width), "dp", axis=0, tiled=True)
            for rows in (
                gate_weight[layer].transpose(1, 0, 2),
                up_weight[layer].transpose(1, 0, 2),
                down_weight[layer].transpose(2, 0, 1),
            )
        )
        for layer in range(LAYER_COUNT)
    ]

    def shares_of(rows, router_full, hot):
        logits = jnp.dot(rows, router_full, preferred_element_type=jnp.float32)
        masked = jnp.where(hot, logits, -1e30)
        exps = jnp.where(hot, jnp.exp(masked - jnp.max(masked, axis=1, keepdims=True)), 0.0)
        return exps / jnp.sum(exps, axis=1, keepdims=True)

    def layer_forward(hidden, layer):
        full = packed[layer]
        qkv_full = full[:, : edges[2]]
        output_full = full[:, edges[2] : edges[3]]
        router_full = full[:, edges[3] : edges[4]]
        gain_one = full[:, edges[4]].astype(jnp.float32)
        gain_two = full[:, edges[5]].astype(jnp.float32)
        gate_full, up_full, down_full = gathered[layer]
        first_normalized, inv_one = norm_forward(hidden, gain_one)
        first_normalized = first_normalized.astype(jnp.bfloat16)
        linear = jnp.dot(first_normalized, qkv_full, preferred_element_type=jnp.float32)
        query_rotated = rotate_features(
            linear[:, : edges[0]].reshape(token_total, QUERY_HEADS, HEAD_SIZE),
            cosine_table,
            sine_table,
        ).astype(jnp.bfloat16)
        query_rotated = query_rotated.reshape(token_total, query_width)
        key_rot = rotate_features(
            linear[:, edges[0] : edges[1]].reshape(token_total, KEY_VALUE_HEADS, HEAD_SIZE),
            cosine_table,
            sine_table,
        ).astype(jnp.bfloat16)
        key_value = jnp.concatenate(
            [
                key_rot.reshape(token_total, key_width),
                linear[:, edges[1] :].astype(jnp.bfloat16),
            ],
            axis=1,
        )
        key_value_all = gather_rows(key_value)
        attended = attention_forward(block_at, query_rotated, key_value_all)
        middle = hidden + dot_f32(attended, output_full, (1,), (1,))
        normed_two, inv_two = norm_forward(middle, gain_two)
        normed_two = normed_two.astype(jnp.bfloat16)
        arrived = gather_rows(normed_two)
        share_all = shares_of(arrived, router_full, chosen_all[:, layer] > 0)
        share_own = shares_of(normed_two, router_full, chosen_hot[layer])
        share_local = lax.dynamic_slice_in_dim(share_all, my_group * exp_dev, exp_dev, axis=1)
        gate_low, up_low, scaled_act = expert_forward(
            arrived, gate_full, up_full, share_local
        )
        out_rows = dot_f32(scaled_act, down_full, (1,), (1,)).astype(jnp.bfloat16)
        output = middle + sum_rows(out_rows)
        kept_state = (
            hidden,
            inv_one,
            first_normalized,
            query_rotated,
            key_value_all,
            attended,
            middle,
            inv_two,
            normed_two,
            share_own,
            share_local,
            arrived,
            gate_low,
            up_low,
            scaled_act,
            qkv_full,
            output_full,
            gain_one,
            gain_two,
            router_full,
            gate_full,
            up_full,
            down_full,
        )
        return (output, kept_state)

    hidden = inputs.astype(jnp.float32).reshape(token_total, model_width)
    kept_states = []
    for layer in range(LAYER_COUNT):
        hidden, kept_state = layer_forward(hidden, layer)
        kept_states.append(kept_state)
    output = hidden.astype(jnp.bfloat16).reshape(sequences_per_device, block_length, model_width)
    grad_hidden = cotangent.astype(jnp.float32).reshape(token_total, model_width)
    attention_list = [None] * LAYER_COUNT
    expert_held = [None] * 3
    waiting = None
    for layer in range(LAYER_COUNT - 1, -1, -1):
        (
            layer_hidden,
            inv_one,
            first_normalized,
            query_rotated,
            key_value_all,
            attended,
            middle,
            inv_two,
            normed_two,
            share_own,
            share_local,
            arrived,
            gate_low,
            up_low,
            scaled_act,
            qkv_full,
            output_full,
            gain_one,
            gain_two,
            router_full,
            gate_full,
            up_full,
            down_full,
        ) = kept_states[layer]
        grad_all = gather_rows(grad_hidden.astype(jnp.bfloat16))
        if waiting is not None:
            grad_all, waiting = lax.optimization_barrier((grad_all, waiting))
            waiting = [sum_groups(part) for part in waiting]
        grad_down = dot_f32(grad_all, scaled_act, (0,), (0,)).astype(jnp.bfloat16)
        grad_all, grad_down = lax.optimization_barrier((grad_all, grad_down))
        expert_parts = [lax.psum_scatter(grad_down, "dp", scatter_dimension=0, tiled=True)]
        grad_gate_val, grad_up_val, grad_rows, grad_sums = expert_backward(
            grad_all, down_full, gate_full, up_full, gate_low, up_low, share_local
        )
        grad_gates = grad_sums[:, :exp_dev]
        if waiting is not None:
            grad_rows, waiting = lax.optimization_barrier((grad_rows, waiting))
            attention_list[layer + 1] = sum_chips(jnp.concatenate(waiting, axis=1))
        grad_gate_w = dot_f32(arrived, grad_gate_val, (0,), (0,)).astype(jnp.bfloat16)
        grad_up_w = dot_f32(arrived, grad_up_val, (0,), (0,)).astype(jnp.bfloat16)
        gates_high = grad_gates.astype(jnp.bfloat16)
        gates_low = (grad_gates - gates_high.astype(jnp.float32)).astype(jnp.bfloat16)
        gate_columns = jnp.zeros((all_rows, gate_width), jnp.bfloat16)
        gate_columns = lax.dynamic_update_slice_in_dim(
            gate_columns, gates_high, my_group * exp_dev, axis=1
        )
        gate_columns = lax.dynamic_update_slice_in_dim(
            gate_columns, gates_low, expert_total + my_group * exp_dev, axis=1
        )
        back = sum_rows(
            jnp.concatenate([grad_rows, gate_columns], axis=1)
        )
        if waiting is not None:
            back, attention_list[layer + 1] = lax.optimization_barrier(
                (back, attention_list[layer + 1])
            )
        back, grad_gate_w, grad_up_w = lax.optimization_barrier((back, grad_gate_w, grad_up_w))
        expert_parts += [
            lax.psum_scatter(grad_gate_w, "dp", scatter_dimension=0, tiled=True),
            lax.psum_scatter(grad_up_w, "dp", scatter_dimension=0, tiled=True),
        ]
        grad_gates_own = (
            back[:, model_width : model_width + expert_total]
            + back[:, model_width + expert_total : model_width + 2 * expert_total]
        )
        grad_logits = (
            share_own
            * (grad_gates_own - jnp.sum(share_own * grad_gates_own, axis=-1, keepdims=True))
        ).astype(jnp.bfloat16)
        grad_router = dot_f32(normed_two, grad_logits, (0,), (0,))
        grad_normed_two = back[:, :model_width] + dot_f32(grad_logits, router_full, (1,), (1,))
        grad_norm_mid, grad_gain_two = norm_backward(middle, inv_two, gain_two, grad_normed_two)
        grad_middle = grad_hidden + grad_norm_mid
        grad_branch = grad_middle.astype(jnp.bfloat16)
        grad_output_w = dot_f32(core_major(grad_branch), both_cores(attended), (0,), (0,))
        grad_attended = dot_f32(grad_branch, output_full, (1,), (0,)).astype(jnp.bfloat16)
        grad_query, grad_key_value_all = attention_backward(
            block_at, query_rotated, grad_attended, key_value_all
        )
        grad_kv = sum_rows(grad_key_value_all).reshape(token_total, -1, 2, 2 * HEAD_SIZE)
        grad_kv = grad_kv.transpose(0, 2, 1, 3).reshape(token_total, 2 * key_width)
        grad_query_lin = (
            rotate_features(
                grad_query.reshape(token_total, QUERY_HEADS, HEAD_SIZE), cosine_table, -sine_table
            )
            .astype(jnp.bfloat16)
            .reshape(token_total, query_width)
        )
        grad_key_lin = (
            rotate_features(
                grad_kv[:, :key_width].reshape(token_total, KEY_VALUE_HEADS, HEAD_SIZE),
                cosine_table,
                -sine_table,
            )
            .astype(jnp.bfloat16)
            .reshape(token_total, key_width)
        )
        grad_kv_lin = jnp.concatenate(
            [grad_key_lin, grad_kv[:, key_width:].astype(jnp.bfloat16)], axis=1
        )
        normed_split = core_major(first_normalized)
        grad_query_w = dot_f32(normed_split, both_cores(grad_query_lin), (0,), (0,))
        grad_kv_w = dot_f32(normed_split, both_cores(grad_kv_lin), (0,), (0,))
        grad_normed_one = dot_f32(grad_query_lin, qkv_full[:, : edges[0]], (1,), (1,)) + dot_f32(
            grad_kv_lin, qkv_full[:, edges[0] :], (1,), (1,)
        )
        grad_norm_in, grad_gain_one = norm_backward(
            layer_hidden, inv_one, gain_one, grad_normed_one
        )
        fill = jnp.zeros((model_width, small_width - expert_total - 2), jnp.bfloat16)
        small_part = jnp.concatenate(
            [
                grad_router.astype(jnp.bfloat16),
                grad_gain_one[:, None].astype(jnp.bfloat16),
                grad_gain_two[:, None].astype(jnp.bfloat16),
                fill,
            ],
            axis=1,
        )
        small_split = core_major(small_part.T).reshape(2, small_width, -1)
        small_half = jnp.sum(small_split.astype(jnp.float32), axis=0).T
        grad_kv_w = jnp.concatenate([grad_kv_w, small_half], axis=1)
        partials = [grad_output_w, grad_query_w, grad_kv_w]
        partials = [partial.astype(jnp.bfloat16) for partial in partials]
        if layer > 0:
            waiting = partials
        else:
            early = [sum_groups(part) for part in partials[:2]]
            attention_list[layer] = jnp.concatenate(
                [sum_chips(jnp.concatenate(early, axis=1)), sum_chips(sum_groups(partials[2]))],
                axis=1,
            )
        expert_held = [
            place(part, held, layer, exp_dev, turned)
            for part, held, turned in zip(expert_parts, expert_held, (True, False, False))
        ]
        grad_hidden = grad_middle + grad_norm_in
    stacked = jnp.stack(attention_list)
    cuts = [query_width, query_width, key_width, key_width, expert_total, 1, 1]
    cuts = [sum(cuts[:index]) for index in range(len(cuts) + 1)]
    output_grads, query_grads, key_grads, value_grads, router_grads, one, two = (
        stacked[:, :, start:stop] for start, stop in zip(cuts[:-1], cuts[1:])
    )
    down_grads, gate_grads, up_grads = expert_held
    return (
        output,
        grad_hidden.reshape(sequences_per_device, block_length, model_width),
        query_grads,
        key_grads,
        value_grads,
        jnp.swapaxes(output_grads, 1, 2),
        one[:, :, 0],
        two[:, :, 0],
        router_grads,
        gate_grads,
        up_grads,
        down_grads,
    )


def solution(mesh):
    in_specs = (
        P("dp", "expert", None),
        P(None, "expert", "dp", None, None),
        P("dp", "expert", None),
        P(None, ("dp", "expert"), None),
        P(None, ("dp", "expert"), None),
        P(None, ("dp", "expert"), None),
        P(None, None, ("dp", "expert")),
        P(None, ("dp", "expert")),
        P(None, ("dp", "expert")),
        P(None, ("dp", "expert"), None),
        P(None, "expert", "dp", None),
        P(None, "expert", "dp", None),
        P(None, "expert", None, "dp"),
    )
    out_specs = (
        P("dp", "expert", None),
        P("dp", "expert", None),
        P(None, ("dp", "expert"), None),
        P(None, ("dp", "expert"), None),
        P(None, ("dp", "expert"), None),
        P(None, None, ("dp", "expert")),
        P(None, ("dp", "expert")),
        P(None, ("dp", "expert")),
        P(None, ("dp", "expert"), None),
        P(None, "expert", "dp", None),
        P(None, "expert", "dp", None),
        P(None, "expert", None, "dp"),
    )
    return jax.shard_map(body, mesh=mesh, in_specs=in_specs, out_specs=out_specs, check_vma=False)
```

```python
import math

import jax
import jax.numpy as jnp
from jax import lax
from jax.experimental import pallas as pl
from jax.experimental.pallas import tpu as pltpu
from jax.sharding import PartitionSpec as P

QUERY_HEADS = 24
KEY_VALUE_HEADS = 8
HEAD_SIZE = 64
LAYER_COUNT = 2


eps_norm = 1e-06
highest_precision = lax.Precision.HIGHEST


def rotary_tables(positions, half_dim):
    frequency = jnp.exp(-math.log(10000.0) * jnp.arange(half_dim, dtype=jnp.float32) / half_dim)
    angles = positions.astype(jnp.float32)[:, None] * frequency[None, :]
    return (jnp.cos(angles), jnp.sin(angles))


def rotate_features(values, cosine_table, sine_table):
    half_dim = values.shape[-1] // 2
    first_half = values[..., :half_dim]
    second_half = values[..., half_dim:]
    cos_part = cosine_table[:, None, :]
    sin_part = sine_table[:, None, :]
    return jnp.concatenate(
        [
            first_half * cos_part - second_half * sin_part,
            second_half * cos_part + first_half * sin_part,
        ],
        axis=-1,
    )


def norm_forward(values, gain_vec):
    inv_rms = lax.rsqrt(jnp.mean(values * values, axis=-1, keepdims=True) + eps_norm)
    return (values * inv_rms * gain_vec, inv_rms)


def norm_backward(values, inv_rms, gain_vec, upstream):
    scaled = upstream * gain_vec
    grad_gain = jnp.sum(upstream * values * inv_rms, axis=0)
    grad_values = inv_rms * (
        scaled - values * inv_rms * inv_rms * jnp.mean(scaled * values, axis=-1, keepdims=True)
    )
    return (grad_values, grad_gain)


def stack_member(layer_list, member):
    return jnp.stack([layer_parts[member] for layer_parts in layer_list], axis=0)


def exchange(blocks):
    return lax.all_to_all(blocks, "expert", split_axis=0, concat_axis=0, tiled=True)


def gather_rows(rows):
    groups = lax.axis_size("expert")
    blocks = exchange(jnp.broadcast_to(rows[None], (groups,) + rows.shape))
    return blocks.reshape((groups * rows.shape[0],) + rows.shape[1:])


def sum_rows(partial_rows):
    groups = lax.axis_size("expert")
    blocks = partial_rows.reshape((groups, -1) + partial_rows.shape[1:])
    return jnp.sum(exchange(blocks).astype(jnp.float32), axis=0)


def same_core():
    members = range(lax.axis_size("dp"))
    return [[i for i in members if i % 2 == core] for core in range(2)]


def swap_cores(values):
    return lax.ppermute(values, "dp", [(i, i ^ 1) for i in range(lax.axis_size("dp"))])


def exchange_chips(blocks):
    return lax.all_to_all(
        blocks, "dp", split_axis=0, concat_axis=0, axis_index_groups=same_core(), tiled=True
    )


def gather_chips(shard):
    chips = lax.axis_size("dp") // 2
    return exchange_chips(jnp.broadcast_to(shard[None], (chips,) + shard.shape))


def gather_groups(chip_rows):
    groups = lax.axis_size("expert")
    return exchange(jnp.broadcast_to(chip_rows[None], (groups,) + chip_rows.shape))


def join_cores(own):
    width = own.shape[-1]
    other = swap_cores(own)
    first = lax.axis_index("dp") % 2 == 0
    both = jnp.stack([jnp.where(first, own, other), jnp.where(first, other, own)])
    return both.transpose(2, 0, 1, 3, 4).reshape(-1, width)


def core_major(columns):
    chips = lax.axis_size("dp") // 2
    groups = lax.axis_size("expert")
    split = columns.reshape(columns.shape[0], chips, 2, groups, -1)
    halves = split.transpose(2, 0, 3, 1, 4).reshape(2, columns.shape[0], -1)
    core = lax.axis_index("dp") % 2
    mine = lax.dynamic_index_in_dim(halves, core, 0, keepdims=False)
    theirs = lax.dynamic_index_in_dim(halves, 1 - core, 0, keepdims=False)
    return jnp.concatenate([mine, swap_cores(theirs)], axis=0)


def both_cores(rows):
    return jnp.concatenate([rows, swap_cores(rows)], axis=0)


def halve(blocks, axis_name, step):
    size = lax.axis_size(axis_name)
    side = (lax.axis_index(axis_name) // step) % 2
    mine = lax.dynamic_index_in_dim(blocks, side, 0, keepdims=False)
    theirs = lax.dynamic_index_in_dim(blocks, 1 - side, 0, keepdims=False)
    arrived = lax.ppermute(theirs, axis_name, [(i, i ^ step) for i in range(size)])
    return (mine.astype(jnp.float32) + arrived.astype(jnp.float32)).astype(jnp.bfloat16)


def halvings(axis_name, least):
    steps = [lax.axis_size(axis_name) // 2]
    while steps[-1] > least:
        steps.append(steps[-1] // 2)
    return [(axis_name, step) for step in steps]


def halve_all(partial, steps):
    width = partial.shape[-1]
    for axis_name, step in steps:
        partial = halve(partial.reshape(2, -1, width), axis_name, step)
    return partial


def dot_f32(left, right, left_dims, right_dims):
    return lax.dot_general(
        left, right, ((left_dims, right_dims), ((), ())), preferred_element_type=jnp.float32
    )


def contract(left, right, left_dim, right_dim):
    return lax.dot_general(
        left,
        right,
        (((left_dim,), (right_dim,)), ((), ())),
        preferred_element_type=jnp.float32,
    )


def pick_column(table, column):
    lanes = lax.broadcasted_iota(jnp.int32, table.shape, 1)
    return jnp.sum(jnp.where(lanes == column, table, 0.0), axis=1, keepdims=True)


def expert_forward_kernel(rows_ref, gate_ref, up_ref, share_ref, gate_out, up_out, act_out):
    rows = rows_ref[...]
    gate_val = contract(rows, gate_ref[...], 1, 0)
    up_val = contract(rows, up_ref[...], 1, 0)
    share = pick_column(share_ref[...], pl.program_id(0))
    gate_out[...] = gate_val.astype(jnp.bfloat16)
    up_out[...] = up_val.astype(jnp.bfloat16)
    act_out[...] = (gate_val * jax.nn.sigmoid(gate_val) * up_val * share).astype(jnp.bfloat16)


def expert_forward(rows, gate, up, share):
    row_total, width = rows.shape
    experts = share.shape[1]
    hidden = gate.shape[1] // experts
    tile = row_total // 2
    row_block = pl.BlockSpec((tile, width), lambda e, r: (r, 0))
    weight_block = pl.BlockSpec((width, hidden), lambda e, r: (0, e))
    hidden_block = pl.BlockSpec((tile, hidden), lambda e, r: (r, e))
    return pl.pallas_call(
        expert_forward_kernel,
        grid=(experts, 2),
        in_specs=[
            row_block,
            weight_block,
            weight_block,
            pl.BlockSpec((tile, experts), lambda e, r: (r, 0)),
        ],
        out_specs=[hidden_block] * 3,
        out_shape=[jax.ShapeDtypeStruct((row_total, gate.shape[1]), jnp.bfloat16)] * 3,
        cost_estimate=pl.CostEstimate(
            flops=4 * row_total * width * gate.shape[1],
            transcendentals=row_total * gate.shape[1],
            bytes_accessed=4 * width * gate.shape[1] + 6 * row_total * gate.shape[1],
        ),
    )(rows, gate, up, share)


def expert_backward_kernel(
    grad_ref,
    down_ref,
    gate_ref,
    up_ref,
    gate_val_ref,
    up_val_ref,
    share_ref,
    grad_gate_out,
    grad_up_out,
    rows_out,
    sums_out,
    rows_acc,
    sums_acc,
):
    expert = pl.program_id(0)
    tile = grad_ref.shape[0]
    window = pl.ds(pl.multiple_of(pl.program_id(1) * tile, tile), tile)
    grad_scaled = contract(grad_ref[...], down_ref[...], 1, 0)
    gate_val = gate_val_ref[...].astype(jnp.float32)
    up_val = up_val_ref[...].astype(jnp.float32)
    sigmoid_val = jax.nn.sigmoid(gate_val)
    silu_val = gate_val * sigmoid_val
    grad_sum = jnp.sum(grad_scaled * silu_val * up_val, axis=1, keepdims=True)
    grad_inner = grad_scaled * pick_column(share_ref[...], expert)
    grad_gate = (
        grad_inner * up_val * sigmoid_val * (1.0 + gate_val * (1.0 - sigmoid_val))
    ).astype(jnp.bfloat16)
    grad_up = (grad_inner * silu_val).astype(jnp.bfloat16)
    grad_gate_out[...] = grad_gate
    grad_up_out[...] = grad_up
    grad_rows = contract(grad_gate, gate_ref[...], 1, 1) + contract(
        grad_up, up_ref[...], 1, 1
    )
    lanes = lax.broadcasted_iota(jnp.int32, (tile, sums_acc.shape[1]), 1)
    grad_sums = jnp.where(lanes == expert, grad_sum, 0.0)

    @pl.when(expert == 0)
    def _():
        rows_acc[window, :] = grad_rows
        sums_acc[window, :] = grad_sums

    @pl.when(expert > 0)
    def _():
        rows_acc[window, :] += grad_rows
        sums_acc[window, :] += grad_sums

    @pl.when(expert == pl.num_programs(0) - 1)
    def _():
        rows_out[...] = rows_acc[window, :].astype(jnp.bfloat16)
        sums_out[...] = sums_acc[window, :]


def expert_backward(grad, down, gate, up, gate_val, up_val, share):
    row_total, width = grad.shape
    experts = share.shape[1]
    hidden = gate.shape[1] // experts
    tile = row_total // 2
    row_block = pl.BlockSpec((tile, width), lambda e, r: (r, 0))
    weight_block = pl.BlockSpec((width, hidden), lambda e, r: (0, e))
    hidden_block = pl.BlockSpec((tile, hidden), lambda e, r: (r, e))
    hidden_shape = jax.ShapeDtypeStruct((row_total, gate.shape[1]), jnp.bfloat16)

    def last_block(e, r):
        return (jnp.where(e == experts - 1, r, 0), 0)

    return pl.pallas_call(
        expert_backward_kernel,
        grid=(experts, 2),
        in_specs=[
            row_block,
            weight_block,
            weight_block,
            weight_block,
            hidden_block,
            hidden_block,
            pl.BlockSpec((tile, experts), lambda e, r: (r, 0)),
        ],
        out_specs=[
            hidden_block,
            hidden_block,
            pl.BlockSpec((tile, width), last_block),
            pl.BlockSpec((tile, 128), last_block),
        ],
        out_shape=[
            hidden_shape,
            hidden_shape,
            jax.ShapeDtypeStruct((row_total, width), jnp.bfloat16),
            jax.ShapeDtypeStruct((row_total, 128), jnp.float32),
        ],
        scratch_shapes=[
            pltpu.VMEM((row_total, width), jnp.float32),
            pltpu.VMEM((row_total, 128), jnp.float32),
        ],
        cost_estimate=pl.CostEstimate(
            flops=6 * row_total * width * gate.shape[1],
            transcendentals=row_total * gate.shape[1],
            bytes_accessed=6 * width * gate.shape[1] + 8 * row_total * gate.shape[1],
        ),
    )(grad, down, gate, up, gate_val, up_val, share)


def attention_probs(block_ref, query, key):
    scores = contract(key, query, 1, 1) * HEAD_SIZE ** (-0.5)
    key_at = lax.broadcasted_iota(jnp.int32, scores.shape, 0)
    query_at = lax.broadcasted_iota(jnp.int32, scores.shape, 1)
    offset = block_ref[0] * query.shape[0]
    masked = jnp.where(key_at <= query_at + offset, scores, -1e30)
    exp_scores = jnp.exp(masked - jnp.max(masked, axis=0, keepdims=True))
    return exp_scores / jnp.sum(exp_scores, axis=0, keepdims=True)


def head(values, index):
    return values[:, index * HEAD_SIZE : (index + 1) * HEAD_SIZE]


def attention_forward_kernel(block_ref, query_ref, key_ref, value_ref, out_ref):
    query, key, value = query_ref[...], key_ref[...], value_ref[...]
    group = QUERY_HEADS // KEY_VALUE_HEADS
    outs = []
    for index in range(2 * group):
        shared = index // group
        probs = attention_probs(block_ref, head(query, index), head(key, shared))
        outs.append(contract(head(value, shared), probs.astype(jnp.bfloat16), 0, 0))
    out_ref[...] = jnp.concatenate(outs, axis=0).T.astype(jnp.bfloat16)


def attention_specs(tokens, keys):
    pairs = KEY_VALUE_HEADS // 2
    query_block = pl.BlockSpec((tokens, QUERY_HEADS // pairs * HEAD_SIZE), lambda i, b: (0, i))
    key_block = pl.BlockSpec((keys, 2 * HEAD_SIZE), lambda i, b: (0, i))
    value_block = pl.BlockSpec((keys, 2 * HEAD_SIZE), lambda i, b: (0, i + pairs))
    return (pairs, query_block, key_block, value_block)


def attention_forward(block, query, key_value):
    tokens, width = query.shape
    keys = key_value.shape[0]
    pairs, query_block, key_block, value_block = attention_specs(tokens, keys)
    return pl.pallas_call(
        attention_forward_kernel,
        grid_spec=pltpu.PrefetchScalarGridSpec(
            num_scalar_prefetch=1,
            grid=(pairs,),
            in_specs=[query_block, key_block, value_block],
            out_specs=query_block,
        ),
        out_shape=jax.ShapeDtypeStruct((tokens, width), jnp.bfloat16),
        cost_estimate=pl.CostEstimate(
            flops=16 * tokens * width * keys,
            transcendentals=QUERY_HEADS * tokens * keys,
            bytes_accessed=4 * tokens * width + 2 * key_value.size,
        ),
    )(block, query, key_value, key_value)


def attention_backward_kernel(
    block_ref, query_ref, grad_ref, key_ref, value_ref, grad_query_out, grad_key_value_out
):
    query, grad, key, value = query_ref[...], grad_ref[...], key_ref[...], value_ref[...]
    group = QUERY_HEADS // KEY_VALUE_HEADS
    scale = HEAD_SIZE ** (-0.5)
    grad_queries, grad_keys, grad_values = [], [], []
    for shared in range(2):
        grad_key, grad_value = 0.0, 0.0
        for index in range(shared * group, (shared + 1) * group):
            query_one, grad_one = head(query, index), head(grad, index)
            probs = attention_probs(block_ref, query_one, head(key, shared))
            grad_probs = contract(head(value, shared), grad_one, 1, 1)
            centre = jnp.sum(probs * grad_probs, axis=0, keepdims=True)
            grad_scores = (probs * (grad_probs - centre)).astype(jnp.bfloat16)
            grad_queries.append(contract(head(key, shared), grad_scores, 0, 0) * scale)
            grad_key += contract(grad_scores, query_one, 1, 0)
            grad_value += contract(probs.astype(jnp.bfloat16), grad_one, 1, 0)
        grad_keys.append(grad_key * scale)
        grad_values.append(grad_value)
    grad_query_out[...] = jnp.concatenate(grad_queries, axis=0).T
    grad_key_value_out[...] = jnp.concatenate(grad_keys + grad_values, axis=1).astype(
        jnp.bfloat16
    )


def attention_backward(block, query, grad, key_value):
    tokens, width = query.shape
    keys = key_value.shape[0]
    pairs, query_block, key_block, value_block = attention_specs(tokens, keys)
    return pl.pallas_call(
        attention_backward_kernel,
        grid_spec=pltpu.PrefetchScalarGridSpec(
            num_scalar_prefetch=1,
            grid=(pairs,),
            in_specs=[query_block, query_block, key_block, value_block],
            out_specs=[
                query_block,
                pl.BlockSpec((keys, 4 * HEAD_SIZE), lambda i, b: (0, i)),
            ],
        ),
        out_shape=[
            jax.ShapeDtypeStruct((tokens, width), jnp.float32),
            jax.ShapeDtypeStruct(key_value.shape, jnp.bfloat16),
        ],
        cost_estimate=pl.CostEstimate(
            flops=40 * tokens * width * keys,
            transcendentals=QUERY_HEADS * tokens * keys,
            bytes_accessed=8 * tokens * width + 4 * key_value.size,
        ),
    )(block, query, grad, key_value, key_value)


def place_kernel(part_ref, held_ref, out_ref):
    del held_ref
    out_ref[0, 0] = part_ref[...].astype(jnp.float32)


def place_first_kernel(part_ref, out_ref):
    out_ref[0, 0] = part_ref[...].astype(jnp.float32)


def place(part, held, layer, experts):
    rows = part.shape[0]
    block = (rows, part.shape[1] // experts)
    in_specs = [pl.BlockSpec(block, lambda e: (0, e))]
    operands = [part]
    if held is not None:
        in_specs.append(pl.BlockSpec(memory_space=pl.ANY))
        operands.append(held)
    return pl.pallas_call(
        place_first_kernel if held is None else place_kernel,
        grid=(experts,),
        in_specs=in_specs,
        out_specs=pl.BlockSpec((1, 1) + block, lambda e: (layer, e, 0, 0)),
        out_shape=jax.ShapeDtypeStruct((LAYER_COUNT, experts) + block, jnp.float32),
        input_output_aliases={} if held is None else {1: 0},
    )(*operands)


def body(
    inputs,
    routes,
    cotangent,
    query_weight,
    key_projection_weight,
    value_projection_weight,
    output_weight,
    attention_gain,
    expert_gain,
    router_weight,
    gate_weight,
    up_weight,
    down_weight,
):
    sequences_per_device, block_length, model_width = inputs.shape
    token_total = sequences_per_device * block_length
    exp_dev = gate_weight.shape[1]
    groups = lax.axis_size("expert")
    expert_total = exp_dev * groups
    all_rows = token_total * groups
    query_width = query_weight.shape[2]
    key_width = key_projection_weight.shape[2]
    my_group = lax.axis_index("expert")
    positions = my_group * block_length + jnp.arange(block_length, dtype=jnp.int32)
    cosine_table, sine_table = rotary_tables(positions, HEAD_SIZE // 2)
    block_at = my_group.astype(jnp.int32).reshape(1)
    expert_ids = jnp.arange(expert_total, dtype=jnp.int32)
    small_width = -(-(expert_total + 2) // 128) * 128
    gate_width = -(-(2 * expert_total) // 128) * 128
    edges = (
        query_width,
        query_width + key_width,
        query_width + 2 * key_width,
        query_width + 2 * key_width + model_width,
        query_width + 2 * key_width + model_width + expert_total,
        query_width + 2 * key_width + model_width + expert_total + 1,
    )

    def pack_attention(query_part, key_part, value_part, output_part, router_part, one, two):
        rows = query_part.shape[0]
        fill = jnp.zeros((rows, small_width - expert_total - 2), query_part.dtype)
        return jnp.concatenate(
            [
                query_part,
                key_part,
                value_part,
                output_part,
                router_part,
                one[:, None],
                two[:, None],
                fill,
            ],
            axis=1,
        )

    chosen_hot = jnp.any(
        routes.reshape(LAYER_COUNT, token_total, -1)[:, :, :, None] == expert_ids, axis=2
    )
    chosen_all = gather_rows(
        jnp.moveaxis(chosen_hot, 0, 1).reshape(token_total, -1).astype(jnp.bfloat16)
    ).reshape(all_rows, LAYER_COUNT, expert_total)

    shards = [
        pack_attention(
            query_weight[layer],
            key_projection_weight[layer],
            value_projection_weight[layer],
            output_weight[layer].T,
            router_weight[layer],
            attention_gain[layer],
            expert_gain[layer],
        )
        for layer in range(LAYER_COUNT)
    ]
    packed = [lax.all_gather(shards[0], ("dp", "expert"), axis=0, tiled=True)]
    ff_width = gate_weight.shape[3]
    hidden_width = exp_dev * ff_width
    gathered = [
        tuple(
            lax.all_gather(rows.reshape(-1, hidden_width), "dp", axis=0, tiled=True)
            for rows in (
                gate_weight[layer].transpose(1, 0, 2),
                up_weight[layer].transpose(1, 0, 2),
                down_weight[layer].transpose(2, 0, 1),
            )
        )
        for layer in range(LAYER_COUNT)
    ]

    def shares_of(rows, router_full, hot):
        logits = jnp.dot(rows, router_full, preferred_element_type=jnp.float32)
        masked = jnp.where(hot, logits, -1e30)
        exps = jnp.where(hot, jnp.exp(masked - jnp.max(masked, axis=1, keepdims=True)), 0.0)
        return exps / jnp.sum(exps, axis=1, keepdims=True)

    def expert_rows(act, down):
        return dot_f32(act, down, (1,), (1,)).astype(jnp.bfloat16)

    def layer_forward(hidden, layer):
        full = packed[layer]
        qkv_full = full[:, : edges[2]]
        output_full = full[:, edges[2] : edges[3]]
        router_full = full[:, edges[3] : edges[4]]
        gain_one = full[:, edges[4]].astype(jnp.float32)
        gain_two = full[:, edges[5]].astype(jnp.float32)
        gate_full, up_full, down_full = gathered[layer]
        first_normalized, inv_one = norm_forward(hidden, gain_one)
        first_normalized = first_normalized.astype(jnp.bfloat16)
        linear = jnp.dot(first_normalized, qkv_full, preferred_element_type=jnp.float32)
        query_rotated = rotate_features(
            linear[:, : edges[0]].reshape(token_total, QUERY_HEADS, HEAD_SIZE),
            cosine_table,
            sine_table,
        ).astype(jnp.bfloat16)
        query_rotated = query_rotated.reshape(token_total, query_width)
        key_rot = rotate_features(
            linear[:, edges[0] : edges[1]].reshape(token_total, KEY_VALUE_HEADS, HEAD_SIZE),
            cosine_table,
            sine_table,
        ).astype(jnp.bfloat16)
        key_value = jnp.concatenate(
            [
                key_rot.reshape(token_total, key_width),
                linear[:, edges[1] :].astype(jnp.bfloat16),
            ],
            axis=1,
        )
        key_value_all = gather_rows(key_value)
        ahead = layer + 1 < LAYER_COUNT
        if ahead:
            key_value_all, next_shard = lax.optimization_barrier(
                (key_value_all, shards[layer + 1])
            )
            next_rows = gather_chips(next_shard)
        attended = attention_forward(block_at, query_rotated, key_value_all)
        middle = hidden + dot_f32(attended, output_full, (1,), (1,))
        normed_two, inv_two = norm_forward(middle, gain_two)
        normed_two = normed_two.astype(jnp.bfloat16)
        arrived = gather_rows(normed_two)
        if ahead:
            arrived, next_rows = lax.optimization_barrier((arrived, next_rows))
            next_rows = gather_groups(next_rows)
        share_all = shares_of(arrived, router_full, chosen_all[:, layer] > 0)
        share_own = shares_of(normed_two, router_full, chosen_hot[layer])
        share_local = lax.dynamic_slice_in_dim(share_all, my_group * exp_dev, exp_dev, axis=1)
        gate_low, up_low, scaled_act = expert_forward(
            arrived, gate_full, up_full, share_local
        )
        if ahead:
            scaled_act, next_rows = lax.optimization_barrier((scaled_act, next_rows))
            packed.append(join_cores(next_rows))
        kept_state = (
            hidden,
            inv_one,
            first_normalized,
            query_rotated,
            key_value_all,
            attended,
            middle,
            inv_two,
            normed_two,
            share_own,
            share_local,
            arrived,
            gate_low,
            up_low,
            scaled_act,
            qkv_full,
            output_full,
            gain_one,
            gain_two,
            router_full,
            gate_full,
            up_full,
            down_full,
        )
        return kept_state

    hidden = inputs.astype(jnp.float32).reshape(token_total, model_width)
    kept_states = []
    for layer in range(LAYER_COUNT):
        kept_state = layer_forward(hidden, layer)
        kept_states.append(kept_state)
        last_middle, last_act, last_down = kept_state[6], kept_state[14], kept_state[-1]
        if layer + 1 < LAYER_COUNT:
            hidden = last_middle + sum_rows(expert_rows(last_act, last_down))
    output = None
    grad_hidden = cotangent.astype(jnp.float32).reshape(token_total, model_width)
    attention_list = [None] * LAYER_COUNT
    expert_held = [None] * 3
    waiting = None
    group_steps = halvings("expert", 1)
    chip_steps = halvings("dp", 2)
    for layer in range(LAYER_COUNT - 1, -1, -1):
        (
            layer_hidden,
            inv_one,
            first_normalized,
            query_rotated,
            key_value_all,
            attended,
            middle,
            inv_two,
            normed_two,
            share_own,
            share_local,
            arrived,
            gate_low,
            up_low,
            scaled_act,
            qkv_full,
            output_full,
            gain_one,
            gain_two,
            router_full,
            gate_full,
            up_full,
            down_full,
        ) = kept_states[layer]
        grad_all = gather_rows(grad_hidden.astype(jnp.bfloat16))
        if waiting is not None:
            last_act, waiting = lax.optimization_barrier((last_act, waiting))
            last_rows = expert_rows(last_act, last_down)
            grad_all, waiting, last_rows = lax.optimization_barrier(
                (grad_all, waiting, last_rows)
            )
            waiting = halve_all(waiting, group_steps[:1])
        grad_down = dot_f32(grad_all, scaled_act, (0,), (0,)).astype(jnp.bfloat16)
        grad_all, grad_down = lax.optimization_barrier((grad_all, grad_down))
        expert_parts = [lax.psum_scatter(grad_down, "dp", scatter_dimension=0, tiled=True)]
        grad_gate_val, grad_up_val, grad_rows, grad_sums = expert_backward(
            grad_all, down_full, gate_full, up_full, gate_low, up_low, share_local
        )
        grad_gates = grad_sums[:, :exp_dev]
        if waiting is not None:
            output = last_middle + sum_rows(last_rows)
            grad_rows, output = lax.optimization_barrier((grad_rows, output))
        grad_gate_w = dot_f32(arrived, grad_gate_val, (0,), (0,)).astype(jnp.bfloat16)
        grad_up_w = dot_f32(arrived, grad_up_val, (0,), (0,)).astype(jnp.bfloat16)
        gates_high = grad_gates.astype(jnp.bfloat16)
        gates_low = (grad_gates - gates_high.astype(jnp.float32)).astype(jnp.bfloat16)
        gate_columns = jnp.zeros((all_rows, gate_width), jnp.bfloat16)
        gate_columns = lax.dynamic_update_slice_in_dim(
            gate_columns, gates_high, my_group * exp_dev, axis=1
        )
        gate_columns = lax.dynamic_update_slice_in_dim(
            gate_columns, gates_low, expert_total + my_group * exp_dev, axis=1
        )
        back = sum_rows(
            jnp.concatenate([grad_rows, gate_columns], axis=1)
        )
        if waiting is not None:
            back, waiting, expert_held = lax.optimization_barrier(
                (back, waiting, expert_held)
            )
            waiting = halve_all(waiting, group_steps[1:])
        back, grad_gate_w, grad_up_w = lax.optimization_barrier((back, grad_gate_w, grad_up_w))
        expert_parts += [
            lax.psum_scatter(grad_gate_w, "dp", scatter_dimension=0, tiled=True),
            lax.psum_scatter(grad_up_w, "dp", scatter_dimension=0, tiled=True),
        ]
        grad_gates_own = (
            back[:, model_width : model_width + expert_total]
            + back[:, model_width + expert_total : model_width + 2 * expert_total]
        )
        grad_logits = (
            share_own
            * (grad_gates_own - jnp.sum(share_own * grad_gates_own, axis=-1, keepdims=True))
        ).astype(jnp.bfloat16)
        grad_router = dot_f32(normed_two, grad_logits, (0,), (0,))
        grad_normed_two = back[:, :model_width] + dot_f32(grad_logits, router_full, (1,), (1,))
        grad_norm_mid, grad_gain_two = norm_backward(middle, inv_two, gain_two, grad_normed_two)
        grad_middle = grad_hidden + grad_norm_mid
        grad_branch = grad_middle.astype(jnp.bfloat16)
        grad_output_w = dot_f32(core_major(grad_branch), both_cores(attended), (0,), (0,))
        grad_output_w = grad_output_w.astype(jnp.bfloat16)
        if layer == 0:
            grad_output_w = halve_all(grad_output_w, group_steps[:1])
        grad_attended = dot_f32(grad_branch, output_full, (1,), (0,)).astype(jnp.bfloat16)
        grad_query, grad_key_value_all = attention_backward(
            block_at, query_rotated, grad_attended, key_value_all
        )
        if waiting is not None:
            grad_query, waiting = lax.optimization_barrier((grad_query, waiting))
            attention_list[layer + 1] = halve_all(waiting, chip_steps)
        if layer == 0:
            grad_query, grad_output_w = lax.optimization_barrier((grad_query, grad_output_w))
            grad_output_w = halve_all(grad_output_w, group_steps[1:])
        grad_kv = sum_rows(grad_key_value_all).reshape(token_total, -1, 2, 2 * HEAD_SIZE)
        grad_kv = grad_kv.transpose(0, 2, 1, 3).reshape(token_total, 2 * key_width)
        grad_query_lin = (
            rotate_features(
                grad_query.reshape(token_total, QUERY_HEADS, HEAD_SIZE), cosine_table, -sine_table
            )
            .astype(jnp.bfloat16)
            .reshape(token_total, query_width)
        )
        grad_key_lin = (
            rotate_features(
                grad_kv[:, :key_width].reshape(token_total, KEY_VALUE_HEADS, HEAD_SIZE),
                cosine_table,
                -sine_table,
            )
            .astype(jnp.bfloat16)
            .reshape(token_total, key_width)
        )
        grad_kv_lin = jnp.concatenate(
            [grad_key_lin, grad_kv[:, key_width:].astype(jnp.bfloat16)], axis=1
        )
        normed_split = core_major(first_normalized)
        grad_query_w = dot_f32(normed_split, both_cores(grad_query_lin), (0,), (0,))
        grad_kv_w = dot_f32(normed_split, both_cores(grad_kv_lin), (0,), (0,))
        grad_normed_one = dot_f32(grad_query_lin, qkv_full[:, : edges[0]], (1,), (1,)) + dot_f32(
            grad_kv_lin, qkv_full[:, edges[0] :], (1,), (1,)
        )
        grad_norm_in, grad_gain_one = norm_backward(
            layer_hidden, inv_one, gain_one, grad_normed_one
        )
        fill = jnp.zeros((model_width, small_width - expert_total - 2), jnp.bfloat16)
        small_part = jnp.concatenate(
            [
                grad_router.astype(jnp.bfloat16),
                grad_gain_one[:, None].astype(jnp.bfloat16),
                grad_gain_two[:, None].astype(jnp.bfloat16),
                fill,
            ],
            axis=1,
        )
        small_split = core_major(small_part.T).reshape(2, small_width, -1)
        small_half = jnp.sum(small_split.astype(jnp.float32), axis=0).T
        grad_kv_w = jnp.concatenate([grad_kv_w, small_half], axis=1).astype(jnp.bfloat16)
        grad_query_w = grad_query_w.astype(jnp.bfloat16)
        if layer > 0:
            waiting = jnp.concatenate([grad_output_w, grad_query_w, grad_kv_w], axis=1)
        else:
            attention_list[layer] = jnp.concatenate(
                [
                    halve_all(grad_output_w, chip_steps),
                    halve_all(grad_query_w, group_steps + chip_steps),
                    halve_all(grad_kv_w, group_steps + chip_steps),
                ],
                axis=1,
            )
        expert_held = [
            place(part, held, layer, exp_dev) for part, held in zip(expert_parts, expert_held)
        ]
        grad_hidden = grad_middle + grad_norm_in
    stacked = jnp.stack(attention_list).astype(jnp.float32)
    cuts = [query_width, query_width, key_width, key_width, expert_total, 1, 1]
    cuts = [sum(cuts[:index]) for index in range(len(cuts) + 1)]
    output_grads, query_grads, key_grads, value_grads, router_grads, one, two = (
        stacked[:, :, start:stop] for start, stop in zip(cuts[:-1], cuts[1:])
    )
    down_grads, gate_grads, up_grads = expert_held
    return (
        output.astype(jnp.bfloat16).reshape(sequences_per_device, block_length, model_width),
        grad_hidden.reshape(sequences_per_device, block_length, model_width),
        query_grads,
        key_grads,
        value_grads,
        jnp.swapaxes(output_grads, 1, 2),
        one[:, :, 0],
        two[:, :, 0],
        router_grads,
        gate_grads,
        up_grads,
        jnp.swapaxes(down_grads, 2, 3),
    )


def solution(mesh):
    in_specs = (
        P("dp", "expert", None),
        P(None, "expert", "dp", None, None),
        P("dp", "expert", None),
        P(None, ("dp", "expert"), None),
        P(None, ("dp", "expert"), None),
        P(None, ("dp", "expert"), None),
        P(None, None, ("dp", "expert")),
        P(None, ("dp", "expert")),
        P(None, ("dp", "expert")),
        P(None, ("dp", "expert"), None),
        P(None, "expert", "dp", None),
        P(None, "expert", "dp", None),
        P(None, "expert", None, "dp"),
    )
    out_specs = (
        P("dp", "expert", None),
        P("dp", "expert", None),
        P(None, ("dp", "expert"), None),
        P(None, ("dp", "expert"), None),
        P(None, ("dp", "expert"), None),
        P(None, None, ("dp", "expert")),
        P(None, ("dp", "expert")),
        P(None, ("dp", "expert")),
        P(None, ("dp", "expert"), None),
        P(None, "expert", "dp", None),
        P(None, "expert", "dp", None),
        P(None, "expert", None, "dp"),
    )
    return jax.shard_map(body, mesh=mesh, in_specs=in_specs, out_specs=out_specs, check_vma=False)
```

```python
import math

import jax
import jax.numpy as jnp
from jax import lax
from jax.experimental import pallas as pl
from jax.experimental.pallas import tpu as pltpu
from jax.sharding import PartitionSpec as P

QUERY_HEADS = 24
KEY_VALUE_HEADS = 8
HEAD_SIZE = 64
LAYER_COUNT = 2


eps_norm = 1e-06
highest_precision = lax.Precision.HIGHEST


def rotary_tables(positions, half_dim):
    frequency = jnp.exp(-math.log(10000.0) * jnp.arange(half_dim, dtype=jnp.float32) / half_dim)
    angles = positions.astype(jnp.float32)[:, None] * frequency[None, :]
    return (jnp.cos(angles), jnp.sin(angles))


def rotate_features(values, cosine_table, sine_table):
    half_dim = values.shape[-1] // 2
    first_half = values[..., :half_dim]
    second_half = values[..., half_dim:]
    cos_part = cosine_table[:, None, :]
    sin_part = sine_table[:, None, :]
    return jnp.concatenate(
        [
            first_half * cos_part - second_half * sin_part,
            second_half * cos_part + first_half * sin_part,
        ],
        axis=-1,
    )


def norm_forward(values, gain_vec):
    inv_rms = lax.rsqrt(jnp.mean(values * values, axis=-1, keepdims=True) + eps_norm)
    return (values * inv_rms * gain_vec, inv_rms)


def norm_backward(values, inv_rms, gain_vec, upstream):
    scaled = upstream * gain_vec
    grad_gain = jnp.sum(upstream * values * inv_rms, axis=0)
    grad_values = inv_rms * (
        scaled - values * inv_rms * inv_rms * jnp.mean(scaled * values, axis=-1, keepdims=True)
    )
    return (grad_values, grad_gain)


def stack_member(layer_list, member):
    return jnp.stack([layer_parts[member] for layer_parts in layer_list], axis=0)


def exchange(blocks):
    return lax.all_to_all(blocks, "expert", split_axis=0, concat_axis=0, tiled=True)


def gather_rows(rows):
    groups = lax.axis_size("expert")
    blocks = exchange(jnp.broadcast_to(rows[None], (groups,) + rows.shape))
    return blocks.reshape((groups * rows.shape[0],) + rows.shape[1:])


def sum_rows(partial_rows):
    groups = lax.axis_size("expert")
    blocks = partial_rows.reshape((groups, -1) + partial_rows.shape[1:])
    return jnp.sum(exchange(blocks).astype(jnp.float32), axis=0)


def same_core():
    members = range(lax.axis_size("dp"))
    return [[i for i in members if i % 2 == core] for core in range(2)]


def swap_cores(values):
    return lax.ppermute(values, "dp", [(i, i ^ 1) for i in range(lax.axis_size("dp"))])


def exchange_chips(blocks):
    return lax.all_to_all(
        blocks, "dp", split_axis=0, concat_axis=0, axis_index_groups=same_core(), tiled=True
    )


def gather_chips(shard):
    chips = lax.axis_size("dp") // 2
    return exchange_chips(jnp.broadcast_to(shard[None], (chips,) + shard.shape))


def gather_groups(chip_rows):
    groups = lax.axis_size("expert")
    return exchange(jnp.broadcast_to(chip_rows[None], (groups,) + chip_rows.shape))


def join_cores(own):
    width = own.shape[-1]
    other = swap_cores(own)
    first = lax.axis_index("dp") % 2 == 0
    both = jnp.stack([jnp.where(first, own, other), jnp.where(first, other, own)])
    return both.transpose(2, 0, 1, 3, 4).reshape(-1, width)


def core_major(columns):
    chips = lax.axis_size("dp") // 2
    groups = lax.axis_size("expert")
    split = columns.reshape(columns.shape[0], chips, 2, groups, -1)
    halves = split.transpose(2, 0, 3, 1, 4).reshape(2, columns.shape[0], -1)
    core = lax.axis_index("dp") % 2
    mine = lax.dynamic_index_in_dim(halves, core, 0, keepdims=False)
    theirs = lax.dynamic_index_in_dim(halves, 1 - core, 0, keepdims=False)
    return jnp.concatenate([mine, swap_cores(theirs)], axis=0)


def both_cores(rows):
    return jnp.concatenate([rows, swap_cores(rows)], axis=0)


def halve(partial, axis_name, step):
    size = lax.axis_size(axis_name)
    width = partial.shape[-1]
    blocks = partial.reshape(size // (2 * step), 2, -1, width)
    side = (lax.axis_index(axis_name) // step) % 2
    mine = lax.dynamic_index_in_dim(blocks, side, 1, keepdims=False)
    theirs = lax.dynamic_index_in_dim(blocks, 1 - side, 1, keepdims=False)
    arrived = lax.ppermute(
        theirs.reshape(-1, width), axis_name, [(i, i ^ step) for i in range(size)]
    )
    total = mine.reshape(-1, width).astype(jnp.float32) + arrived.astype(jnp.float32)
    return total.astype(jnp.bfloat16)


def halvings(axis_name, least):
    steps = [least]
    while 2 * steps[-1] < lax.axis_size(axis_name):
        steps.append(2 * steps[-1])
    return [(axis_name, step) for step in steps]


def halve_all(partial, steps):
    for axis_name, step in steps:
        partial = halve(partial, axis_name, step)
    return partial


def dot_f32(left, right, left_dims, right_dims):
    return lax.dot_general(
        left, right, ((left_dims, right_dims), ((), ())), preferred_element_type=jnp.float32
    )


def contract(left, right, left_dim, right_dim):
    return lax.dot_general(
        left,
        right,
        (((left_dim,), (right_dim,)), ((), ())),
        preferred_element_type=jnp.float32,
    )


def pick_column(table, column):
    lanes = lax.broadcasted_iota(jnp.int32, table.shape, 1)
    return jnp.sum(jnp.where(lanes == column, table, 0.0), axis=1, keepdims=True)


def expert_forward_kernel(rows_ref, gate_ref, up_ref, share_ref, gate_out, up_out, act_out):
    rows = rows_ref[...]
    gate_val = contract(rows, gate_ref[...], 1, 0)
    up_val = contract(rows, up_ref[...], 1, 0)
    share = pick_column(share_ref[...], pl.program_id(0))
    gate_out[...] = gate_val.astype(jnp.bfloat16)
    up_out[...] = up_val.astype(jnp.bfloat16)
    act_out[...] = (gate_val * jax.nn.sigmoid(gate_val) * up_val * share).astype(jnp.bfloat16)


def expert_forward(rows, gate, up, share):
    row_total, width = rows.shape
    experts = share.shape[1]
    hidden = gate.shape[1] // experts
    tile = row_total // 2
    row_block = pl.BlockSpec((tile, width), lambda e, r: (r, 0))
    weight_block = pl.BlockSpec((width, hidden), lambda e, r: (0, e))
    hidden_block = pl.BlockSpec((tile, hidden), lambda e, r: (r, e))
    return pl.pallas_call(
        expert_forward_kernel,
        grid=(experts, 2),
        in_specs=[
            row_block,
            weight_block,
            weight_block,
            pl.BlockSpec((tile, experts), lambda e, r: (r, 0)),
        ],
        out_specs=[hidden_block] * 3,
        out_shape=[jax.ShapeDtypeStruct((row_total, gate.shape[1]), jnp.bfloat16)] * 3,
        cost_estimate=pl.CostEstimate(
            flops=4 * row_total * width * gate.shape[1],
            transcendentals=row_total * gate.shape[1],
            bytes_accessed=4 * width * gate.shape[1] + 6 * row_total * gate.shape[1],
        ),
    )(rows, gate, up, share)


def expert_backward_kernel(
    group_ref,
    grad_ref,
    down_ref,
    gate_ref,
    up_ref,
    gate_val_ref,
    up_val_ref,
    share_ref,
    grad_gate_out,
    grad_up_out,
    rows_out,
    rows_acc,
    sums_acc,
):
    expert = pl.program_id(0)
    tile, width = grad_ref.shape
    experts = pl.num_programs(0)
    window = pl.ds(pl.multiple_of(pl.program_id(1) * tile, tile), tile)
    grad_scaled = contract(grad_ref[...], down_ref[...], 1, 0)
    gate_val = gate_val_ref[...].astype(jnp.float32)
    up_val = up_val_ref[...].astype(jnp.float32)
    sigmoid_val = jax.nn.sigmoid(gate_val)
    silu_val = gate_val * sigmoid_val
    grad_sum = jnp.sum(grad_scaled * silu_val * up_val, axis=1, keepdims=True)
    grad_inner = grad_scaled * pick_column(share_ref[...], expert)
    grad_gate = (
        grad_inner * up_val * sigmoid_val * (1.0 + gate_val * (1.0 - sigmoid_val))
    ).astype(jnp.bfloat16)
    grad_up = (grad_inner * silu_val).astype(jnp.bfloat16)
    grad_gate_out[...] = grad_gate
    grad_up_out[...] = grad_up
    grad_rows = contract(grad_gate, gate_ref[...], 1, 1) + contract(
        grad_up, up_ref[...], 1, 1
    )
    lanes = lax.broadcasted_iota(jnp.int32, (tile, sums_acc.shape[1]), 1)
    sum_high = grad_sum.astype(jnp.bfloat16).astype(jnp.float32)
    column = group_ref[0] * experts + expert
    grad_sums = jnp.where(lanes == column, sum_high, 0.0) + jnp.where(
        lanes == column + group_ref[1], grad_sum - sum_high, 0.0
    )

    @pl.when(expert == 0)
    def _():
        rows_acc[window, :] = grad_rows
        sums_acc[window, :] = grad_sums

    @pl.when(expert > 0)
    def _():
        rows_acc[window, :] += grad_rows
        sums_acc[window, :] += grad_sums

    @pl.when(expert == pl.num_programs(0) - 1)
    def _():
        rows_out[:, :width] = rows_acc[window, :].astype(jnp.bfloat16)
        rows_out[:, width:] = sums_acc[window, :].astype(jnp.bfloat16)


def expert_backward(group, grad, down, gate, up, gate_val, up_val, share, extra):
    row_total, width = grad.shape
    experts = share.shape[1]
    hidden = gate.shape[1] // experts
    tile = row_total // 2
    row_block = pl.BlockSpec((tile, width), lambda e, r, g: (r, 0))
    weight_block = pl.BlockSpec((width, hidden), lambda e, r, g: (0, e))
    hidden_block = pl.BlockSpec((tile, hidden), lambda e, r, g: (r, e))
    hidden_shape = jax.ShapeDtypeStruct((row_total, gate.shape[1]), jnp.bfloat16)
    return pl.pallas_call(
        expert_backward_kernel,
        grid_spec=pltpu.PrefetchScalarGridSpec(
            num_scalar_prefetch=1,
            grid=(experts, 2),
            in_specs=[
                row_block,
                weight_block,
                weight_block,
                weight_block,
                hidden_block,
                hidden_block,
                pl.BlockSpec((tile, experts), lambda e, r, g: (r, 0)),
            ],
            out_specs=[
                hidden_block,
                hidden_block,
                pl.BlockSpec(
                    (tile, width + extra),
                    lambda e, r, g: (jnp.where(e == experts - 1, r, 0), 0),
                ),
            ],
            scratch_shapes=[
                pltpu.VMEM((row_total, width), jnp.float32),
                pltpu.VMEM((row_total, extra), jnp.float32),
            ],
        ),
        out_shape=[
            hidden_shape,
            hidden_shape,
            jax.ShapeDtypeStruct((row_total, width + extra), jnp.bfloat16),
        ],
        cost_estimate=pl.CostEstimate(
            flops=6 * row_total * width * gate.shape[1],
            transcendentals=row_total * gate.shape[1],
            bytes_accessed=6 * width * gate.shape[1] + 8 * row_total * gate.shape[1],
        ),
    )(group, grad, down, gate, up, gate_val, up_val, share)


def attention_probs(block_ref, query, key):
    scores = contract(key, query, 1, 1) * HEAD_SIZE ** (-0.5)
    key_at = lax.broadcasted_iota(jnp.int32, scores.shape, 0)
    query_at = lax.broadcasted_iota(jnp.int32, scores.shape, 1)
    offset = block_ref[0] * query.shape[0]
    masked = jnp.where(key_at <= query_at + offset, scores, -1e30)
    exp_scores = jnp.exp(masked - jnp.max(masked, axis=0, keepdims=True))
    return exp_scores / jnp.sum(exp_scores, axis=0, keepdims=True)


def head(values, index):
    return values[:, index * HEAD_SIZE : (index + 1) * HEAD_SIZE]


def attention_forward_kernel(block_ref, query_ref, key_ref, value_ref, out_ref):
    query, key, value = query_ref[...], key_ref[...], value_ref[...]
    group = QUERY_HEADS // KEY_VALUE_HEADS
    outs = []
    for index in range(2 * group):
        shared = index // group
        probs = attention_probs(block_ref, head(query, index), head(key, shared))
        outs.append(contract(head(value, shared), probs.astype(jnp.bfloat16), 0, 0))
    out_ref[...] = jnp.concatenate(outs, axis=0).T.astype(jnp.bfloat16)


def attention_specs(tokens, keys):
    pairs = KEY_VALUE_HEADS // 2
    query_block = pl.BlockSpec((tokens, QUERY_HEADS // pairs * HEAD_SIZE), lambda i, b: (0, i))
    key_block = pl.BlockSpec((keys, 2 * HEAD_SIZE), lambda i, b: (0, i))
    value_block = pl.BlockSpec((keys, 2 * HEAD_SIZE), lambda i, b: (0, i + pairs))
    return (pairs, query_block, key_block, value_block)


def attention_forward(block, query, key_value):
    tokens, width = query.shape
    keys = key_value.shape[0]
    pairs, query_block, key_block, value_block = attention_specs(tokens, keys)
    return pl.pallas_call(
        attention_forward_kernel,
        grid_spec=pltpu.PrefetchScalarGridSpec(
            num_scalar_prefetch=1,
            grid=(pairs,),
            in_specs=[query_block, key_block, value_block],
            out_specs=query_block,
        ),
        out_shape=jax.ShapeDtypeStruct((tokens, width), jnp.bfloat16),
        cost_estimate=pl.CostEstimate(
            flops=16 * tokens * width * keys,
            transcendentals=QUERY_HEADS * tokens * keys,
            bytes_accessed=4 * tokens * width + 2 * key_value.size,
        ),
    )(block, query, key_value, key_value)


def attention_backward_kernel(
    block_ref, query_ref, grad_ref, key_ref, value_ref, grad_query_out, grad_key_value_out
):
    query, grad, key, value = query_ref[...], grad_ref[...], key_ref[...], value_ref[...]
    group = QUERY_HEADS // KEY_VALUE_HEADS
    scale = HEAD_SIZE ** (-0.5)
    grad_queries, grad_keys, grad_values = [], [], []
    for shared in range(2):
        grad_key, grad_value = 0.0, 0.0
        for index in range(shared * group, (shared + 1) * group):
            query_one, grad_one = head(query, index), head(grad, index)
            probs = attention_probs(block_ref, query_one, head(key, shared))
            grad_probs = contract(head(value, shared), grad_one, 1, 1)
            centre = jnp.sum(probs * grad_probs, axis=0, keepdims=True)
            grad_scores = (probs * (grad_probs - centre)).astype(jnp.bfloat16)
            grad_queries.append(contract(head(key, shared), grad_scores, 0, 0) * scale)
            grad_key += contract(grad_scores, query_one, 1, 0)
            grad_value += contract(probs.astype(jnp.bfloat16), grad_one, 1, 0)
        grad_keys.append(grad_key * scale)
        grad_values.append(grad_value)
    grad_query_out[...] = jnp.concatenate(grad_queries, axis=0).T
    grad_key_value_out[...] = jnp.concatenate(grad_keys + grad_values, axis=1).astype(
        jnp.bfloat16
    )


def attention_backward(block, query, grad, key_value):
    tokens, width = query.shape
    keys = key_value.shape[0]
    pairs, query_block, key_block, value_block = attention_specs(tokens, keys)
    return pl.pallas_call(
        attention_backward_kernel,
        grid_spec=pltpu.PrefetchScalarGridSpec(
            num_scalar_prefetch=1,
            grid=(pairs,),
            in_specs=[query_block, query_block, key_block, value_block],
            out_specs=[
                query_block,
                pl.BlockSpec((keys, 4 * HEAD_SIZE), lambda i, b: (0, i)),
            ],
        ),
        out_shape=[
            jax.ShapeDtypeStruct((tokens, width), jnp.float32),
            jax.ShapeDtypeStruct(key_value.shape, jnp.bfloat16),
        ],
        cost_estimate=pl.CostEstimate(
            flops=40 * tokens * width * keys,
            transcendentals=QUERY_HEADS * tokens * keys,
            bytes_accessed=8 * tokens * width + 4 * key_value.size,
        ),
    )(block, query, grad, key_value, key_value)


def place_kernel(part_ref, held_ref, out_ref):
    del held_ref
    out_ref[0, 0] = part_ref[...].astype(jnp.float32)


def place_first_kernel(part_ref, out_ref):
    out_ref[0, 0] = part_ref[...].astype(jnp.float32)


def place(part, held, layer, experts):
    rows = part.shape[0]
    block = (rows, part.shape[1] // experts)
    in_specs = [pl.BlockSpec(block, lambda e: (0, e))]
    operands = [part]
    if held is not None:
        in_specs.append(pl.BlockSpec(memory_space=pl.ANY))
        operands.append(held)
    return pl.pallas_call(
        place_first_kernel if held is None else place_kernel,
        grid=(experts,),
        in_specs=in_specs,
        out_specs=pl.BlockSpec((1, 1) + block, lambda e: (layer, e, 0, 0)),
        out_shape=jax.ShapeDtypeStruct((LAYER_COUNT, experts) + block, jnp.float32),
        input_output_aliases={} if held is None else {1: 0},
    )(*operands)


def body(
    inputs,
    routes,
    cotangent,
    query_weight,
    key_projection_weight,
    value_projection_weight,
    output_weight,
    attention_gain,
    expert_gain,
    router_weight,
    gate_weight,
    up_weight,
    down_weight,
):
    sequences_per_device, block_length, model_width = inputs.shape
    token_total = sequences_per_device * block_length
    exp_dev = gate_weight.shape[1]
    groups = lax.axis_size("expert")
    expert_total = exp_dev * groups
    all_rows = token_total * groups
    query_width = query_weight.shape[2]
    key_width = key_projection_weight.shape[2]
    my_group = lax.axis_index("expert")
    positions = my_group * block_length + jnp.arange(block_length, dtype=jnp.int32)
    cosine_table, sine_table = rotary_tables(positions, HEAD_SIZE // 2)
    block_at = my_group.astype(jnp.int32).reshape(1)
    group_at = jnp.stack([my_group.astype(jnp.int32), jnp.int32(expert_total)])
    expert_ids = jnp.arange(expert_total, dtype=jnp.int32)
    small_width = -(-(expert_total + 2) // 128) * 128
    gate_width = -(-(2 * expert_total) // 128) * 128
    edges = (
        query_width,
        query_width + key_width,
        query_width + 2 * key_width,
        query_width + 2 * key_width + model_width,
        query_width + 2 * key_width + model_width + expert_total,
        query_width + 2 * key_width + model_width + expert_total + 1,
    )

    def pack_attention(query_part, key_part, value_part, output_part, router_part, one, two):
        rows = query_part.shape[0]
        fill = jnp.zeros((rows, small_width - expert_total - 2), query_part.dtype)
        return jnp.concatenate(
            [
                query_part,
                key_part,
                value_part,
                output_part,
                router_part,
                one[:, None],
                two[:, None],
                fill,
            ],
            axis=1,
        )

    chosen_hot = jnp.any(
        routes.reshape(LAYER_COUNT, token_total, -1)[:, :, :, None] == expert_ids, axis=2
    )
    chosen_all = gather_rows(
        jnp.moveaxis(chosen_hot, 0, 1).reshape(token_total, -1).astype(jnp.bfloat16)
    ).reshape(all_rows, LAYER_COUNT, expert_total)

    shards = [
        pack_attention(
            query_weight[layer],
            key_projection_weight[layer],
            value_projection_weight[layer],
            output_weight[layer].T,
            router_weight[layer],
            attention_gain[layer],
            expert_gain[layer],
        )
        for layer in range(LAYER_COUNT)
    ]
    packed = [lax.all_gather(shards[0], ("dp", "expert"), axis=0, tiled=True)]
    ff_width = gate_weight.shape[3]
    hidden_width = exp_dev * ff_width
    gathered = [
        tuple(
            lax.all_gather(rows.reshape(-1, hidden_width), "dp", axis=0, tiled=True)
            for rows in (
                gate_weight[layer].transpose(1, 0, 2),
                up_weight[layer].transpose(1, 0, 2),
                down_weight[layer].transpose(2, 0, 1),
            )
        )
        for layer in range(LAYER_COUNT)
    ]

    def shares_of(rows, router_full, hot):
        logits = jnp.dot(rows, router_full, preferred_element_type=jnp.float32)
        masked = jnp.where(hot, logits, -1e30)
        exps = jnp.where(hot, jnp.exp(masked - jnp.max(masked, axis=1, keepdims=True)), 0.0)
        return exps / jnp.sum(exps, axis=1, keepdims=True)

    def expert_rows(act, down):
        return dot_f32(act, down, (1,), (1,)).astype(jnp.bfloat16)

    def layer_forward(hidden, layer):
        full = packed[layer]
        qkv_full = full[:, : edges[2]]
        output_full = full[:, edges[2] : edges[3]]
        router_full = full[:, edges[3] : edges[4]]
        gain_one = full[:, edges[4]].astype(jnp.float32)
        gain_two = full[:, edges[5]].astype(jnp.float32)
        gate_full, up_full, down_full = gathered[layer]
        first_normalized, inv_one = norm_forward(hidden, gain_one)
        first_normalized = first_normalized.astype(jnp.bfloat16)
        linear = jnp.dot(first_normalized, qkv_full, preferred_element_type=jnp.float32)
        query_rotated = rotate_features(
            linear[:, : edges[0]].reshape(token_total, QUERY_HEADS, HEAD_SIZE),
            cosine_table,
            sine_table,
        ).astype(jnp.bfloat16)
        query_rotated = query_rotated.reshape(token_total, query_width)
        key_rot = rotate_features(
            linear[:, edges[0] : edges[1]].reshape(token_total, KEY_VALUE_HEADS, HEAD_SIZE),
            cosine_table,
            sine_table,
        ).astype(jnp.bfloat16)
        key_value = jnp.concatenate(
            [
                key_rot.reshape(token_total, key_width),
                linear[:, edges[1] :].astype(jnp.bfloat16),
            ],
            axis=1,
        )
        key_value_all = gather_rows(key_value)
        ahead = layer + 1 < LAYER_COUNT
        if ahead:
            key_value_all, next_shard = lax.optimization_barrier(
                (key_value_all, shards[layer + 1])
            )
            next_rows = gather_chips(next_shard)
        attended = attention_forward(block_at, query_rotated, key_value_all)
        middle = hidden + dot_f32(attended, output_full, (1,), (1,))
        normed_two, inv_two = norm_forward(middle, gain_two)
        normed_two = normed_two.astype(jnp.bfloat16)
        arrived = gather_rows(normed_two)
        if ahead:
            arrived, next_rows = lax.optimization_barrier((arrived, next_rows))
            next_rows = gather_groups(next_rows)
        share_all = shares_of(arrived, router_full, chosen_all[:, layer] > 0)
        share_own = shares_of(normed_two, router_full, chosen_hot[layer])
        share_local = lax.dynamic_slice_in_dim(share_all, my_group * exp_dev, exp_dev, axis=1)
        gate_low, up_low, scaled_act = expert_forward(
            arrived, gate_full, up_full, share_local
        )
        if ahead:
            scaled_act, next_rows = lax.optimization_barrier((scaled_act, next_rows))
            packed.append(join_cores(next_rows))
        kept_state = (
            hidden,
            inv_one,
            first_normalized,
            query_rotated,
            key_value_all,
            attended,
            middle,
            inv_two,
            normed_two,
            share_own,
            share_local,
            arrived,
            gate_low,
            up_low,
            scaled_act,
            qkv_full,
            output_full,
            gain_one,
            gain_two,
            router_full,
            gate_full,
            up_full,
            down_full,
        )
        return kept_state

    hidden = inputs.astype(jnp.float32).reshape(token_total, model_width)
    kept_states = []
    for layer in range(LAYER_COUNT):
        kept_state = layer_forward(hidden, layer)
        kept_states.append(kept_state)
        last_middle, last_act, last_down = kept_state[6], kept_state[14], kept_state[-1]
        if layer + 1 < LAYER_COUNT:
            hidden = last_middle + sum_rows(expert_rows(last_act, last_down))
    output = None
    grad_hidden = cotangent.astype(jnp.float32).reshape(token_total, model_width)
    attention_list = [None] * LAYER_COUNT
    expert_held = [None] * 3
    waiting = None
    group_steps = halvings("expert", 1)
    chip_steps = halvings("dp", 2)
    for layer in range(LAYER_COUNT - 1, -1, -1):
        (
            layer_hidden,
            inv_one,
            first_normalized,
            query_rotated,
            key_value_all,
            attended,
            middle,
            inv_two,
            normed_two,
            share_own,
            share_local,
            arrived,
            gate_low,
            up_low,
            scaled_act,
            qkv_full,
            output_full,
            gain_one,
            gain_two,
            router_full,
            gate_full,
            up_full,
            down_full,
        ) = kept_states[layer]
        grad_all = gather_rows(grad_hidden.astype(jnp.bfloat16))
        if waiting is not None:
            out_part, query_part, kv_part = waiting
            last_act, query_part, kv_part = lax.optimization_barrier(
                (last_act, query_part, kv_part)
            )
            last_rows = expert_rows(last_act, last_down)
            grad_all, out_part, query_part, kv_part, last_rows = lax.optimization_barrier(
                (grad_all, out_part, query_part, kv_part, last_rows)
            )
            query_part = halve_all(query_part, group_steps[1:])
            kv_part = halve_all(kv_part, group_steps[:1])
        grad_down = dot_f32(grad_all, scaled_act, (0,), (0,)).astype(jnp.bfloat16)
        grad_all, grad_down = lax.optimization_barrier((grad_all, grad_down))
        expert_parts = [lax.psum_scatter(grad_down, "dp", scatter_dimension=0, tiled=True)]
        grad_gate_val, grad_up_val, grad_rows = expert_backward(
            group_at,
            grad_all,
            down_full,
            gate_full,
            up_full,
            gate_low,
            up_low,
            share_local,
            gate_width,
        )
        if waiting is not None:
            grad_rows, query_part, kv_part = lax.optimization_barrier(
                (grad_rows, query_part, kv_part)
            )
            kv_part = halve_all(kv_part, group_steps[1:])
        grad_gate_w = dot_f32(arrived, grad_gate_val, (0,), (0,)).astype(jnp.bfloat16)
        grad_up_w = dot_f32(arrived, grad_up_val, (0,), (0,)).astype(jnp.bfloat16)
        back = sum_rows(grad_rows)
        if waiting is not None:
            back, kv_part, last_rows = lax.optimization_barrier((back, kv_part, last_rows))
            output = last_middle + sum_rows(last_rows)
            chip_part = jnp.concatenate([out_part, query_part, kv_part], axis=1)
            chip_part = halve_all(chip_part, chip_steps[:1])
        back, grad_gate_w, grad_up_w = lax.optimization_barrier((back, grad_gate_w, grad_up_w))
        expert_parts += [
            lax.psum_scatter(grad_gate_w, "dp", scatter_dimension=0, tiled=True),
            lax.psum_scatter(grad_up_w, "dp", scatter_dimension=0, tiled=True),
        ]
        grad_gates_own = (
            back[:, model_width : model_width + expert_total]
            + back[:, model_width + expert_total : model_width + 2 * expert_total]
        )
        grad_logits = (
            share_own
            * (grad_gates_own - jnp.sum(share_own * grad_gates_own, axis=-1, keepdims=True))
        ).astype(jnp.bfloat16)
        grad_router = dot_f32(normed_two, grad_logits, (0,), (0,))
        grad_normed_two = back[:, :model_width] + dot_f32(grad_logits, router_full, (1,), (1,))
        grad_norm_mid, grad_gain_two = norm_backward(middle, inv_two, gain_two, grad_normed_two)
        grad_middle = grad_hidden + grad_norm_mid
        grad_branch = grad_middle.astype(jnp.bfloat16)
        grad_output_w = dot_f32(core_major(grad_branch), both_cores(attended), (0,), (0,))
        grad_output_w = halve_all(grad_output_w.astype(jnp.bfloat16), group_steps[:1])
        grad_attended = dot_f32(grad_branch, output_full, (1,), (0,)).astype(jnp.bfloat16)
        grad_query, grad_key_value_all = attention_backward(
            block_at, query_rotated, grad_attended, key_value_all
        )
        grad_query, grad_output_w = lax.optimization_barrier((grad_query, grad_output_w))
        grad_output_w = halve_all(grad_output_w, group_steps[1:])
        if waiting is not None:
            grad_query, output, chip_part = lax.optimization_barrier(
                (grad_query, output, chip_part)
            )
            chip_part = halve_all(chip_part, chip_steps[1:])
        grad_kv = sum_rows(grad_key_value_all)
        if waiting is not None:
            grad_kv, expert_held, chip_part = lax.optimization_barrier(
                (grad_kv, expert_held, chip_part)
            )
            attention_list[layer + 1] = chip_part
        grad_kv = grad_kv.reshape(token_total, -1, 2, 2 * HEAD_SIZE)
        grad_kv = grad_kv.transpose(0, 2, 1, 3).reshape(token_total, 2 * key_width)
        grad_query_lin = (
            rotate_features(
                grad_query.reshape(token_total, QUERY_HEADS, HEAD_SIZE), cosine_table, -sine_table
            )
            .astype(jnp.bfloat16)
            .reshape(token_total, query_width)
        )
        grad_key_lin = (
            rotate_features(
                grad_kv[:, :key_width].reshape(token_total, KEY_VALUE_HEADS, HEAD_SIZE),
                cosine_table,
                -sine_table,
            )
            .astype(jnp.bfloat16)
            .reshape(token_total, key_width)
        )
        grad_kv_lin = jnp.concatenate(
            [grad_key_lin, grad_kv[:, key_width:].astype(jnp.bfloat16)], axis=1
        )
        normed_split = core_major(first_normalized)
        grad_query_w = dot_f32(normed_split, both_cores(grad_query_lin), (0,), (0,))
        grad_kv_w = dot_f32(normed_split, both_cores(grad_kv_lin), (0,), (0,))
        grad_normed_one = dot_f32(grad_query_lin, qkv_full[:, : edges[0]], (1,), (1,)) + dot_f32(
            grad_kv_lin, qkv_full[:, edges[0] :], (1,), (1,)
        )
        grad_norm_in, grad_gain_one = norm_backward(
            layer_hidden, inv_one, gain_one, grad_normed_one
        )
        fill = jnp.zeros((model_width, small_width - expert_total - 2), jnp.bfloat16)
        small_part = jnp.concatenate(
            [
                grad_router.astype(jnp.bfloat16),
                grad_gain_one[:, None].astype(jnp.bfloat16),
                grad_gain_two[:, None].astype(jnp.bfloat16),
                fill,
            ],
            axis=1,
        )
        small_split = core_major(small_part.T).reshape(2, small_width, -1)
        small_half = jnp.sum(small_split.astype(jnp.float32), axis=0).T
        grad_kv_w = jnp.concatenate([grad_kv_w, small_half], axis=1).astype(jnp.bfloat16)
        grad_query_w = halve_all(grad_query_w.astype(jnp.bfloat16), group_steps[:1])
        if layer > 0:
            waiting = (grad_output_w, grad_query_w, grad_kv_w)
        else:
            grad_query_w = halve_all(grad_query_w, group_steps[1:])
            early = jnp.concatenate([grad_output_w, grad_query_w], axis=1)
            attention_list[layer] = jnp.concatenate(
                [
                    halve_all(early, chip_steps),
                    halve_all(grad_kv_w, group_steps + chip_steps),
                ],
                axis=1,
            )
        expert_held = [
            place(part, held, layer, exp_dev) for part, held in zip(expert_parts, expert_held)
        ]
        grad_hidden = grad_middle + grad_norm_in
    stacked = jnp.stack(attention_list).astype(jnp.float32)
    cuts = [query_width, query_width, key_width, key_width, expert_total, 1, 1]
    cuts = [sum(cuts[:index]) for index in range(len(cuts) + 1)]
    output_grads, query_grads, key_grads, value_grads, router_grads, one, two = (
        stacked[:, :, start:stop] for start, stop in zip(cuts[:-1], cuts[1:])
    )
    down_grads, gate_grads, up_grads = expert_held
    return (
        output.astype(jnp.bfloat16).reshape(sequences_per_device, block_length, model_width),
        grad_hidden.reshape(sequences_per_device, block_length, model_width),
        query_grads,
        key_grads,
        value_grads,
        jnp.swapaxes(output_grads, 1, 2),
        one[:, :, 0],
        two[:, :, 0],
        router_grads,
        gate_grads,
        up_grads,
        jnp.swapaxes(down_grads, 2, 3),
    )


def solution(mesh):
    in_specs = (
        P("dp", "expert", None),
        P(None, "expert", "dp", None, None),
        P("dp", "expert", None),
        P(None, ("dp", "expert"), None),
        P(None, ("dp", "expert"), None),
        P(None, ("dp", "expert"), None),
        P(None, None, ("dp", "expert")),
        P(None, ("dp", "expert")),
        P(None, ("dp", "expert")),
        P(None, ("dp", "expert"), None),
        P(None, "expert", "dp", None),
        P(None, "expert", "dp", None),
        P(None, "expert", None, "dp"),
    )
    out_specs = (
        P("dp", "expert", None),
        P("dp", "expert", None),
        P(None, ("dp", "expert"), None),
        P(None, ("dp", "expert"), None),
        P(None, ("dp", "expert"), None),
        P(None, None, ("dp", "expert")),
        P(None, ("dp", "expert")),
        P(None, ("dp", "expert")),
        P(None, ("dp", "expert"), None),
        P(None, "expert", "dp", None),
        P(None, "expert", "dp", None),
        P(None, "expert", None, "dp"),
    )
    return jax.shard_map(body, mesh=mesh, in_specs=in_specs, out_specs=out_specs, check_vma=False)
```

```python
import math

import jax
import jax.numpy as jnp
from jax import lax
from jax.experimental import pallas as pl
from jax.experimental.pallas import tpu as pltpu
from jax.sharding import PartitionSpec as P

QUERY_HEADS = 24
KEY_VALUE_HEADS = 8
HEAD_SIZE = 64
LAYER_COUNT = 2


eps_norm = 1e-06
highest_precision = lax.Precision.HIGHEST


def rotary_tables(positions, half_dim):
    frequency = jnp.exp(-math.log(10000.0) * jnp.arange(half_dim, dtype=jnp.float32) / half_dim)
    angles = positions.astype(jnp.float32)[:, None] * frequency[None, :]
    return (jnp.cos(angles), jnp.sin(angles))


def rotate_features(values, cosine_table, sine_table):
    half_dim = values.shape[-1] // 2
    first_half = values[..., :half_dim]
    second_half = values[..., half_dim:]
    cos_part = cosine_table[:, None, :]
    sin_part = sine_table[:, None, :]
    return jnp.concatenate(
        [
            first_half * cos_part - second_half * sin_part,
            second_half * cos_part + first_half * sin_part,
        ],
        axis=-1,
    )


def norm_forward(values, gain_vec):
    inv_rms = lax.rsqrt(jnp.mean(values * values, axis=-1, keepdims=True) + eps_norm)
    return (values * inv_rms * gain_vec, inv_rms)


def norm_backward(values, inv_rms, gain_vec, upstream):
    scaled = upstream * gain_vec
    grad_gain = jnp.sum(upstream * values * inv_rms, axis=0)
    grad_values = inv_rms * (
        scaled - values * inv_rms * inv_rms * jnp.mean(scaled * values, axis=-1, keepdims=True)
    )
    return (grad_values, grad_gain)


def stack_member(layer_list, member):
    return jnp.stack([layer_parts[member] for layer_parts in layer_list], axis=0)


def exchange(blocks):
    return lax.all_to_all(blocks, "expert", split_axis=0, concat_axis=0, tiled=True)


def gather_rows(rows):
    groups = lax.axis_size("expert")
    blocks = exchange(jnp.broadcast_to(rows[None], (groups,) + rows.shape))
    return blocks.reshape((groups * rows.shape[0],) + rows.shape[1:])


def sum_rows(partial_rows):
    groups = lax.axis_size("expert")
    blocks = partial_rows.reshape((groups, -1) + partial_rows.shape[1:])
    return jnp.sum(exchange(blocks).astype(jnp.float32), axis=0)


def same_core():
    members = range(lax.axis_size("dp"))
    return [[i for i in members if i % 2 == core] for core in range(2)]


def swap_cores(values):
    return lax.ppermute(values, "dp", [(i, i ^ 1) for i in range(lax.axis_size("dp"))])


def exchange_chips(blocks):
    return lax.all_to_all(
        blocks, "dp", split_axis=0, concat_axis=0, axis_index_groups=same_core(), tiled=True
    )


def gather_chips(shard):
    chips = lax.axis_size("dp") // 2
    return exchange_chips(jnp.broadcast_to(shard[None], (chips,) + shard.shape))


def gather_groups(chip_rows):
    groups = lax.axis_size("expert")
    return exchange(jnp.broadcast_to(chip_rows[None], (groups,) + chip_rows.shape))


def join_cores(own):
    width = own.shape[-1]
    other = swap_cores(own)
    first = lax.axis_index("dp") % 2 == 0
    both = jnp.stack([jnp.where(first, own, other), jnp.where(first, other, own)])
    return both.transpose(2, 0, 1, 3, 4).reshape(-1, width)


def core_major(columns):
    chips = lax.axis_size("dp") // 2
    groups = lax.axis_size("expert")
    split = columns.reshape(columns.shape[0], chips, 2, groups, -1)
    halves = split.transpose(2, 0, 3, 1, 4).reshape(2, columns.shape[0], -1)
    core = lax.axis_index("dp") % 2
    mine = lax.dynamic_index_in_dim(halves, core, 0, keepdims=False)
    theirs = lax.dynamic_index_in_dim(halves, 1 - core, 0, keepdims=False)
    return jnp.concatenate([mine, swap_cores(theirs)], axis=0)


def both_cores(rows):
    return jnp.concatenate([rows, swap_cores(rows)], axis=0)


def halve(partial, axis_name, step):
    size = lax.axis_size(axis_name)
    width = partial.shape[-1]
    blocks = partial.reshape(size // (2 * step), 2, -1, width)
    side = (lax.axis_index(axis_name) // step) % 2
    mine = lax.dynamic_index_in_dim(blocks, side, 1, keepdims=False)
    theirs = lax.dynamic_index_in_dim(blocks, 1 - side, 1, keepdims=False)
    arrived = lax.ppermute(
        theirs.reshape(-1, width), axis_name, [(i, i ^ step) for i in range(size)]
    )
    total = mine.reshape(-1, width).astype(jnp.float32) + arrived.astype(jnp.float32)
    return total.astype(jnp.bfloat16)


def halvings(axis_name, least):
    steps = [least]
    while 2 * steps[-1] < lax.axis_size(axis_name):
        steps.append(2 * steps[-1])
    return [(axis_name, step) for step in steps]


def halve_all(partial, steps):
    for axis_name, step in steps:
        partial = halve(partial, axis_name, step)
    return partial


def dot_f32(left, right, left_dims, right_dims):
    return lax.dot_general(
        left, right, ((left_dims, right_dims), ((), ())), preferred_element_type=jnp.float32
    )


def contract(left, right, left_dim, right_dim):
    return lax.dot_general(
        left,
        right,
        (((left_dim,), (right_dim,)), ((), ())),
        preferred_element_type=jnp.float32,
    )


def pick_column(table, column):
    lanes = lax.broadcasted_iota(jnp.int32, table.shape, 1)
    return jnp.sum(jnp.where(lanes == column, table, 0.0), axis=1, keepdims=True)


def expert_forward_kernel(rows_ref, gate_ref, up_ref, share_ref, gate_out, up_out, act_out):
    rows = rows_ref[...]
    gate_val = contract(rows, gate_ref[...], 1, 0)
    up_val = contract(rows, up_ref[...], 1, 0)
    share = pick_column(share_ref[...], pl.program_id(0))
    gate_out[...] = gate_val.astype(jnp.bfloat16)
    up_out[...] = up_val.astype(jnp.bfloat16)
    act_out[...] = (gate_val * jax.nn.sigmoid(gate_val) * up_val * share).astype(jnp.bfloat16)


def expert_forward(rows, gate, up, share):
    row_total, width = rows.shape
    experts = share.shape[1]
    hidden = gate.shape[1] // experts
    tile = row_total // 2
    row_block = pl.BlockSpec((tile, width), lambda e, r: (r, 0))
    weight_block = pl.BlockSpec((width, hidden), lambda e, r: (0, e))
    hidden_block = pl.BlockSpec((tile, hidden), lambda e, r: (r, e))
    return pl.pallas_call(
        expert_forward_kernel,
        grid=(experts, 2),
        in_specs=[
            row_block,
            weight_block,
            weight_block,
            pl.BlockSpec((tile, experts), lambda e, r: (r, 0)),
        ],
        out_specs=[hidden_block] * 3,
        out_shape=[jax.ShapeDtypeStruct((row_total, gate.shape[1]), jnp.bfloat16)] * 3,
        cost_estimate=pl.CostEstimate(
            flops=4 * row_total * width * gate.shape[1],
            transcendentals=row_total * gate.shape[1],
            bytes_accessed=4 * width * gate.shape[1] + 6 * row_total * gate.shape[1],
        ),
    )(rows, gate, up, share)


def expert_backward_kernel(
    group_ref,
    grad_ref,
    down_ref,
    gate_ref,
    up_ref,
    gate_val_ref,
    up_val_ref,
    share_ref,
    grad_gate_out,
    grad_up_out,
    rows_out,
    rows_acc,
    sums_acc,
):
    expert = pl.program_id(0)
    tile, width = grad_ref.shape
    experts = pl.num_programs(0)
    window = pl.ds(pl.multiple_of(pl.program_id(1) * tile, tile), tile)
    grad_scaled = contract(grad_ref[...], down_ref[...], 1, 0)
    gate_val = gate_val_ref[...].astype(jnp.float32)
    up_val = up_val_ref[...].astype(jnp.float32)
    sigmoid_val = jax.nn.sigmoid(gate_val)
    silu_val = gate_val * sigmoid_val
    grad_sum = jnp.sum(grad_scaled * silu_val * up_val, axis=1, keepdims=True)
    grad_inner = grad_scaled * pick_column(share_ref[...], expert)
    grad_gate = (
        grad_inner * up_val * sigmoid_val * (1.0 + gate_val * (1.0 - sigmoid_val))
    ).astype(jnp.bfloat16)
    grad_up = (grad_inner * silu_val).astype(jnp.bfloat16)
    grad_gate_out[...] = grad_gate
    grad_up_out[...] = grad_up
    grad_rows = contract(grad_gate, gate_ref[...], 1, 1) + contract(
        grad_up, up_ref[...], 1, 1
    )
    lanes = lax.broadcasted_iota(jnp.int32, (tile, sums_acc.shape[1]), 1)
    sum_high = grad_sum.astype(jnp.bfloat16).astype(jnp.float32)
    column = group_ref[0] * experts + expert
    grad_sums = jnp.where(lanes == column, sum_high, 0.0) + jnp.where(
        lanes == column + group_ref[1], grad_sum - sum_high, 0.0
    )

    @pl.when(expert == 0)
    def _():
        rows_acc[window, :] = grad_rows
        sums_acc[window, :] = grad_sums

    @pl.when(expert > 0)
    def _():
        rows_acc[window, :] += grad_rows
        sums_acc[window, :] += grad_sums

    @pl.when(expert == pl.num_programs(0) - 1)
    def _():
        rows_out[:, :width] = rows_acc[window, :].astype(jnp.bfloat16)
        rows_out[:, width:] = sums_acc[window, :].astype(jnp.bfloat16)


def expert_backward(group, grad, down, gate, up, gate_val, up_val, share, extra):
    row_total, width = grad.shape
    experts = share.shape[1]
    hidden = gate.shape[1] // experts
    tile = row_total // 2
    row_block = pl.BlockSpec((tile, width), lambda e, r, g: (r, 0))
    weight_block = pl.BlockSpec((width, hidden), lambda e, r, g: (0, e))
    hidden_block = pl.BlockSpec((tile, hidden), lambda e, r, g: (r, e))
    hidden_shape = jax.ShapeDtypeStruct((row_total, gate.shape[1]), jnp.bfloat16)
    return pl.pallas_call(
        expert_backward_kernel,
        grid_spec=pltpu.PrefetchScalarGridSpec(
            num_scalar_prefetch=1,
            grid=(experts, 2),
            in_specs=[
                row_block,
                weight_block,
                weight_block,
                weight_block,
                hidden_block,
                hidden_block,
                pl.BlockSpec((tile, experts), lambda e, r, g: (r, 0)),
            ],
            out_specs=[
                hidden_block,
                hidden_block,
                pl.BlockSpec(
                    (tile, width + extra),
                    lambda e, r, g: (jnp.where(e == experts - 1, r, 0), 0),
                ),
            ],
            scratch_shapes=[
                pltpu.VMEM((row_total, width), jnp.float32),
                pltpu.VMEM((row_total, extra), jnp.float32),
            ],
        ),
        out_shape=[
            hidden_shape,
            hidden_shape,
            jax.ShapeDtypeStruct((row_total, width + extra), jnp.bfloat16),
        ],
        cost_estimate=pl.CostEstimate(
            flops=6 * row_total * width * gate.shape[1],
            transcendentals=row_total * gate.shape[1],
            bytes_accessed=6 * width * gate.shape[1] + 8 * row_total * gate.shape[1],
        ),
    )(group, grad, down, gate, up, gate_val, up_val, share)


def attention_probs(block_ref, query, key):
    scores = contract(key, query, 1, 1) * HEAD_SIZE ** (-0.5)
    key_at = lax.broadcasted_iota(jnp.int32, scores.shape, 0)
    query_at = lax.broadcasted_iota(jnp.int32, scores.shape, 1)
    offset = block_ref[0] * query.shape[0]
    masked = jnp.where(key_at <= query_at + offset, scores, -1e30)
    exp_scores = jnp.exp(masked - jnp.max(masked, axis=0, keepdims=True))
    return exp_scores / jnp.sum(exp_scores, axis=0, keepdims=True)


def head(values, index):
    return values[:, index * HEAD_SIZE : (index + 1) * HEAD_SIZE]


def attention_forward_kernel(block_ref, query_ref, key_ref, value_ref, out_ref):
    query, key, value = query_ref[...], key_ref[...], value_ref[...]
    group = QUERY_HEADS // KEY_VALUE_HEADS
    outs = []
    for index in range(2 * group):
        shared = index // group
        probs = attention_probs(block_ref, head(query, index), head(key, shared))
        outs.append(contract(head(value, shared), probs.astype(jnp.bfloat16), 0, 0))
    out_ref[...] = jnp.concatenate(outs, axis=0).T.astype(jnp.bfloat16)


def attention_specs(tokens, keys):
    pairs = KEY_VALUE_HEADS // 2
    query_block = pl.BlockSpec((tokens, QUERY_HEADS // pairs * HEAD_SIZE), lambda i, b: (0, i))
    key_block = pl.BlockSpec((keys, 2 * HEAD_SIZE), lambda i, b: (0, i))
    value_block = pl.BlockSpec((keys, 2 * HEAD_SIZE), lambda i, b: (0, i + pairs))
    return (pairs, query_block, key_block, value_block)


def attention_forward(block, query, key_value):
    tokens, width = query.shape
    keys = key_value.shape[0]
    pairs, query_block, key_block, value_block = attention_specs(tokens, keys)
    return pl.pallas_call(
        attention_forward_kernel,
        grid_spec=pltpu.PrefetchScalarGridSpec(
            num_scalar_prefetch=1,
            grid=(pairs,),
            in_specs=[query_block, key_block, value_block],
            out_specs=query_block,
        ),
        out_shape=jax.ShapeDtypeStruct((tokens, width), jnp.bfloat16),
        cost_estimate=pl.CostEstimate(
            flops=16 * tokens * width * keys,
            transcendentals=QUERY_HEADS * tokens * keys,
            bytes_accessed=4 * tokens * width + 2 * key_value.size,
        ),
    )(block, query, key_value, key_value)


def attention_backward_kernel(
    block_ref, query_ref, grad_ref, key_ref, value_ref, grad_query_out, grad_key_value_out
):
    query, grad, key, value = query_ref[...], grad_ref[...], key_ref[...], value_ref[...]
    group = QUERY_HEADS // KEY_VALUE_HEADS
    scale = HEAD_SIZE ** (-0.5)
    grad_queries, grad_keys, grad_values = [], [], []
    for shared in range(2):
        grad_key, grad_value = 0.0, 0.0
        for index in range(shared * group, (shared + 1) * group):
            query_one, grad_one = head(query, index), head(grad, index)
            probs = attention_probs(block_ref, query_one, head(key, shared))
            grad_probs = contract(head(value, shared), grad_one, 1, 1)
            centre = jnp.sum(probs * grad_probs, axis=0, keepdims=True)
            grad_scores = (probs * (grad_probs - centre)).astype(jnp.bfloat16)
            grad_queries.append(contract(head(key, shared), grad_scores, 0, 0) * scale)
            grad_key += contract(grad_scores, query_one, 1, 0)
            grad_value += contract(probs.astype(jnp.bfloat16), grad_one, 1, 0)
        grad_keys.append(grad_key * scale)
        grad_values.append(grad_value)
    grad_query_out[...] = jnp.concatenate(grad_queries, axis=0).T
    grad_key_value_out[...] = jnp.concatenate(grad_keys + grad_values, axis=1).astype(
        jnp.bfloat16
    )


def attention_backward(block, query, grad, key_value):
    tokens, width = query.shape
    keys = key_value.shape[0]
    pairs, query_block, key_block, value_block = attention_specs(tokens, keys)
    return pl.pallas_call(
        attention_backward_kernel,
        grid_spec=pltpu.PrefetchScalarGridSpec(
            num_scalar_prefetch=1,
            grid=(pairs,),
            in_specs=[query_block, query_block, key_block, value_block],
            out_specs=[
                query_block,
                pl.BlockSpec((keys, 4 * HEAD_SIZE), lambda i, b: (0, i)),
            ],
        ),
        out_shape=[
            jax.ShapeDtypeStruct((tokens, width), jnp.float32),
            jax.ShapeDtypeStruct(key_value.shape, jnp.bfloat16),
        ],
        cost_estimate=pl.CostEstimate(
            flops=40 * tokens * width * keys,
            transcendentals=QUERY_HEADS * tokens * keys,
            bytes_accessed=8 * tokens * width + 4 * key_value.size,
        ),
    )(block, query, grad, key_value, key_value)


def place_kernel(part_ref, held_ref, out_ref):
    del held_ref
    out_ref[0, 0] = part_ref[...].astype(jnp.float32)


def place_first_kernel(part_ref, out_ref):
    out_ref[0, 0] = part_ref[...].astype(jnp.float32)


def place(part, held, layer, experts):
    rows = part.shape[0]
    block = (rows, part.shape[1] // experts)
    in_specs = [pl.BlockSpec(block, lambda e: (0, e))]
    operands = [part]
    if held is not None:
        in_specs.append(pl.BlockSpec(memory_space=pl.ANY))
        operands.append(held)
    return pl.pallas_call(
        place_first_kernel if held is None else place_kernel,
        grid=(experts,),
        in_specs=in_specs,
        out_specs=pl.BlockSpec((1, 1) + block, lambda e: (layer, e, 0, 0)),
        out_shape=jax.ShapeDtypeStruct((LAYER_COUNT, experts) + block, jnp.float32),
        input_output_aliases={} if held is None else {1: 0},
    )(*operands)


def body(
    inputs,
    routes,
    cotangent,
    query_weight,
    key_projection_weight,
    value_projection_weight,
    output_weight,
    attention_gain,
    expert_gain,
    router_weight,
    gate_weight,
    up_weight,
    down_weight,
):
    sequences_per_device, block_length, model_width = inputs.shape
    token_total = sequences_per_device * block_length
    exp_dev = gate_weight.shape[1]
    groups = lax.axis_size("expert")
    expert_total = exp_dev * groups
    all_rows = token_total * groups
    query_width = query_weight.shape[2]
    key_width = key_projection_weight.shape[2]
    my_group = lax.axis_index("expert")
    positions = my_group * block_length + jnp.arange(block_length, dtype=jnp.int32)
    cosine_table, sine_table = rotary_tables(positions, HEAD_SIZE // 2)
    block_at = my_group.astype(jnp.int32).reshape(1)
    group_at = jnp.stack([my_group.astype(jnp.int32), jnp.int32(expert_total)])
    expert_ids = jnp.arange(expert_total, dtype=jnp.int32)
    small_width = -(-(expert_total + 2) // 128) * 128
    gate_width = -(-(2 * expert_total) // 128) * 128
    edges = (
        query_width,
        query_width + key_width,
        query_width + 2 * key_width,
        query_width + 2 * key_width + model_width,
        query_width + 2 * key_width + model_width + expert_total,
        query_width + 2 * key_width + model_width + expert_total + 1,
    )

    def pack_attention(query_part, key_part, value_part, output_part, router_part, one, two):
        rows = query_part.shape[0]
        fill = jnp.zeros((rows, small_width - expert_total - 2), query_part.dtype)
        return jnp.concatenate(
            [
                query_part,
                key_part,
                value_part,
                output_part,
                router_part,
                one[:, None],
                two[:, None],
                fill,
            ],
            axis=1,
        )

    chosen_hot = jnp.any(
        routes.reshape(LAYER_COUNT, token_total, -1)[:, :, :, None] == expert_ids, axis=2
    )
    chosen_all = gather_rows(
        jnp.moveaxis(chosen_hot, 0, 1).reshape(token_total, -1).astype(jnp.bfloat16)
    ).reshape(all_rows, LAYER_COUNT, expert_total)

    shards = [
        pack_attention(
            query_weight[layer],
            key_projection_weight[layer],
            value_projection_weight[layer],
            output_weight[layer].T,
            router_weight[layer],
            attention_gain[layer],
            expert_gain[layer],
        )
        for layer in range(LAYER_COUNT)
    ]
    packed = [lax.all_gather(shards[0], ("dp", "expert"), axis=0, tiled=True)]
    ff_width = gate_weight.shape[3]
    hidden_width = exp_dev * ff_width
    gathered = [
        tuple(
            lax.all_gather(rows.reshape(-1, hidden_width), "dp", axis=0, tiled=True)
            for rows in (
                gate_weight[layer].transpose(1, 0, 2),
                up_weight[layer].transpose(1, 0, 2),
                down_weight[layer].transpose(2, 0, 1),
            )
        )
        for layer in range(LAYER_COUNT)
    ]

    def shares_of(rows, router_full, hot):
        logits = jnp.dot(rows, router_full, preferred_element_type=jnp.float32)
        masked = jnp.where(hot, logits, -1e30)
        exps = jnp.where(hot, jnp.exp(masked - jnp.max(masked, axis=1, keepdims=True)), 0.0)
        return exps / jnp.sum(exps, axis=1, keepdims=True)

    def expert_rows(act, down):
        return dot_f32(act, down, (1,), (1,)).astype(jnp.bfloat16)

    def layer_forward(hidden, layer):
        full = packed[layer]
        qkv_full = full[:, : edges[2]]
        output_full = full[:, edges[2] : edges[3]]
        router_full = full[:, edges[3] : edges[4]]
        gain_one = full[:, edges[4]].astype(jnp.float32)
        gain_two = full[:, edges[5]].astype(jnp.float32)
        gate_full, up_full, down_full = gathered[layer]
        first_normalized, inv_one = norm_forward(hidden, gain_one)
        first_normalized = first_normalized.astype(jnp.bfloat16)
        linear = jnp.dot(first_normalized, qkv_full, preferred_element_type=jnp.float32)
        query_rotated = rotate_features(
            linear[:, : edges[0]].reshape(token_total, QUERY_HEADS, HEAD_SIZE),
            cosine_table,
            sine_table,
        ).astype(jnp.bfloat16)
        query_rotated = query_rotated.reshape(token_total, query_width)
        key_rot = rotate_features(
            linear[:, edges[0] : edges[1]].reshape(token_total, KEY_VALUE_HEADS, HEAD_SIZE),
            cosine_table,
            sine_table,
        ).astype(jnp.bfloat16)
        key_value = jnp.concatenate(
            [
                key_rot.reshape(token_total, key_width),
                linear[:, edges[1] :].astype(jnp.bfloat16),
            ],
            axis=1,
        )
        key_value_all = gather_rows(key_value)
        ahead = layer + 1 < LAYER_COUNT
        if ahead:
            key_value_all, next_shard = lax.optimization_barrier(
                (key_value_all, shards[layer + 1])
            )
            next_rows = gather_chips(next_shard)
        attended = attention_forward(block_at, query_rotated, key_value_all)
        middle = hidden + dot_f32(attended, output_full, (1,), (1,))
        normed_two, inv_two = norm_forward(middle, gain_two)
        normed_two = normed_two.astype(jnp.bfloat16)
        arrived = gather_rows(normed_two)
        if ahead:
            arrived, next_rows = lax.optimization_barrier((arrived, next_rows))
            next_rows = gather_groups(next_rows)
        share_all = shares_of(arrived, router_full, chosen_all[:, layer] > 0)
        share_own = shares_of(normed_two, router_full, chosen_hot[layer])
        share_local = lax.dynamic_slice_in_dim(share_all, my_group * exp_dev, exp_dev, axis=1)
        gate_low, up_low, scaled_act = expert_forward(
            arrived, gate_full, up_full, share_local
        )
        if ahead:
            scaled_act, next_rows = lax.optimization_barrier((scaled_act, next_rows))
            packed.append(join_cores(next_rows))
        kept_state = (
            hidden,
            inv_one,
            first_normalized,
            query_rotated,
            key_value_all,
            attended,
            middle,
            inv_two,
            normed_two,
            share_own,
            share_local,
            arrived,
            gate_low,
            up_low,
            scaled_act,
            qkv_full,
            output_full,
            gain_one,
            gain_two,
            router_full,
            gate_full,
            up_full,
            down_full,
        )
        return kept_state

    hidden = inputs.astype(jnp.float32).reshape(token_total, model_width)
    kept_states = []
    for layer in range(LAYER_COUNT):
        kept_state = layer_forward(hidden, layer)
        kept_states.append(kept_state)
        last_middle, last_act, last_down = kept_state[6], kept_state[14], kept_state[-1]
        if layer + 1 < LAYER_COUNT:
            hidden = last_middle + sum_rows(expert_rows(last_act, last_down))
    output = None
    grad_hidden = cotangent.astype(jnp.float32).reshape(token_total, model_width)
    attention_list = [None] * LAYER_COUNT
    placed = []
    waiting = None
    group_steps = halvings("expert", 1)
    chip_steps = halvings("dp", 2)
    for layer in range(LAYER_COUNT - 1, -1, -1):
        (
            layer_hidden,
            inv_one,
            first_normalized,
            query_rotated,
            key_value_all,
            attended,
            middle,
            inv_two,
            normed_two,
            share_own,
            share_local,
            arrived,
            gate_low,
            up_low,
            scaled_act,
            qkv_full,
            output_full,
            gain_one,
            gain_two,
            router_full,
            gate_full,
            up_full,
            down_full,
        ) = kept_states[layer]
        grad_all = gather_rows(grad_hidden.astype(jnp.bfloat16))
        if waiting is not None:
            grad_all, waiting = lax.optimization_barrier((grad_all, waiting))
            out_part, query_part, kv_part = waiting
            out_part = halve_all(out_part, group_steps[1:])
            query_part = halve_all(query_part, group_steps[:1])
            kv_part = halve_all(kv_part, group_steps[:1])
        grad_down = dot_f32(grad_all, scaled_act, (0,), (0,)).astype(jnp.bfloat16)
        grad_all, grad_down = lax.optimization_barrier((grad_all, grad_down))
        expert_parts = [lax.psum_scatter(grad_down, "dp", scatter_dimension=0, tiled=True)]
        grad_gate_val, grad_up_val, grad_rows = expert_backward(
            group_at,
            grad_all,
            down_full,
            gate_full,
            up_full,
            gate_low,
            up_low,
            share_local,
            gate_width,
        )
        grad_gate_w = dot_f32(arrived, grad_gate_val, (0,), (0,)).astype(jnp.bfloat16)
        grad_up_w = dot_f32(arrived, grad_up_val, (0,), (0,)).astype(jnp.bfloat16)
        back = sum_rows(grad_rows)
        if waiting is None:
            last_rows = expert_rows(last_act, last_down)
            back, last_rows = lax.optimization_barrier((back, last_rows))
            output = last_middle + sum_rows(last_rows)
        else:
            back, out_part, query_part, kv_part = lax.optimization_barrier(
                (back, out_part, query_part, kv_part)
            )
            late_part = jnp.concatenate([query_part, kv_part], axis=1)
            late_part = halve_all(late_part, group_steps[1:])
        back, grad_gate_w, grad_up_w = lax.optimization_barrier((back, grad_gate_w, grad_up_w))
        expert_parts += [
            lax.psum_scatter(grad_gate_w, "dp", scatter_dimension=0, tiled=True),
            lax.psum_scatter(grad_up_w, "dp", scatter_dimension=0, tiled=True),
        ]
        grad_gates_own = (
            back[:, model_width : model_width + expert_total]
            + back[:, model_width + expert_total : model_width + 2 * expert_total]
        )
        grad_logits = (
            share_own
            * (grad_gates_own - jnp.sum(share_own * grad_gates_own, axis=-1, keepdims=True))
        ).astype(jnp.bfloat16)
        grad_router = dot_f32(normed_two, grad_logits, (0,), (0,))
        grad_normed_two = back[:, :model_width] + dot_f32(grad_logits, router_full, (1,), (1,))
        grad_norm_mid, grad_gain_two = norm_backward(middle, inv_two, gain_two, grad_normed_two)
        grad_middle = grad_hidden + grad_norm_mid
        grad_branch = grad_middle.astype(jnp.bfloat16)
        grad_output_w = dot_f32(core_major(grad_branch), both_cores(attended), (0,), (0,))
        grad_output_w = halve_all(grad_output_w.astype(jnp.bfloat16), group_steps[:1])
        grad_attended = dot_f32(grad_branch, output_full, (1,), (0,)).astype(jnp.bfloat16)
        grad_query, grad_key_value_all = attention_backward(
            block_at, query_rotated, grad_attended, key_value_all
        )
        if waiting is None:
            grad_query, grad_key_value_all, output = lax.optimization_barrier(
                (grad_query, grad_key_value_all, output)
            )
        else:
            grad_query, grad_output_w, late_part = lax.optimization_barrier(
                (grad_query, grad_output_w, late_part)
            )
            grad_output_w = halve_all(grad_output_w, group_steps[1:])
            chip_part = jnp.concatenate([out_part, late_part], axis=1)
            attention_list[layer + 1] = halve_all(chip_part, chip_steps)
        grad_kv = sum_rows(grad_key_value_all)
        normed_split = core_major(first_normalized)
        grad_query_lin = (
            rotate_features(
                grad_query.reshape(token_total, QUERY_HEADS, HEAD_SIZE), cosine_table, -sine_table
            )
            .astype(jnp.bfloat16)
            .reshape(token_total, query_width)
        )
        grad_query_w = dot_f32(normed_split, both_cores(grad_query_lin), (0,), (0,))
        grad_query_w = grad_query_w.astype(jnp.bfloat16)
        if layer == 0:
            grad_kv, grad_query_w = lax.optimization_barrier((grad_kv, grad_query_w))
        grad_kv = grad_kv.reshape(token_total, -1, 2, 2 * HEAD_SIZE)
        grad_kv = grad_kv.transpose(0, 2, 1, 3).reshape(token_total, 2 * key_width)
        grad_key_lin = (
            rotate_features(
                grad_kv[:, :key_width].reshape(token_total, KEY_VALUE_HEADS, HEAD_SIZE),
                cosine_table,
                -sine_table,
            )
            .astype(jnp.bfloat16)
            .reshape(token_total, key_width)
        )
        grad_kv_lin = jnp.concatenate(
            [grad_key_lin, grad_kv[:, key_width:].astype(jnp.bfloat16)], axis=1
        )
        grad_kv_w = dot_f32(normed_split, both_cores(grad_kv_lin), (0,), (0,))
        grad_normed_one = dot_f32(grad_query_lin, qkv_full[:, : edges[0]], (1,), (1,)) + dot_f32(
            grad_kv_lin, qkv_full[:, edges[0] :], (1,), (1,)
        )
        grad_norm_in, grad_gain_one = norm_backward(
            layer_hidden, inv_one, gain_one, grad_normed_one
        )
        fill = jnp.zeros((model_width, small_width - expert_total - 2), jnp.bfloat16)
        small_part = jnp.concatenate(
            [
                grad_router.astype(jnp.bfloat16),
                grad_gain_one[:, None].astype(jnp.bfloat16),
                grad_gain_two[:, None].astype(jnp.bfloat16),
                fill,
            ],
            axis=1,
        )
        small_split = core_major(small_part.T).reshape(2, small_width, -1)
        small_half = jnp.sum(small_split.astype(jnp.float32), axis=0).T
        grad_kv_w = jnp.concatenate([grad_kv_w, small_half], axis=1).astype(jnp.bfloat16)
        if layer > 0:
            waiting = (grad_output_w, grad_query_w, grad_kv_w)
        else:
            grad_query_w = halve_all(grad_query_w, group_steps)
            early = jnp.concatenate([grad_output_w, grad_query_w], axis=1)
            attention_list[layer] = jnp.concatenate(
                [
                    halve_all(early, chip_steps),
                    halve_all(grad_kv_w, group_steps + chip_steps),
                ],
                axis=1,
            )
        placed = placed + [(layer, expert_parts)]
        grad_hidden = grad_middle + grad_norm_in
    stacked = jnp.stack(attention_list).astype(jnp.float32)
    cuts = [query_width, query_width, key_width, key_width, expert_total, 1, 1]
    cuts = [sum(cuts[:index]) for index in range(len(cuts) + 1)]
    output_grads, query_grads, key_grads, value_grads, router_grads, one, two = (
        stacked[:, :, start:stop] for start, stop in zip(cuts[:-1], cuts[1:])
    )
    expert_held = [None] * 3
    for layer, expert_parts in placed:
        if layer > 0:
            grad_kv_w, expert_parts = lax.optimization_barrier((grad_kv_w, expert_parts))
        expert_held = [
            place(part, held, layer, exp_dev) for part, held in zip(expert_parts, expert_held)
        ]
    down_grads, gate_grads, up_grads = expert_held
    return (
        output.astype(jnp.bfloat16).reshape(sequences_per_device, block_length, model_width),
        grad_hidden.reshape(sequences_per_device, block_length, model_width),
        query_grads,
        key_grads,
        value_grads,
        jnp.swapaxes(output_grads, 1, 2),
        one[:, :, 0],
        two[:, :, 0],
        router_grads,
        gate_grads,
        up_grads,
        jnp.swapaxes(down_grads, 2, 3),
    )


def solution(mesh):
    in_specs = (
        P("dp", "expert", None),
        P(None, "expert", "dp", None, None),
        P("dp", "expert", None),
        P(None, ("dp", "expert"), None),
        P(None, ("dp", "expert"), None),
        P(None, ("dp", "expert"), None),
        P(None, None, ("dp", "expert")),
        P(None, ("dp", "expert")),
        P(None, ("dp", "expert")),
        P(None, ("dp", "expert"), None),
        P(None, "expert", "dp", None),
        P(None, "expert", "dp", None),
        P(None, "expert", None, "dp"),
    )
    out_specs = (
        P("dp", "expert", None),
        P("dp", "expert", None),
        P(None, ("dp", "expert"), None),
        P(None, ("dp", "expert"), None),
        P(None, ("dp", "expert"), None),
        P(None, None, ("dp", "expert")),
        P(None, ("dp", "expert")),
        P(None, ("dp", "expert")),
        P(None, ("dp", "expert"), None),
        P(None, "expert", "dp", None),
        P(None, "expert", "dp", None),
        P(None, "expert", None, "dp"),
    )
    return jax.shard_map(body, mesh=mesh, in_specs=in_specs, out_specs=out_specs, check_vma=False)
```

```python
import math

import jax
import jax.numpy as jnp
from jax import lax
from jax.experimental import pallas as pl
from jax.experimental.pallas import tpu as pltpu
from jax.sharding import PartitionSpec as P

QUERY_HEADS = 24
KEY_VALUE_HEADS = 8
HEAD_SIZE = 64
LAYER_COUNT = 2


eps_norm = 1e-06
highest_precision = lax.Precision.HIGHEST


def rotary_tables(positions, half_dim):
    frequency = jnp.exp(-math.log(10000.0) * jnp.arange(half_dim, dtype=jnp.float32) / half_dim)
    angles = positions.astype(jnp.float32)[:, None] * frequency[None, :]
    return (jnp.cos(angles), jnp.sin(angles))


def rotate_features(values, cosine_table, sine_table):
    half_dim = values.shape[-1] // 2
    first_half = values[..., :half_dim]
    second_half = values[..., half_dim:]
    cos_part = cosine_table[:, None, :]
    sin_part = sine_table[:, None, :]
    return jnp.concatenate(
        [
            first_half * cos_part - second_half * sin_part,
            second_half * cos_part + first_half * sin_part,
        ],
        axis=-1,
    )


def norm_forward(values, gain_vec):
    inv_rms = lax.rsqrt(jnp.mean(values * values, axis=-1, keepdims=True) + eps_norm)
    return (values * inv_rms * gain_vec, inv_rms)


def norm_backward(values, inv_rms, gain_vec, upstream):
    scaled = upstream * gain_vec
    grad_gain = jnp.sum(upstream * values * inv_rms, axis=0)
    grad_values = inv_rms * (
        scaled - values * inv_rms * inv_rms * jnp.mean(scaled * values, axis=-1, keepdims=True)
    )
    return (grad_values, grad_gain)


def stack_member(layer_list, member):
    return jnp.stack([layer_parts[member] for layer_parts in layer_list], axis=0)


def exchange(blocks):
    return lax.all_to_all(blocks, "expert", split_axis=0, concat_axis=0, tiled=True)


def gather_rows(rows):
    groups = lax.axis_size("expert")
    blocks = exchange(jnp.broadcast_to(rows[None], (groups,) + rows.shape))
    return blocks.reshape((groups * rows.shape[0],) + rows.shape[1:])


def sum_rows(partial_rows):
    groups = lax.axis_size("expert")
    blocks = partial_rows.reshape((groups, -1) + partial_rows.shape[1:])
    return jnp.sum(exchange(blocks).astype(jnp.float32), axis=0)


def same_core():
    members = range(lax.axis_size("dp"))
    return [[i for i in members if i % 2 == core] for core in range(2)]


def swap_cores(values):
    return lax.ppermute(values, "dp", [(i, i ^ 1) for i in range(lax.axis_size("dp"))])


def exchange_chips(blocks):
    return lax.all_to_all(
        blocks, "dp", split_axis=0, concat_axis=0, axis_index_groups=same_core(), tiled=True
    )


def gather_chips(shard):
    chips = lax.axis_size("dp") // 2
    return exchange_chips(jnp.broadcast_to(shard[None], (chips,) + shard.shape))


def gather_groups(chip_rows):
    groups = lax.axis_size("expert")
    return exchange(jnp.broadcast_to(chip_rows[None], (groups,) + chip_rows.shape))


def join_cores(own):
    width = own.shape[-1]
    other = swap_cores(own)
    first = lax.axis_index("dp") % 2 == 0
    both = jnp.stack([jnp.where(first, own, other), jnp.where(first, other, own)])
    return both.transpose(2, 0, 1, 3, 4).reshape(-1, width)


def core_major(columns):
    chips = lax.axis_size("dp") // 2
    groups = lax.axis_size("expert")
    split = columns.reshape(columns.shape[0], chips, 2, groups, -1)
    halves = split.transpose(2, 0, 3, 1, 4).reshape(2, columns.shape[0], -1)
    core = lax.axis_index("dp") % 2
    mine = lax.dynamic_index_in_dim(halves, core, 0, keepdims=False)
    theirs = lax.dynamic_index_in_dim(halves, 1 - core, 0, keepdims=False)
    return jnp.concatenate([mine, swap_cores(theirs)], axis=0)


def both_cores(rows):
    return jnp.concatenate([rows, swap_cores(rows)], axis=0)


def halve(partial, axis_name, step, outer):
    size = lax.axis_size(axis_name)
    width = partial.shape[-1]
    blocks = partial.reshape(outer, 2, -1, width)
    side = (lax.axis_index(axis_name) // step) % 2
    mine = lax.dynamic_index_in_dim(blocks, side, 1, keepdims=False)
    theirs = lax.dynamic_index_in_dim(blocks, 1 - side, 1, keepdims=False)
    arrived = lax.ppermute(
        theirs.reshape(-1, width), axis_name, [(i, i ^ step) for i in range(size)]
    )
    total = mine.reshape(-1, width).astype(jnp.float32) + arrived.astype(jnp.float32)
    return total.astype(jnp.bfloat16)


def near_first(axis_name, least):
    size = lax.axis_size(axis_name)
    steps = [least]
    while 2 * steps[-1] < size:
        steps.append(2 * steps[-1])
    return [(axis_name, step, size // (2 * step)) for step in steps]


def far_first(axis_name, least):
    return [(axis_name, step, 1) for _, step, _ in reversed(near_first(axis_name, least))]


def halve_all(partial, steps):
    for step in steps:
        partial = halve(partial, *step)
    return partial


def dot_f32(left, right, left_dims, right_dims):
    return lax.dot_general(
        left, right, ((left_dims, right_dims), ((), ())), preferred_element_type=jnp.float32
    )


def contract(left, right, left_dim, right_dim):
    return lax.dot_general(
        left,
        right,
        (((left_dim,), (right_dim,)), ((), ())),
        preferred_element_type=jnp.float32,
    )


def pick_column(table, column):
    lanes = lax.broadcasted_iota(jnp.int32, table.shape, 1)
    return jnp.sum(jnp.where(lanes == column, table, 0.0), axis=1, keepdims=True)


def expert_forward_kernel(rows_ref, gate_ref, up_ref, share_ref, gate_out, up_out, act_out):
    rows = rows_ref[...]
    gate_val = contract(rows, gate_ref[...], 1, 0)
    up_val = contract(rows, up_ref[...], 1, 0)
    share = pick_column(share_ref[...], pl.program_id(0))
    gate_out[...] = gate_val.astype(jnp.bfloat16)
    up_out[...] = up_val.astype(jnp.bfloat16)
    act_out[...] = (gate_val * jax.nn.sigmoid(gate_val) * up_val * share).astype(jnp.bfloat16)


def expert_forward(rows, gate, up, share):
    row_total, width = rows.shape
    experts = share.shape[1]
    hidden = gate.shape[1] // experts
    tile = row_total // 2
    row_block = pl.BlockSpec((tile, width), lambda e, r: (r, 0))
    weight_block = pl.BlockSpec((width, hidden), lambda e, r: (0, e))
    hidden_block = pl.BlockSpec((tile, hidden), lambda e, r: (r, e))
    return pl.pallas_call(
        expert_forward_kernel,
        grid=(experts, 2),
        in_specs=[
            row_block,
            weight_block,
            weight_block,
            pl.BlockSpec((tile, experts), lambda e, r: (r, 0)),
        ],
        out_specs=[hidden_block] * 3,
        out_shape=[jax.ShapeDtypeStruct((row_total, gate.shape[1]), jnp.bfloat16)] * 3,
        cost_estimate=pl.CostEstimate(
            flops=4 * row_total * width * gate.shape[1],
            transcendentals=row_total * gate.shape[1],
            bytes_accessed=4 * width * gate.shape[1] + 6 * row_total * gate.shape[1],
        ),
    )(rows, gate, up, share)


def expert_backward_kernel(
    group_ref,
    grad_ref,
    down_ref,
    gate_ref,
    up_ref,
    gate_val_ref,
    up_val_ref,
    share_ref,
    grad_gate_out,
    grad_up_out,
    rows_out,
    rows_acc,
    sums_acc,
):
    expert = pl.program_id(0)
    tile, width = grad_ref.shape
    experts = pl.num_programs(0)
    window = pl.ds(pl.multiple_of(pl.program_id(1) * tile, tile), tile)
    grad_scaled = contract(grad_ref[...], down_ref[...], 1, 0)
    gate_val = gate_val_ref[...].astype(jnp.float32)
    up_val = up_val_ref[...].astype(jnp.float32)
    sigmoid_val = jax.nn.sigmoid(gate_val)
    silu_val = gate_val * sigmoid_val
    grad_sum = jnp.sum(grad_scaled * silu_val * up_val, axis=1, keepdims=True)
    grad_inner = grad_scaled * pick_column(share_ref[...], expert)
    grad_gate = (
        grad_inner * up_val * sigmoid_val * (1.0 + gate_val * (1.0 - sigmoid_val))
    ).astype(jnp.bfloat16)
    grad_up = (grad_inner * silu_val).astype(jnp.bfloat16)
    grad_gate_out[...] = grad_gate
    grad_up_out[...] = grad_up
    grad_rows = contract(grad_gate, gate_ref[...], 1, 1) + contract(
        grad_up, up_ref[...], 1, 1
    )
    lanes = lax.broadcasted_iota(jnp.int32, (tile, sums_acc.shape[1]), 1)
    sum_high = grad_sum.astype(jnp.bfloat16).astype(jnp.float32)
    column = group_ref[0] * experts + expert
    grad_sums = jnp.where(lanes == column, sum_high, 0.0) + jnp.where(
        lanes == column + group_ref[1], grad_sum - sum_high, 0.0
    )

    @pl.when(expert == 0)
    def _():
        rows_acc[window, :] = grad_rows
        sums_acc[window, :] = grad_sums

    @pl.when(expert > 0)
    def _():
        rows_acc[window, :] += grad_rows
        sums_acc[window, :] += grad_sums

    @pl.when(expert == pl.num_programs(0) - 1)
    def _():
        rows_out[:, :width] = rows_acc[window, :].astype(jnp.bfloat16)
        rows_out[:, width:] = sums_acc[window, :].astype(jnp.bfloat16)


def expert_backward(group, grad, down, gate, up, gate_val, up_val, share, extra):
    row_total, width = grad.shape
    experts = share.shape[1]
    hidden = gate.shape[1] // experts
    tile = row_total // 2
    row_block = pl.BlockSpec((tile, width), lambda e, r, g: (r, 0))
    weight_block = pl.BlockSpec((width, hidden), lambda e, r, g: (0, e))
    hidden_block = pl.BlockSpec((tile, hidden), lambda e, r, g: (r, e))
    hidden_shape = jax.ShapeDtypeStruct((row_total, gate.shape[1]), jnp.bfloat16)
    return pl.pallas_call(
        expert_backward_kernel,
        grid_spec=pltpu.PrefetchScalarGridSpec(
            num_scalar_prefetch=1,
            grid=(experts, 2),
            in_specs=[
                row_block,
                weight_block,
                weight_block,
                weight_block,
                hidden_block,
                hidden_block,
                pl.BlockSpec((tile, experts), lambda e, r, g: (r, 0)),
            ],
            out_specs=[
                hidden_block,
                hidden_block,
                pl.BlockSpec(
                    (tile, width + extra),
                    lambda e, r, g: (jnp.where(e == experts - 1, r, 0), 0),
                ),
            ],
            scratch_shapes=[
                pltpu.VMEM((row_total, width), jnp.float32),
                pltpu.VMEM((row_total, extra), jnp.float32),
            ],
        ),
        out_shape=[
            hidden_shape,
            hidden_shape,
            jax.ShapeDtypeStruct((row_total, width + extra), jnp.bfloat16),
        ],
        cost_estimate=pl.CostEstimate(
            flops=6 * row_total * width * gate.shape[1],
            transcendentals=row_total * gate.shape[1],
            bytes_accessed=6 * width * gate.shape[1] + 8 * row_total * gate.shape[1],
        ),
    )(group, grad, down, gate, up, gate_val, up_val, share)


def attention_probs(block_ref, query, key):
    scores = contract(key, query, 1, 1) * HEAD_SIZE ** (-0.5)
    key_at = lax.broadcasted_iota(jnp.int32, scores.shape, 0)
    query_at = lax.broadcasted_iota(jnp.int32, scores.shape, 1)
    offset = block_ref[0] * query.shape[0]
    masked = jnp.where(key_at <= query_at + offset, scores, -1e30)
    exp_scores = jnp.exp(masked - jnp.max(masked, axis=0, keepdims=True))
    return exp_scores / jnp.sum(exp_scores, axis=0, keepdims=True)


def head(values, index):
    return values[:, index * HEAD_SIZE : (index + 1) * HEAD_SIZE]


def attention_forward_kernel(block_ref, query_ref, key_ref, value_ref, out_ref):
    query, key, value = query_ref[...], key_ref[...], value_ref[...]
    group = QUERY_HEADS // KEY_VALUE_HEADS
    outs = []
    for index in range(2 * group):
        shared = index // group
        probs = attention_probs(block_ref, head(query, index), head(key, shared))
        outs.append(contract(head(value, shared), probs.astype(jnp.bfloat16), 0, 0))
    out_ref[...] = jnp.concatenate(outs, axis=0).T.astype(jnp.bfloat16)


def attention_specs(tokens, keys):
    pairs = KEY_VALUE_HEADS // 2
    query_block = pl.BlockSpec((tokens, QUERY_HEADS // pairs * HEAD_SIZE), lambda i, b: (0, i))
    key_block = pl.BlockSpec((keys, 2 * HEAD_SIZE), lambda i, b: (0, i))
    value_block = pl.BlockSpec((keys, 2 * HEAD_SIZE), lambda i, b: (0, i + pairs))
    return (pairs, query_block, key_block, value_block)


def attention_forward(block, query, key_value):
    tokens, width = query.shape
    keys = key_value.shape[0]
    pairs, query_block, key_block, value_block = attention_specs(tokens, keys)
    return pl.pallas_call(
        attention_forward_kernel,
        grid_spec=pltpu.PrefetchScalarGridSpec(
            num_scalar_prefetch=1,
            grid=(pairs,),
            in_specs=[query_block, key_block, value_block],
            out_specs=query_block,
        ),
        out_shape=jax.ShapeDtypeStruct((tokens, width), jnp.bfloat16),
        cost_estimate=pl.CostEstimate(
            flops=16 * tokens * width * keys,
            transcendentals=QUERY_HEADS * tokens * keys,
            bytes_accessed=4 * tokens * width + 2 * key_value.size,
        ),
    )(block, query, key_value, key_value)


def attention_backward_kernel(
    block_ref, query_ref, grad_ref, key_ref, value_ref, grad_query_out, grad_key_value_out
):
    query, grad, key, value = query_ref[...], grad_ref[...], key_ref[...], value_ref[...]
    group = QUERY_HEADS // KEY_VALUE_HEADS
    scale = HEAD_SIZE ** (-0.5)
    grad_queries, grad_keys, grad_values = [], [], []
    for shared in range(2):
        grad_key, grad_value = 0.0, 0.0
        for index in range(shared * group, (shared + 1) * group):
            query_one, grad_one = head(query, index), head(grad, index)
            probs = attention_probs(block_ref, query_one, head(key, shared))
            grad_probs = contract(head(value, shared), grad_one, 1, 1)
            centre = jnp.sum(probs * grad_probs, axis=0, keepdims=True)
            grad_scores = (probs * (grad_probs - centre)).astype(jnp.bfloat16)
            grad_queries.append(contract(head(key, shared), grad_scores, 0, 0) * scale)
            grad_key += contract(grad_scores, query_one, 1, 0)
            grad_value += contract(probs.astype(jnp.bfloat16), grad_one, 1, 0)
        grad_keys.append(grad_key * scale)
        grad_values.append(grad_value)
    grad_query_out[...] = jnp.concatenate(grad_queries, axis=0).T
    grad_key_value_out[...] = jnp.concatenate(grad_keys + grad_values, axis=1).astype(
        jnp.bfloat16
    )


def attention_backward(block, query, grad, key_value):
    tokens, width = query.shape
    keys = key_value.shape[0]
    pairs, query_block, key_block, value_block = attention_specs(tokens, keys)
    return pl.pallas_call(
        attention_backward_kernel,
        grid_spec=pltpu.PrefetchScalarGridSpec(
            num_scalar_prefetch=1,
            grid=(pairs,),
            in_specs=[query_block, query_block, key_block, value_block],
            out_specs=[
                query_block,
                pl.BlockSpec((keys, 4 * HEAD_SIZE), lambda i, b: (0, i)),
            ],
        ),
        out_shape=[
            jax.ShapeDtypeStruct((tokens, width), jnp.float32),
            jax.ShapeDtypeStruct(key_value.shape, jnp.bfloat16),
        ],
        cost_estimate=pl.CostEstimate(
            flops=40 * tokens * width * keys,
            transcendentals=QUERY_HEADS * tokens * keys,
            bytes_accessed=8 * tokens * width + 4 * key_value.size,
        ),
    )(block, query, grad, key_value, key_value)


def place_kernel(part_ref, held_ref, out_ref):
    del held_ref
    out_ref[0, 0] = part_ref[...].astype(jnp.float32)


def place_first_kernel(part_ref, out_ref):
    out_ref[0, 0] = part_ref[...].astype(jnp.float32)


def place(part, held, layer, experts):
    rows = part.shape[0]
    block = (rows, part.shape[1] // experts)
    in_specs = [pl.BlockSpec(block, lambda e: (0, e))]
    operands = [part]
    if held is not None:
        in_specs.append(pl.BlockSpec(memory_space=pl.ANY))
        operands.append(held)
    return pl.pallas_call(
        place_first_kernel if held is None else place_kernel,
        grid=(experts,),
        in_specs=in_specs,
        out_specs=pl.BlockSpec((1, 1) + block, lambda e: (layer, e, 0, 0)),
        out_shape=jax.ShapeDtypeStruct((LAYER_COUNT, experts) + block, jnp.float32),
        input_output_aliases={} if held is None else {1: 0},
    )(*operands)


def body(
    inputs,
    routes,
    cotangent,
    query_weight,
    key_projection_weight,
    value_projection_weight,
    output_weight,
    attention_gain,
    expert_gain,
    router_weight,
    gate_weight,
    up_weight,
    down_weight,
):
    sequences_per_device, block_length, model_width = inputs.shape
    token_total = sequences_per_device * block_length
    exp_dev = gate_weight.shape[1]
    groups = lax.axis_size("expert")
    expert_total = exp_dev * groups
    all_rows = token_total * groups
    query_width = query_weight.shape[2]
    key_width = key_projection_weight.shape[2]
    my_group = lax.axis_index("expert")
    positions = my_group * block_length + jnp.arange(block_length, dtype=jnp.int32)
    cosine_table, sine_table = rotary_tables(positions, HEAD_SIZE // 2)
    block_at = my_group.astype(jnp.int32).reshape(1)
    group_at = jnp.stack([my_group.astype(jnp.int32), jnp.int32(expert_total)])
    expert_ids = jnp.arange(expert_total, dtype=jnp.int32)
    small_width = -(-(expert_total + 2) // 128) * 128
    gate_width = -(-(2 * expert_total) // 128) * 128
    edges = (
        query_width,
        query_width + key_width,
        query_width + 2 * key_width,
        query_width + 2 * key_width + model_width,
        query_width + 2 * key_width + model_width + expert_total,
        query_width + 2 * key_width + model_width + expert_total + 1,
    )

    def pack_attention(query_part, key_part, value_part, output_part, router_part, one, two):
        rows = query_part.shape[0]
        fill = jnp.zeros((rows, small_width - expert_total - 2), query_part.dtype)
        return jnp.concatenate(
            [
                query_part,
                key_part,
                value_part,
                output_part,
                router_part,
                one[:, None],
                two[:, None],
                fill,
            ],
            axis=1,
        )

    chosen_hot = jnp.any(
        routes.reshape(LAYER_COUNT, token_total, -1)[:, :, :, None] == expert_ids, axis=2
    )
    chosen_all = gather_rows(
        jnp.moveaxis(chosen_hot, 0, 1).reshape(token_total, -1).astype(jnp.bfloat16)
    ).reshape(all_rows, LAYER_COUNT, expert_total)

    shards = [
        pack_attention(
            query_weight[layer],
            key_projection_weight[layer],
            value_projection_weight[layer],
            output_weight[layer].T,
            router_weight[layer],
            attention_gain[layer],
            expert_gain[layer],
        )
        for layer in range(LAYER_COUNT)
    ]
    packed = [lax.all_gather(shards[0], ("dp", "expert"), axis=0, tiled=True)]
    ff_width = gate_weight.shape[3]
    hidden_width = exp_dev * ff_width
    gathered = [
        tuple(
            lax.all_gather(rows.reshape(-1, hidden_width), "dp", axis=0, tiled=True)
            for rows in (
                gate_weight[layer].transpose(1, 0, 2),
                up_weight[layer].transpose(1, 0, 2),
                down_weight[layer].transpose(2, 0, 1),
            )
        )
        for layer in range(LAYER_COUNT)
    ]

    def shares_of(rows, router_full, hot):
        logits = jnp.dot(rows, router_full, preferred_element_type=jnp.float32)
        masked = jnp.where(hot, logits, -1e30)
        exps = jnp.where(hot, jnp.exp(masked - jnp.max(masked, axis=1, keepdims=True)), 0.0)
        return exps / jnp.sum(exps, axis=1, keepdims=True)

    def expert_rows(act, down):
        return dot_f32(act, down, (1,), (1,)).astype(jnp.bfloat16)

    def layer_forward(hidden, layer):
        full = packed[layer]
        qkv_full = full[:, : edges[2]]
        output_full = full[:, edges[2] : edges[3]]
        router_full = full[:, edges[3] : edges[4]]
        gain_one = full[:, edges[4]].astype(jnp.float32)
        gain_two = full[:, edges[5]].astype(jnp.float32)
        gate_full, up_full, down_full = gathered[layer]
        first_normalized, inv_one = norm_forward(hidden, gain_one)
        first_normalized = first_normalized.astype(jnp.bfloat16)
        linear = jnp.dot(first_normalized, qkv_full, preferred_element_type=jnp.float32)
        query_rotated = rotate_features(
            linear[:, : edges[0]].reshape(token_total, QUERY_HEADS, HEAD_SIZE),
            cosine_table,
            sine_table,
        ).astype(jnp.bfloat16)
        query_rotated = query_rotated.reshape(token_total, query_width)
        key_rot = rotate_features(
            linear[:, edges[0] : edges[1]].reshape(token_total, KEY_VALUE_HEADS, HEAD_SIZE),
            cosine_table,
            sine_table,
        ).astype(jnp.bfloat16)
        key_value = jnp.concatenate(
            [
                key_rot.reshape(token_total, key_width),
                linear[:, edges[1] :].astype(jnp.bfloat16),
            ],
            axis=1,
        )
        key_value_all = gather_rows(key_value)
        ahead = layer + 1 < LAYER_COUNT
        if ahead:
            key_value_all, next_shard = lax.optimization_barrier(
                (key_value_all, shards[layer + 1])
            )
            next_rows = gather_chips(next_shard)
        attended = attention_forward(block_at, query_rotated, key_value_all)
        middle = hidden + dot_f32(attended, output_full, (1,), (1,))
        normed_two, inv_two = norm_forward(middle, gain_two)
        normed_two = normed_two.astype(jnp.bfloat16)
        arrived = gather_rows(normed_two)
        if ahead:
            arrived, next_rows = lax.optimization_barrier((arrived, next_rows))
            next_rows = gather_groups(next_rows)
        share_all = shares_of(arrived, router_full, chosen_all[:, layer] > 0)
        share_own = shares_of(normed_two, router_full, chosen_hot[layer])
        share_local = lax.dynamic_slice_in_dim(share_all, my_group * exp_dev, exp_dev, axis=1)
        gate_low, up_low, scaled_act = expert_forward(
            arrived, gate_full, up_full, share_local
        )
        if ahead:
            scaled_act, next_rows = lax.optimization_barrier((scaled_act, next_rows))
            packed.append(join_cores(next_rows))
        kept_state = (
            hidden,
            inv_one,
            first_normalized,
            query_rotated,
            key_value_all,
            attended,
            middle,
            inv_two,
            normed_two,
            share_own,
            share_local,
            arrived,
            gate_low,
            up_low,
            scaled_act,
            qkv_full,
            output_full,
            gain_one,
            gain_two,
            router_full,
            gate_full,
            up_full,
            down_full,
        )
        return kept_state

    hidden = inputs.astype(jnp.float32).reshape(token_total, model_width)
    kept_states = []
    for layer in range(LAYER_COUNT):
        kept_state = layer_forward(hidden, layer)
        kept_states.append(kept_state)
        last_middle, last_act, last_down = kept_state[6], kept_state[14], kept_state[-1]
        if layer + 1 < LAYER_COUNT:
            hidden = last_middle + sum_rows(expert_rows(last_act, last_down))
    output = None
    grad_hidden = cotangent.astype(jnp.float32).reshape(token_total, model_width)
    attention_list = [None] * LAYER_COUNT
    waiting = None
    group_steps = near_first("expert", 1)
    far_steps = far_first("expert", 1)
    chip_steps = near_first("dp", 2)
    for layer in range(LAYER_COUNT - 1, -1, -1):
        (
            layer_hidden,
            inv_one,
            first_normalized,
            query_rotated,
            key_value_all,
            attended,
            middle,
            inv_two,
            normed_two,
            share_own,
            share_local,
            arrived,
            gate_low,
            up_low,
            scaled_act,
            qkv_full,
            output_full,
            gain_one,
            gain_two,
            router_full,
            gate_full,
            up_full,
            down_full,
        ) = kept_states[layer]
        grad_all = gather_rows(grad_hidden.astype(jnp.bfloat16))
        if waiting is not None:
            grad_all, waiting = lax.optimization_barrier((grad_all, waiting))
            out_part, query_part, kv_part = waiting
            out_part = halve_all(out_part, group_steps[1:])
            query_part = halve_all(query_part, group_steps[:1])
            kv_part = halve_all(kv_part, group_steps[:1])
        grad_down = dot_f32(grad_all, scaled_act, (0,), (0,)).astype(jnp.bfloat16)
        grad_all, grad_down = lax.optimization_barrier((grad_all, grad_down))
        expert_parts = [lax.psum_scatter(grad_down, "dp", scatter_dimension=0, tiled=True)]
        grad_gate_val, grad_up_val, grad_rows = expert_backward(
            group_at,
            grad_all,
            down_full,
            gate_full,
            up_full,
            gate_low,
            up_low,
            share_local,
            gate_width,
        )
        grad_gate_w = dot_f32(arrived, grad_gate_val, (0,), (0,)).astype(jnp.bfloat16)
        grad_up_w = dot_f32(arrived, grad_up_val, (0,), (0,)).astype(jnp.bfloat16)
        back = sum_rows(grad_rows)
        if waiting is None:
            last_rows = expert_rows(last_act, last_down)
            back, last_rows = lax.optimization_barrier((back, last_rows))
            output = last_middle + sum_rows(last_rows)
        else:
            back, out_part, query_part, kv_part = lax.optimization_barrier(
                (back, out_part, query_part, kv_part)
            )
            late_part = jnp.concatenate([query_part, kv_part], axis=1)
            late_part = halve_all(late_part, group_steps[1:])
        back, grad_gate_w, grad_up_w = lax.optimization_barrier((back, grad_gate_w, grad_up_w))
        expert_parts += [
            lax.psum_scatter(grad_gate_w, "dp", scatter_dimension=0, tiled=True),
            lax.psum_scatter(grad_up_w, "dp", scatter_dimension=0, tiled=True),
        ]
        grad_gates_own = (
            back[:, model_width : model_width + expert_total]
            + back[:, model_width + expert_total : model_width + 2 * expert_total]
        )
        grad_logits = (
            share_own
            * (grad_gates_own - jnp.sum(share_own * grad_gates_own, axis=-1, keepdims=True))
        ).astype(jnp.bfloat16)
        grad_router = dot_f32(normed_two, grad_logits, (0,), (0,))
        grad_normed_two = back[:, :model_width] + dot_f32(grad_logits, router_full, (1,), (1,))
        grad_norm_mid, grad_gain_two = norm_backward(middle, inv_two, gain_two, grad_normed_two)
        grad_middle = grad_hidden + grad_norm_mid
        grad_branch = grad_middle.astype(jnp.bfloat16)
        grad_output_w = dot_f32(core_major(grad_branch), both_cores(attended), (0,), (0,))
        grad_output_w = halve_all(grad_output_w.astype(jnp.bfloat16), group_steps[:1])
        grad_attended = dot_f32(grad_branch, output_full, (1,), (0,)).astype(jnp.bfloat16)
        if waiting is not None:
            grad_attended, late_part = lax.optimization_barrier((grad_attended, late_part))
            chip_part = jnp.concatenate([out_part, late_part], axis=1)
            chip_part = halve_all(chip_part, chip_steps[:1])
        grad_query, grad_key_value_all = attention_backward(
            block_at, query_rotated, grad_attended, key_value_all
        )
        if waiting is None:
            grad_query, grad_key_value_all, output = lax.optimization_barrier(
                (grad_query, grad_key_value_all, output)
            )
        else:
            grad_query, grad_output_w, chip_part = lax.optimization_barrier(
                (grad_query, grad_output_w, chip_part)
            )
            grad_output_w = halve_all(grad_output_w, group_steps[1:])
            chip_part = halve_all(chip_part, chip_steps[1:])
        grad_kv = sum_rows(grad_key_value_all)
        normed_split = core_major(first_normalized)
        grad_query_lin = (
            rotate_features(
                grad_query.reshape(token_total, QUERY_HEADS, HEAD_SIZE), cosine_table, -sine_table
            )
            .astype(jnp.bfloat16)
            .reshape(token_total, query_width)
        )
        grad_query_w = dot_f32(normed_split, both_cores(grad_query_lin), (0,), (0,))
        grad_query_w = grad_query_w.astype(jnp.bfloat16)
        if layer == 0:
            grad_kv, grad_query_w, chip_part = lax.optimization_barrier(
                (grad_kv, grad_query_w, chip_part)
            )
            attention_list[layer + 1] = chip_part
            grad_query_w = halve_all(grad_query_w, far_steps[:1])
        grad_kv = grad_kv.reshape(token_total, -1, 2, 2 * HEAD_SIZE)
        grad_kv = grad_kv.transpose(0, 2, 1, 3).reshape(token_total, 2 * key_width)
        grad_key_lin = (
            rotate_features(
                grad_kv[:, :key_width].reshape(token_total, KEY_VALUE_HEADS, HEAD_SIZE),
                cosine_table,
                -sine_table,
            )
            .astype(jnp.bfloat16)
            .reshape(token_total, key_width)
        )
        grad_kv_lin = jnp.concatenate(
            [grad_key_lin, grad_kv[:, key_width:].astype(jnp.bfloat16)], axis=1
        )
        grad_kv_w = dot_f32(normed_split, both_cores(grad_kv_lin), (0,), (0,))
        grad_normed_one = dot_f32(grad_query_lin, qkv_full[:, : edges[0]], (1,), (1,)) + dot_f32(
            grad_kv_lin, qkv_full[:, edges[0] :], (1,), (1,)
        )
        grad_norm_in, grad_gain_one = norm_backward(
            layer_hidden, inv_one, gain_one, grad_normed_one
        )
        fill = jnp.zeros((model_width, small_width - expert_total - 2), jnp.bfloat16)
        small_part = jnp.concatenate(
            [
                grad_router.astype(jnp.bfloat16),
                grad_gain_one[:, None].astype(jnp.bfloat16),
                grad_gain_two[:, None].astype(jnp.bfloat16),
                fill,
            ],
            axis=1,
        )
        small_split = core_major(small_part.T).reshape(2, small_width, -1)
        small_half = jnp.sum(small_split.astype(jnp.float32), axis=0).T
        grad_kv_w = jnp.concatenate([grad_kv_w, small_half], axis=1).astype(jnp.bfloat16)
        if layer > 0:
            waiting = (grad_output_w, grad_query_w, grad_kv_w)
        else:
            grad_kv_w, last_parts = lax.optimization_barrier((grad_kv_w, last_parts))
            expert_held = [place(part, None, layer + 1, exp_dev) for part in last_parts]
            grad_kv_w = halve_all(grad_kv_w, group_steps[:1])
            grad_kv_w, expert_held = lax.optimization_barrier((grad_kv_w, expert_held))
            late_part = jnp.concatenate(
                [
                    halve_all(grad_query_w, far_steps[1:]),
                    halve_all(grad_kv_w, group_steps[1:]),
                ],
                axis=1,
            )
            attention_list[layer] = jnp.concatenate(
                [halve_all(grad_output_w, chip_steps), halve_all(late_part, chip_steps)], axis=1
            )
        last_parts = expert_parts
        grad_hidden = grad_middle + grad_norm_in
    stacked = jnp.stack(attention_list).astype(jnp.float32)
    cuts = [query_width, query_width, key_width, key_width, expert_total, 1, 1]
    cuts = [sum(cuts[:index]) for index in range(len(cuts) + 1)]
    output_grads, query_grads, key_grads, value_grads, router_grads, one, two = (
        stacked[:, :, start:stop] for start, stop in zip(cuts[:-1], cuts[1:])
    )
    expert_held = [
        place(part, held, 0, exp_dev) for part, held in zip(last_parts, expert_held)
    ]
    down_grads, gate_grads, up_grads = expert_held
    return (
        output.astype(jnp.bfloat16).reshape(sequences_per_device, block_length, model_width),
        grad_hidden.reshape(sequences_per_device, block_length, model_width),
        query_grads,
        key_grads,
        value_grads,
        jnp.swapaxes(output_grads, 1, 2),
        one[:, :, 0],
        two[:, :, 0],
        router_grads,
        gate_grads,
        up_grads,
        jnp.swapaxes(down_grads, 2, 3),
    )


def solution(mesh):
    in_specs = (
        P("dp", "expert", None),
        P(None, "expert", "dp", None, None),
        P("dp", "expert", None),
        P(None, ("dp", "expert"), None),
        P(None, ("dp", "expert"), None),
        P(None, ("dp", "expert"), None),
        P(None, None, ("dp", "expert")),
        P(None, ("dp", "expert")),
        P(None, ("dp", "expert")),
        P(None, ("dp", "expert"), None),
        P(None, "expert", "dp", None),
        P(None, "expert", "dp", None),
        P(None, "expert", None, "dp"),
    )
    out_specs = (
        P("dp", "expert", None),
        P("dp", "expert", None),
        P(None, ("dp", "expert"), None),
        P(None, ("dp", "expert"), None),
        P(None, ("dp", "expert"), None),
        P(None, None, ("dp", "expert")),
        P(None, ("dp", "expert")),
        P(None, ("dp", "expert")),
        P(None, ("dp", "expert"), None),
        P(None, "expert", "dp", None),
        P(None, "expert", "dp", None),
        P(None, "expert", None, "dp"),
    )
    return jax.shard_map(body, mesh=mesh, in_specs=in_specs, out_specs=out_specs, check_vma=False)
```

```python
import math

import jax
import jax.numpy as jnp
from jax import lax
from jax.experimental import pallas as pl
from jax.experimental.pallas import tpu as pltpu
from jax.sharding import PartitionSpec as P

QUERY_HEADS = 24
KEY_VALUE_HEADS = 8
HEAD_SIZE = 64
LAYER_COUNT = 2


eps_norm = 1e-06
highest_precision = lax.Precision.HIGHEST


def rotary_tables(positions, half_dim):
    frequency = jnp.exp(-math.log(10000.0) * jnp.arange(half_dim, dtype=jnp.float32) / half_dim)
    angles = positions.astype(jnp.float32)[:, None] * frequency[None, :]
    return (jnp.cos(angles), jnp.sin(angles))


def rotate_features(values, cosine_table, sine_table):
    half_dim = values.shape[-1] // 2
    first_half = values[..., :half_dim]
    second_half = values[..., half_dim:]
    cos_part = cosine_table[:, None, :]
    sin_part = sine_table[:, None, :]
    return jnp.concatenate(
        [
            first_half * cos_part - second_half * sin_part,
            second_half * cos_part + first_half * sin_part,
        ],
        axis=-1,
    )


def norm_forward(values, gain_vec):
    inv_rms = lax.rsqrt(jnp.mean(values * values, axis=-1, keepdims=True) + eps_norm)
    return (values * inv_rms * gain_vec, inv_rms)


def norm_backward(values, inv_rms, gain_vec, upstream):
    scaled = upstream * gain_vec
    grad_gain = jnp.sum(upstream * values * inv_rms, axis=0)
    grad_values = inv_rms * (
        scaled - values * inv_rms * inv_rms * jnp.mean(scaled * values, axis=-1, keepdims=True)
    )
    return (grad_values, grad_gain)


def stack_member(layer_list, member):
    return jnp.stack([layer_parts[member] for layer_parts in layer_list], axis=0)


def exchange(blocks):
    return lax.all_to_all(blocks, "expert", split_axis=0, concat_axis=0, tiled=True)


def gather_rows(rows):
    groups = lax.axis_size("expert")
    blocks = exchange(jnp.broadcast_to(rows[None], (groups,) + rows.shape))
    return blocks.reshape((groups * rows.shape[0],) + rows.shape[1:])


def sum_rows(partial_rows):
    groups = lax.axis_size("expert")
    blocks = partial_rows.reshape((groups, -1) + partial_rows.shape[1:])
    return jnp.sum(exchange(blocks).astype(jnp.float32), axis=0)


def same_core():
    members = range(lax.axis_size("dp"))
    return [[i for i in members if i % 2 == core] for core in range(2)]


def swap_cores(values):
    return lax.ppermute(values, "dp", [(i, i ^ 1) for i in range(lax.axis_size("dp"))])


def exchange_chips(blocks):
    return lax.all_to_all(
        blocks, "dp", split_axis=0, concat_axis=0, axis_index_groups=same_core(), tiled=True
    )


def gather_chips(shard):
    chips = lax.axis_size("dp") // 2
    return exchange_chips(jnp.broadcast_to(shard[None], (chips,) + shard.shape))


def gather_groups(chip_rows):
    groups = lax.axis_size("expert")
    return exchange(jnp.broadcast_to(chip_rows[None], (groups,) + chip_rows.shape))


def join_cores(own):
    width = own.shape[-1]
    other = swap_cores(own)
    first = lax.axis_index("dp") % 2 == 0
    both = jnp.stack([jnp.where(first, own, other), jnp.where(first, other, own)])
    return both.transpose(2, 0, 1, 3, 4).reshape(-1, width)


def core_major(columns):
    chips = lax.axis_size("dp") // 2
    groups = lax.axis_size("expert")
    split = columns.reshape(columns.shape[0], chips, 2, groups, -1)
    halves = split.transpose(2, 0, 3, 1, 4).reshape(2, columns.shape[0], -1)
    core = lax.axis_index("dp") % 2
    mine = lax.dynamic_index_in_dim(halves, core, 0, keepdims=False)
    theirs = lax.dynamic_index_in_dim(halves, 1 - core, 0, keepdims=False)
    return jnp.concatenate([mine, swap_cores(theirs)], axis=0)


def both_cores(rows):
    return jnp.concatenate([rows, swap_cores(rows)], axis=0)


def halve(partial, axis_name, step, outer):
    size = lax.axis_size(axis_name)
    width = partial.shape[-1]
    blocks = partial.reshape(outer, 2, -1, width)
    side = (lax.axis_index(axis_name) // step) % 2
    mine = lax.dynamic_index_in_dim(blocks, side, 1, keepdims=False)
    theirs = lax.dynamic_index_in_dim(blocks, 1 - side, 1, keepdims=False)
    arrived = lax.ppermute(
        theirs.reshape(-1, width), axis_name, [(i, i ^ step) for i in range(size)]
    )
    total = mine.reshape(-1, width).astype(jnp.float32) + arrived.astype(jnp.float32)
    return total.astype(jnp.bfloat16)


def near_first(axis_name, least):
    size = lax.axis_size(axis_name)
    steps = [least]
    while 2 * steps[-1] < size:
        steps.append(2 * steps[-1])
    return [(axis_name, step, size // (2 * step)) for step in steps]


def far_first(axis_name, least):
    return [(axis_name, step, 1) for _, step, _ in reversed(near_first(axis_name, least))]


def halve_all(partial, steps):
    for step in steps:
        partial = halve(partial, *step)
    return partial


def dot_f32(left, right, left_dims, right_dims):
    return lax.dot_general(
        left, right, ((left_dims, right_dims), ((), ())), preferred_element_type=jnp.float32
    )


def contract(left, right, left_dim, right_dim):
    return lax.dot_general(
        left,
        right,
        (((left_dim,), (right_dim,)), ((), ())),
        preferred_element_type=jnp.float32,
    )


def pick_column(table, column):
    lanes = lax.broadcasted_iota(jnp.int32, table.shape, 1)
    return jnp.sum(jnp.where(lanes == column, table, 0.0), axis=1, keepdims=True)


def expert_forward_kernel(rows_ref, gate_ref, up_ref, share_ref, gate_out, up_out, act_out):
    rows = rows_ref[...]
    gate_val = contract(rows, gate_ref[...], 1, 0)
    up_val = contract(rows, up_ref[...], 1, 0)
    share = pick_column(share_ref[...], pl.program_id(0))
    gate_out[...] = gate_val.astype(jnp.bfloat16)
    up_out[...] = up_val.astype(jnp.bfloat16)
    act_out[...] = (gate_val * jax.nn.sigmoid(gate_val) * up_val * share).astype(jnp.bfloat16)


def expert_forward(rows, gate_up, share):
    row_total, width = rows.shape
    experts = share.shape[1]
    hidden_total = gate_up.shape[1] // 2
    hidden = hidden_total // experts
    tile = row_total // 2
    row_block = pl.BlockSpec((tile, width), lambda e, r: (r, 0))
    weight_block = pl.BlockSpec((width, hidden), lambda e, r: (0, e))
    hidden_block = pl.BlockSpec((tile, hidden), lambda e, r: (r, e))
    return pl.pallas_call(
        expert_forward_kernel,
        grid=(experts, 2),
        in_specs=[
            row_block,
            weight_block,
            pl.BlockSpec((width, hidden), lambda e, r: (0, experts + e)),
            pl.BlockSpec((tile, experts), lambda e, r: (r, 0)),
        ],
        out_specs=[hidden_block] * 3,
        out_shape=[jax.ShapeDtypeStruct((row_total, hidden_total), jnp.bfloat16)] * 3,
        cost_estimate=pl.CostEstimate(
            flops=4 * row_total * width * hidden_total,
            transcendentals=row_total * hidden_total,
            bytes_accessed=4 * width * hidden_total + 6 * row_total * hidden_total,
        ),
    )(rows, gate_up, gate_up, share)


def expert_backward_kernel(
    group_ref,
    grad_ref,
    down_ref,
    gate_ref,
    up_ref,
    gate_val_ref,
    up_val_ref,
    share_ref,
    grad_gate_out,
    grad_up_out,
    rows_out,
    rows_acc,
    sums_acc,
):
    expert = pl.program_id(0)
    tile, width = grad_ref.shape
    experts = pl.num_programs(0)
    window = pl.ds(pl.multiple_of(pl.program_id(1) * tile, tile), tile)
    grad_scaled = contract(grad_ref[...], down_ref[...], 1, 0)
    gate_val = gate_val_ref[...].astype(jnp.float32)
    up_val = up_val_ref[...].astype(jnp.float32)
    sigmoid_val = jax.nn.sigmoid(gate_val)
    silu_val = gate_val * sigmoid_val
    grad_sum = jnp.sum(grad_scaled * silu_val * up_val, axis=1, keepdims=True)
    grad_inner = grad_scaled * pick_column(share_ref[...], expert)
    grad_gate = (
        grad_inner * up_val * sigmoid_val * (1.0 + gate_val * (1.0 - sigmoid_val))
    ).astype(jnp.bfloat16)
    grad_up = (grad_inner * silu_val).astype(jnp.bfloat16)
    grad_gate_out[...] = grad_gate
    grad_up_out[...] = grad_up
    grad_rows = contract(grad_gate, gate_ref[...], 1, 1) + contract(
        grad_up, up_ref[...], 1, 1
    )
    lanes = lax.broadcasted_iota(jnp.int32, (tile, sums_acc.shape[1]), 1)
    sum_high = grad_sum.astype(jnp.bfloat16).astype(jnp.float32)
    column = group_ref[0] * experts + expert
    grad_sums = jnp.where(lanes == column, sum_high, 0.0) + jnp.where(
        lanes == column + group_ref[1], grad_sum - sum_high, 0.0
    )

    @pl.when(expert == 0)
    def _():
        rows_acc[window, :] = grad_rows
        sums_acc[window, :] = grad_sums

    @pl.when(expert > 0)
    def _():
        rows_acc[window, :] += grad_rows
        sums_acc[window, :] += grad_sums

    @pl.when(expert == pl.num_programs(0) - 1)
    def _():
        rows_out[:, :width] = rows_acc[window, :].astype(jnp.bfloat16)
        rows_out[:, width:] = sums_acc[window, :].astype(jnp.bfloat16)


def expert_backward(group, grad, down, gate_up, gate_val, up_val, share, extra):
    row_total, width = grad.shape
    experts = share.shape[1]
    hidden_total = gate_up.shape[1] // 2
    hidden = hidden_total // experts
    tile = row_total // 2
    row_block = pl.BlockSpec((tile, width), lambda e, r, g: (r, 0))
    weight_block = pl.BlockSpec((width, hidden), lambda e, r, g: (0, e))
    hidden_block = pl.BlockSpec((tile, hidden), lambda e, r, g: (r, e))
    hidden_shape = jax.ShapeDtypeStruct((row_total, hidden_total), jnp.bfloat16)
    return pl.pallas_call(
        expert_backward_kernel,
        grid_spec=pltpu.PrefetchScalarGridSpec(
            num_scalar_prefetch=1,
            grid=(experts, 2),
            in_specs=[
                row_block,
                weight_block,
                weight_block,
                pl.BlockSpec((width, hidden), lambda e, r, g: (0, experts + e)),
                hidden_block,
                hidden_block,
                pl.BlockSpec((tile, experts), lambda e, r, g: (r, 0)),
            ],
            out_specs=[
                hidden_block,
                hidden_block,
                pl.BlockSpec(
                    (tile, width + extra),
                    lambda e, r, g: (jnp.where(e == experts - 1, r, 0), 0),
                ),
            ],
            scratch_shapes=[
                pltpu.VMEM((row_total, width), jnp.float32),
                pltpu.VMEM((row_total, extra), jnp.float32),
            ],
        ),
        out_shape=[
            hidden_shape,
            hidden_shape,
            jax.ShapeDtypeStruct((row_total, width + extra), jnp.bfloat16),
        ],
        cost_estimate=pl.CostEstimate(
            flops=6 * row_total * width * hidden_total,
            transcendentals=row_total * hidden_total,
            bytes_accessed=6 * width * hidden_total + 8 * row_total * hidden_total,
        ),
    )(group, grad, down, gate_up, gate_up, gate_val, up_val, share)


def attention_probs(block_ref, query, key):
    scores = contract(key, query, 1, 1) * HEAD_SIZE ** (-0.5)
    key_at = lax.broadcasted_iota(jnp.int32, scores.shape, 0)
    query_at = lax.broadcasted_iota(jnp.int32, scores.shape, 1)
    offset = block_ref[0] * query.shape[0]
    masked = jnp.where(key_at <= query_at + offset, scores, -1e30)
    exp_scores = jnp.exp(masked - jnp.max(masked, axis=0, keepdims=True))
    return exp_scores / jnp.sum(exp_scores, axis=0, keepdims=True)


def head(values, index):
    return values[:, index * HEAD_SIZE : (index + 1) * HEAD_SIZE]


def attention_forward_kernel(block_ref, query_ref, key_ref, value_ref, out_ref):
    query, key, value = query_ref[...], key_ref[...], value_ref[...]
    group = QUERY_HEADS // KEY_VALUE_HEADS
    outs = []
    for index in range(2 * group):
        shared = index // group
        probs = attention_probs(block_ref, head(query, index), head(key, shared))
        outs.append(contract(head(value, shared), probs.astype(jnp.bfloat16), 0, 0))
    out_ref[...] = jnp.concatenate(outs, axis=0).T.astype(jnp.bfloat16)


def attention_specs(tokens, keys):
    pairs = KEY_VALUE_HEADS // 2
    query_block = pl.BlockSpec((tokens, QUERY_HEADS // pairs * HEAD_SIZE), lambda i, b: (0, i))
    key_block = pl.BlockSpec((keys, 2 * HEAD_SIZE), lambda i, b: (0, i))
    value_block = pl.BlockSpec((keys, 2 * HEAD_SIZE), lambda i, b: (0, i + pairs))
    return (pairs, query_block, key_block, value_block)


def attention_forward(block, query, key_value):
    tokens, width = query.shape
    keys = key_value.shape[0]
    pairs, query_block, key_block, value_block = attention_specs(tokens, keys)
    return pl.pallas_call(
        attention_forward_kernel,
        grid_spec=pltpu.PrefetchScalarGridSpec(
            num_scalar_prefetch=1,
            grid=(pairs,),
            in_specs=[query_block, key_block, value_block],
            out_specs=query_block,
        ),
        out_shape=jax.ShapeDtypeStruct((tokens, width), jnp.bfloat16),
        cost_estimate=pl.CostEstimate(
            flops=16 * tokens * width * keys,
            transcendentals=QUERY_HEADS * tokens * keys,
            bytes_accessed=4 * tokens * width + 2 * key_value.size,
        ),
    )(block, query, key_value, key_value)


def attention_backward_kernel(
    block_ref, query_ref, grad_ref, key_ref, value_ref, grad_query_out, grad_key_value_out
):
    query, grad, key, value = query_ref[...], grad_ref[...], key_ref[...], value_ref[...]
    group = QUERY_HEADS // KEY_VALUE_HEADS
    scale = HEAD_SIZE ** (-0.5)
    grad_queries, grad_keys, grad_values = [], [], []
    for shared in range(2):
        grad_key, grad_value = 0.0, 0.0
        for index in range(shared * group, (shared + 1) * group):
            query_one, grad_one = head(query, index), head(grad, index)
            probs = attention_probs(block_ref, query_one, head(key, shared))
            grad_probs = contract(head(value, shared), grad_one, 1, 1)
            centre = jnp.sum(probs * grad_probs, axis=0, keepdims=True)
            grad_scores = (probs * (grad_probs - centre)).astype(jnp.bfloat16)
            grad_queries.append(contract(head(key, shared), grad_scores, 0, 0) * scale)
            grad_key += contract(grad_scores, query_one, 1, 0)
            grad_value += contract(probs.astype(jnp.bfloat16), grad_one, 1, 0)
        grad_keys.append(grad_key * scale)
        grad_values.append(grad_value)
    grad_query_out[...] = jnp.concatenate(grad_queries, axis=0).T
    grad_key_value_out[...] = jnp.concatenate(grad_keys + grad_values, axis=1).astype(
        jnp.bfloat16
    )


def attention_backward(block, query, grad, key_value):
    tokens, width = query.shape
    keys = key_value.shape[0]
    pairs, query_block, key_block, value_block = attention_specs(tokens, keys)
    return pl.pallas_call(
        attention_backward_kernel,
        grid_spec=pltpu.PrefetchScalarGridSpec(
            num_scalar_prefetch=1,
            grid=(pairs,),
            in_specs=[query_block, query_block, key_block, value_block],
            out_specs=[
                query_block,
                pl.BlockSpec((keys, 4 * HEAD_SIZE), lambda i, b: (0, i)),
            ],
        ),
        out_shape=[
            jax.ShapeDtypeStruct((tokens, width), jnp.float32),
            jax.ShapeDtypeStruct(key_value.shape, jnp.bfloat16),
        ],
        cost_estimate=pl.CostEstimate(
            flops=40 * tokens * width * keys,
            transcendentals=QUERY_HEADS * tokens * keys,
            bytes_accessed=8 * tokens * width + 4 * key_value.size,
        ),
    )(block, query, grad, key_value, key_value)


def place_kernel(part_ref, held_ref, out_ref):
    del held_ref
    out_ref[0, 0] = part_ref[...].astype(jnp.float32)


def place_first_kernel(part_ref, out_ref):
    out_ref[0, 0] = part_ref[...].astype(jnp.float32)


def place(part, held, layer, experts):
    rows = part.shape[0]
    block = (rows, part.shape[1] // experts)
    in_specs = [pl.BlockSpec(block, lambda e: (0, e))]
    operands = [part]
    if held is not None:
        in_specs.append(pl.BlockSpec(memory_space=pl.ANY))
        operands.append(held)
    return pl.pallas_call(
        place_first_kernel if held is None else place_kernel,
        grid=(experts,),
        in_specs=in_specs,
        out_specs=pl.BlockSpec((1, 1) + block, lambda e: (layer, e, 0, 0)),
        out_shape=jax.ShapeDtypeStruct((LAYER_COUNT, experts) + block, jnp.float32),
        input_output_aliases={} if held is None else {1: 0},
    )(*operands)


def body(
    inputs,
    routes,
    cotangent,
    query_weight,
    key_projection_weight,
    value_projection_weight,
    output_weight,
    attention_gain,
    expert_gain,
    router_weight,
    gate_weight,
    up_weight,
    down_weight,
):
    sequences_per_device, block_length, model_width = inputs.shape
    token_total = sequences_per_device * block_length
    exp_dev = gate_weight.shape[1]
    groups = lax.axis_size("expert")
    expert_total = exp_dev * groups
    all_rows = token_total * groups
    query_width = query_weight.shape[2]
    key_width = key_projection_weight.shape[2]
    my_group = lax.axis_index("expert")
    positions = my_group * block_length + jnp.arange(block_length, dtype=jnp.int32)
    cosine_table, sine_table = rotary_tables(positions, HEAD_SIZE // 2)
    block_at = my_group.astype(jnp.int32).reshape(1)
    group_at = jnp.stack([my_group.astype(jnp.int32), jnp.int32(expert_total)])
    expert_ids = jnp.arange(expert_total, dtype=jnp.int32)
    small_width = -(-(expert_total + 2) // 128) * 128
    gate_width = -(-(2 * expert_total) // 128) * 128
    edges = (
        query_width,
        query_width + key_width,
        query_width + 2 * key_width,
        query_width + 2 * key_width + model_width,
        query_width + 2 * key_width + model_width + expert_total,
        query_width + 2 * key_width + model_width + expert_total + 1,
    )

    def pack_attention(query_part, key_part, value_part, output_part, router_part, one, two):
        rows = query_part.shape[0]
        fill = jnp.zeros((rows, small_width - expert_total - 2), query_part.dtype)
        return jnp.concatenate(
            [
                query_part,
                key_part,
                value_part,
                output_part,
                router_part,
                one[:, None],
                two[:, None],
                fill,
            ],
            axis=1,
        )

    chosen_hot = jnp.any(
        routes.reshape(LAYER_COUNT, token_total, -1)[:, :, :, None] == expert_ids, axis=2
    )
    chosen_all = gather_rows(
        jnp.moveaxis(chosen_hot, 0, 1).reshape(token_total, -1).astype(jnp.bfloat16)
    ).reshape(all_rows, LAYER_COUNT, expert_total)

    shards = [
        pack_attention(
            query_weight[layer],
            key_projection_weight[layer],
            value_projection_weight[layer],
            output_weight[layer].T,
            router_weight[layer],
            attention_gain[layer],
            expert_gain[layer],
        )
        for layer in range(LAYER_COUNT)
    ]
    packed = [lax.all_gather(shards[0], ("dp", "expert"), axis=0, tiled=True)]
    chip_rows = [None] + [gather_chips(shard) for shard in shards[1:]]
    inputs, chip_rows = lax.optimization_barrier((inputs, chip_rows))
    ff_width = gate_weight.shape[3]
    hidden_width = exp_dev * ff_width
    def gather_weights(*weights):
        rows = [weight.reshape(weight.shape[0], hidden_width) for weight in weights]
        return lax.all_gather(jnp.concatenate(rows, axis=1), "dp", axis=0, tiled=True)

    gathered = [
        (
            gather_weights(
                gate_weight[layer].transpose(1, 0, 2), up_weight[layer].transpose(1, 0, 2)
            ),
            gather_weights(down_weight[layer].transpose(2, 0, 1)),
        )
        for layer in range(LAYER_COUNT)
    ]

    def shares_of(rows, router_full, hot):
        logits = jnp.dot(rows, router_full, preferred_element_type=jnp.float32)
        masked = jnp.where(hot, logits, -1e30)
        exps = jnp.where(hot, jnp.exp(masked - jnp.max(masked, axis=1, keepdims=True)), 0.0)
        return exps / jnp.sum(exps, axis=1, keepdims=True)

    def expert_rows(act, down):
        return dot_f32(act, down, (1,), (1,)).astype(jnp.bfloat16)

    def layer_forward(hidden, layer):
        full = packed[layer]
        qkv_full = full[:, : edges[2]]
        output_full = full[:, edges[2] : edges[3]]
        router_full = full[:, edges[3] : edges[4]]
        gain_one = full[:, edges[4]].astype(jnp.float32)
        gain_two = full[:, edges[5]].astype(jnp.float32)
        gate_up_full, down_full = gathered[layer]
        first_normalized, inv_one = norm_forward(hidden, gain_one)
        first_normalized = first_normalized.astype(jnp.bfloat16)
        linear = jnp.dot(first_normalized, qkv_full, preferred_element_type=jnp.float32)
        query_rotated = rotate_features(
            linear[:, : edges[0]].reshape(token_total, QUERY_HEADS, HEAD_SIZE),
            cosine_table,
            sine_table,
        ).astype(jnp.bfloat16)
        query_rotated = query_rotated.reshape(token_total, query_width)
        key_rot = rotate_features(
            linear[:, edges[0] : edges[1]].reshape(token_total, KEY_VALUE_HEADS, HEAD_SIZE),
            cosine_table,
            sine_table,
        ).astype(jnp.bfloat16)
        key_value = jnp.concatenate(
            [
                key_rot.reshape(token_total, key_width),
                linear[:, edges[1] :].astype(jnp.bfloat16),
            ],
            axis=1,
        )
        key_value_all = gather_rows(key_value)
        ahead = layer + 1 < LAYER_COUNT
        attended = attention_forward(block_at, query_rotated, key_value_all)
        middle = hidden + dot_f32(attended, output_full, (1,), (1,))
        normed_two, inv_two = norm_forward(middle, gain_two)
        normed_two = normed_two.astype(jnp.bfloat16)
        arrived = gather_rows(normed_two)
        if ahead:
            arrived, next_rows = lax.optimization_barrier((arrived, chip_rows[layer + 1]))
            next_rows = gather_groups(next_rows)
        share_all = shares_of(arrived, router_full, chosen_all[:, layer] > 0)
        share_own = shares_of(normed_two, router_full, chosen_hot[layer])
        share_local = lax.dynamic_slice_in_dim(share_all, my_group * exp_dev, exp_dev, axis=1)
        gate_low, up_low, scaled_act = expert_forward(
            arrived, gate_up_full, share_local
        )
        if ahead:
            scaled_act, next_rows = lax.optimization_barrier((scaled_act, next_rows))
            packed.append(join_cores(next_rows))
        kept_state = (
            hidden,
            inv_one,
            first_normalized,
            query_rotated,
            key_value_all,
            attended,
            middle,
            inv_two,
            normed_two,
            share_own,
            share_local,
            arrived,
            gate_low,
            up_low,
            scaled_act,
            qkv_full,
            output_full,
            gain_one,
            gain_two,
            router_full,
            gate_up_full,
            down_full,
        )
        return kept_state

    hidden = inputs.astype(jnp.float32).reshape(token_total, model_width)
    kept_states = []
    for layer in range(LAYER_COUNT):
        kept_state = layer_forward(hidden, layer)
        kept_states.append(kept_state)
        last_middle, last_act, last_down = kept_state[6], kept_state[14], kept_state[-1]
        if layer + 1 < LAYER_COUNT:
            hidden = last_middle + sum_rows(expert_rows(last_act, last_down))
    output = None
    grad_hidden = cotangent.astype(jnp.float32).reshape(token_total, model_width)
    attention_list = [None] * LAYER_COUNT
    waiting = None
    group_steps = near_first("expert", 1)
    far_steps = far_first("expert", 1)
    chip_steps = near_first("dp", 2)
    for layer in range(LAYER_COUNT - 1, -1, -1):
        (
            layer_hidden,
            inv_one,
            first_normalized,
            query_rotated,
            key_value_all,
            attended,
            middle,
            inv_two,
            normed_two,
            share_own,
            share_local,
            arrived,
            gate_low,
            up_low,
            scaled_act,
            qkv_full,
            output_full,
            gain_one,
            gain_two,
            router_full,
            gate_up_full,
            down_full,
        ) = kept_states[layer]
        grad_all = gather_rows(grad_hidden.astype(jnp.bfloat16))
        if waiting is not None:
            grad_all, waiting = lax.optimization_barrier((grad_all, waiting))
            out_part, query_part, kv_part = waiting
            out_part = halve_all(out_part, group_steps[1:])
            query_part = halve_all(query_part, group_steps[:1])
            kv_part = halve_all(kv_part, group_steps[:1])
        grad_down = dot_f32(grad_all, scaled_act, (0,), (0,)).astype(jnp.bfloat16)
        grad_all, grad_down = lax.optimization_barrier((grad_all, grad_down))
        expert_parts = [lax.psum_scatter(grad_down, "dp", scatter_dimension=0, tiled=True)]
        grad_gate_val, grad_up_val, grad_rows = expert_backward(
            group_at,
            grad_all,
            down_full,
            gate_up_full,
            gate_low,
            up_low,
            share_local,
            gate_width,
        )
        grad_gate_w = dot_f32(arrived, grad_gate_val, (0,), (0,)).astype(jnp.bfloat16)
        grad_up_w = dot_f32(arrived, grad_up_val, (0,), (0,)).astype(jnp.bfloat16)
        back = sum_rows(grad_rows)
        if waiting is None:
            last_rows = expert_rows(last_act, last_down)
            back, last_rows = lax.optimization_barrier((back, last_rows))
            output = last_middle + sum_rows(last_rows)
        else:
            back, out_part, query_part, kv_part = lax.optimization_barrier(
                (back, out_part, query_part, kv_part)
            )
            late_part = jnp.concatenate([query_part, kv_part], axis=1)
            late_part = halve_all(late_part, group_steps[1:])
        back, grad_gate_w, grad_up_w = lax.optimization_barrier((back, grad_gate_w, grad_up_w))
        expert_parts += [
            lax.psum_scatter(grad_gate_w, "dp", scatter_dimension=0, tiled=True),
            lax.psum_scatter(grad_up_w, "dp", scatter_dimension=0, tiled=True),
        ]
        grad_gates_own = (
            back[:, model_width : model_width + expert_total]
            + back[:, model_width + expert_total : model_width + 2 * expert_total]
        )
        grad_logits = (
            share_own
            * (grad_gates_own - jnp.sum(share_own * grad_gates_own, axis=-1, keepdims=True))
        ).astype(jnp.bfloat16)
        grad_router = dot_f32(normed_two, grad_logits, (0,), (0,))
        grad_normed_two = back[:, :model_width] + dot_f32(grad_logits, router_full, (1,), (1,))
        grad_norm_mid, grad_gain_two = norm_backward(middle, inv_two, gain_two, grad_normed_two)
        grad_middle = grad_hidden + grad_norm_mid
        grad_branch = grad_middle.astype(jnp.bfloat16)
        grad_output_w = dot_f32(core_major(grad_branch), both_cores(attended), (0,), (0,))
        grad_output_w = halve_all(grad_output_w.astype(jnp.bfloat16), group_steps[:1])
        grad_attended = dot_f32(grad_branch, output_full, (1,), (0,)).astype(jnp.bfloat16)
        if waiting is not None:
            grad_attended, late_part = lax.optimization_barrier((grad_attended, late_part))
            chip_part = jnp.concatenate([out_part, late_part], axis=1)
            chip_part = halve_all(chip_part, chip_steps[:1])
        grad_query, grad_key_value_all = attention_backward(
            block_at, query_rotated, grad_attended, key_value_all
        )
        if waiting is None:
            grad_query, grad_key_value_all, output = lax.optimization_barrier(
                (grad_query, grad_key_value_all, output)
            )
        else:
            grad_query, grad_output_w, chip_part = lax.optimization_barrier(
                (grad_query, grad_output_w, chip_part)
            )
            grad_output_w = halve_all(grad_output_w, group_steps[1:])
            chip_part = halve_all(chip_part, chip_steps[1:])
        grad_kv = sum_rows(grad_key_value_all)
        normed_split = core_major(first_normalized)
        grad_query_lin = (
            rotate_features(
                grad_query.reshape(token_total, QUERY_HEADS, HEAD_SIZE), cosine_table, -sine_table
            )
            .astype(jnp.bfloat16)
            .reshape(token_total, query_width)
        )
        grad_query_w = dot_f32(normed_split, both_cores(grad_query_lin), (0,), (0,))
        grad_query_w = grad_query_w.astype(jnp.bfloat16)
        if layer == 0:
            grad_kv, grad_query_w, chip_part = lax.optimization_barrier(
                (grad_kv, grad_query_w, chip_part)
            )
            attention_list[layer + 1] = chip_part
            grad_query_w = halve_all(grad_query_w, far_steps[:1])
        grad_kv = grad_kv.reshape(token_total, -1, 2, 2 * HEAD_SIZE)
        grad_kv = grad_kv.transpose(0, 2, 1, 3).reshape(token_total, 2 * key_width)
        grad_key_lin = (
            rotate_features(
                grad_kv[:, :key_width].reshape(token_total, KEY_VALUE_HEADS, HEAD_SIZE),
                cosine_table,
                -sine_table,
            )
            .astype(jnp.bfloat16)
            .reshape(token_total, key_width)
        )
        grad_kv_lin = jnp.concatenate(
            [grad_key_lin, grad_kv[:, key_width:].astype(jnp.bfloat16)], axis=1
        )
        grad_kv_w = dot_f32(normed_split, both_cores(grad_kv_lin), (0,), (0,))
        grad_normed_one = dot_f32(grad_query_lin, qkv_full[:, : edges[0]], (1,), (1,)) + dot_f32(
            grad_kv_lin, qkv_full[:, edges[0] :], (1,), (1,)
        )
        grad_norm_in, grad_gain_one = norm_backward(
            layer_hidden, inv_one, gain_one, grad_normed_one
        )
        fill = jnp.zeros((model_width, small_width - expert_total - 2), jnp.bfloat16)
        small_part = jnp.concatenate(
            [
                grad_router.astype(jnp.bfloat16),
                grad_gain_one[:, None].astype(jnp.bfloat16),
                grad_gain_two[:, None].astype(jnp.bfloat16),
                fill,
            ],
            axis=1,
        )
        small_split = core_major(small_part.T).reshape(2, small_width, -1)
        small_half = jnp.sum(small_split.astype(jnp.float32), axis=0).T
        grad_kv_w = jnp.concatenate([grad_kv_w, small_half], axis=1).astype(jnp.bfloat16)
        if layer > 0:
            waiting = (grad_output_w, grad_query_w, grad_kv_w)
        else:
            grad_kv_w, last_parts = lax.optimization_barrier((grad_kv_w, last_parts))
            expert_held = [place(part, None, layer + 1, exp_dev) for part in last_parts]
            grad_kv_w = halve_all(grad_kv_w, group_steps[:1])
            grad_kv_w, expert_held = lax.optimization_barrier((grad_kv_w, expert_held))
            late_part = jnp.concatenate(
                [
                    halve_all(grad_query_w, far_steps[1:]),
                    halve_all(grad_kv_w, group_steps[1:]),
                ],
                axis=1,
            )
            late_part = halve_all(late_part, chip_steps[:1])
            expert_held = [
                place(part, held, layer, exp_dev)
                for part, held in zip(expert_parts[:2], expert_held[:2])
            ] + expert_held[2:]
            late_part, expert_held = lax.optimization_barrier((late_part, expert_held))
            attention_list[layer] = jnp.concatenate(
                [
                    halve_all(grad_output_w, chip_steps),
                    halve_all(late_part, chip_steps[1:]),
                ],
                axis=1,
            )
        last_parts = expert_parts
        grad_hidden = grad_middle + grad_norm_in
    stacked = jnp.stack(attention_list).astype(jnp.float32)
    cuts = [query_width, query_width, key_width, key_width, expert_total, 1, 1]
    cuts = [sum(cuts[:index]) for index in range(len(cuts) + 1)]
    output_grads, query_grads, key_grads, value_grads, router_grads, one, two = (
        stacked[:, :, start:stop] for start, stop in zip(cuts[:-1], cuts[1:])
    )
    expert_held[2] = place(last_parts[2], expert_held[2], 0, exp_dev)
    down_grads, gate_grads, up_grads = expert_held
    return (
        output.astype(jnp.bfloat16).reshape(sequences_per_device, block_length, model_width),
        grad_hidden.reshape(sequences_per_device, block_length, model_width),
        query_grads,
        key_grads,
        value_grads,
        jnp.swapaxes(output_grads, 1, 2),
        one[:, :, 0],
        two[:, :, 0],
        router_grads,
        gate_grads,
        up_grads,
        jnp.swapaxes(down_grads, 2, 3),
    )


def solution(mesh):
    in_specs = (
        P("dp", "expert", None),
        P(None, "expert", "dp", None, None),
        P("dp", "expert", None),
        P(None, ("dp", "expert"), None),
        P(None, ("dp", "expert"), None),
        P(None, ("dp", "expert"), None),
        P(None, None, ("dp", "expert")),
        P(None, ("dp", "expert")),
        P(None, ("dp", "expert")),
        P(None, ("dp", "expert"), None),
        P(None, "expert", "dp", None),
        P(None, "expert", "dp", None),
        P(None, "expert", None, "dp"),
    )
    out_specs = (
        P("dp", "expert", None),
        P("dp", "expert", None),
        P(None, ("dp", "expert"), None),
        P(None, ("dp", "expert"), None),
        P(None, ("dp", "expert"), None),
        P(None, None, ("dp", "expert")),
        P(None, ("dp", "expert")),
        P(None, ("dp", "expert")),
        P(None, ("dp", "expert"), None),
        P(None, "expert", "dp", None),
        P(None, "expert", "dp", None),
        P(None, "expert", None, "dp"),
    )
    return jax.shard_map(body, mesh=mesh, in_specs=in_specs, out_specs=out_specs, check_vma=False)
```

```python
import math

import jax
import jax.numpy as jnp
from jax import lax
from jax.experimental import pallas as pl
from jax.experimental.pallas import tpu as pltpu
from jax.sharding import PartitionSpec as P

QUERY_HEADS = 24
KEY_VALUE_HEADS = 8
HEAD_SIZE = 64
LAYER_COUNT = 2


eps_norm = 1e-06
highest_precision = lax.Precision.HIGHEST


def rotary_tables(positions, half_dim):
    frequency = jnp.exp(-math.log(10000.0) * jnp.arange(half_dim, dtype=jnp.float32) / half_dim)
    angles = positions.astype(jnp.float32)[:, None] * frequency[None, :]
    return (jnp.cos(angles), jnp.sin(angles))


def rotate_features(values, cosine_table, sine_table):
    half_dim = values.shape[-1] // 2
    first_half = values[..., :half_dim]
    second_half = values[..., half_dim:]
    cos_part = cosine_table[:, None, :]
    sin_part = sine_table[:, None, :]
    return jnp.concatenate(
        [
            first_half * cos_part - second_half * sin_part,
            second_half * cos_part + first_half * sin_part,
        ],
        axis=-1,
    )


def norm_forward(values, gain_vec):
    inv_rms = lax.rsqrt(jnp.mean(values * values, axis=-1, keepdims=True) + eps_norm)
    return (values * inv_rms * gain_vec, inv_rms)


def norm_backward(values, inv_rms, gain_vec, upstream):
    scaled = upstream * gain_vec
    grad_gain = jnp.sum(upstream * values * inv_rms, axis=0)
    grad_values = inv_rms * (
        scaled - values * inv_rms * inv_rms * jnp.mean(scaled * values, axis=-1, keepdims=True)
    )
    return (grad_values, grad_gain)


def stack_member(layer_list, member):
    return jnp.stack([layer_parts[member] for layer_parts in layer_list], axis=0)


def exchange(blocks):
    return lax.all_to_all(blocks, "expert", split_axis=0, concat_axis=0, tiled=True)


def gather_rows(rows):
    groups = lax.axis_size("expert")
    blocks = exchange(jnp.broadcast_to(rows[None], (groups,) + rows.shape))
    return blocks.reshape((groups * rows.shape[0],) + rows.shape[1:])


def sum_rows(partial_rows):
    groups = lax.axis_size("expert")
    blocks = partial_rows.reshape((groups, -1) + partial_rows.shape[1:])
    return jnp.sum(exchange(blocks).astype(jnp.float32), axis=0)


def same_core():
    members = range(lax.axis_size("dp"))
    return [[i for i in members if i % 2 == core] for core in range(2)]


def swap_cores(values):
    return lax.ppermute(values, "dp", [(i, i ^ 1) for i in range(lax.axis_size("dp"))])


def exchange_chips(blocks):
    return lax.all_to_all(
        blocks, "dp", split_axis=0, concat_axis=0, axis_index_groups=same_core(), tiled=True
    )


def gather_chips(shard):
    chips = lax.axis_size("dp") // 2
    return exchange_chips(jnp.broadcast_to(shard[None], (chips,) + shard.shape))


def gather_groups(chip_rows):
    groups = lax.axis_size("expert")
    return exchange(jnp.broadcast_to(chip_rows[None], (groups,) + chip_rows.shape))


def join_cores(own):
    width = own.shape[-1]
    other = swap_cores(own)
    first = lax.axis_index("dp") % 2 == 0
    both = jnp.stack([jnp.where(first, own, other), jnp.where(first, other, own)])
    return both.transpose(2, 0, 1, 3, 4).reshape(-1, width)


def core_major(columns):
    chips = lax.axis_size("dp") // 2
    groups = lax.axis_size("expert")
    split = columns.reshape(columns.shape[0], chips, 2, groups, -1)
    halves = split.transpose(2, 0, 3, 1, 4).reshape(2, columns.shape[0], -1)
    core = lax.axis_index("dp") % 2
    mine = lax.dynamic_index_in_dim(halves, core, 0, keepdims=False)
    theirs = lax.dynamic_index_in_dim(halves, 1 - core, 0, keepdims=False)
    return jnp.concatenate([mine, swap_cores(theirs)], axis=0)


def both_cores(rows):
    return jnp.concatenate([rows, swap_cores(rows)], axis=0)


def halve(partial, axis_name, step, outer):
    size = lax.axis_size(axis_name)
    width = partial.shape[-1]
    blocks = partial.reshape(outer, 2, -1, width)
    side = (lax.axis_index(axis_name) // step) % 2
    mine = lax.dynamic_index_in_dim(blocks, side, 1, keepdims=False)
    theirs = lax.dynamic_index_in_dim(blocks, 1 - side, 1, keepdims=False)
    arrived = lax.ppermute(
        theirs.reshape(-1, width), axis_name, [(i, i ^ step) for i in range(size)]
    )
    total = mine.reshape(-1, width).astype(jnp.float32) + arrived.astype(jnp.float32)
    return total.astype(jnp.bfloat16)


def near_first(axis_name, least):
    size = lax.axis_size(axis_name)
    steps = [least]
    while 2 * steps[-1] < size:
        steps.append(2 * steps[-1])
    return [(axis_name, step, size // (2 * step)) for step in steps]


def far_first(axis_name, least):
    return [(axis_name, step, 1) for _, step, _ in reversed(near_first(axis_name, least))]


def halve_all(partial, steps):
    for step in steps:
        partial = halve(partial, *step)
    return partial


def dot_f32(left, right, left_dims, right_dims):
    return lax.dot_general(
        left, right, ((left_dims, right_dims), ((), ())), preferred_element_type=jnp.float32
    )


def contract(left, right, left_dim, right_dim):
    return lax.dot_general(
        left,
        right,
        (((left_dim,), (right_dim,)), ((), ())),
        preferred_element_type=jnp.float32,
    )


def pick_column(table, column):
    lanes = lax.broadcasted_iota(jnp.int32, table.shape, 1)
    return jnp.sum(jnp.where(lanes == column, table, 0.0), axis=1, keepdims=True)


def expert_forward_kernel(rows_ref, gate_ref, up_ref, share_ref, gate_out, up_out, act_out):
    rows = rows_ref[...]
    gate_val = contract(rows, gate_ref[...], 1, 0)
    up_val = contract(rows, up_ref[...], 1, 0)
    share = pick_column(share_ref[...], pl.program_id(0))
    gate_out[...] = gate_val.astype(jnp.bfloat16)
    up_out[...] = up_val.astype(jnp.bfloat16)
    act_out[...] = (gate_val * jax.nn.sigmoid(gate_val) * up_val * share).astype(jnp.bfloat16)


def expert_forward(rows, gate_up, share):
    row_total, width = rows.shape
    experts = share.shape[1]
    hidden_total = gate_up.shape[1] // 2
    hidden = hidden_total // experts
    tile = row_total // 2
    row_block = pl.BlockSpec((tile, width), lambda e, r: (r, 0))
    weight_block = pl.BlockSpec((width, hidden), lambda e, r: (0, e))
    hidden_block = pl.BlockSpec((tile, hidden), lambda e, r: (r, e))
    return pl.pallas_call(
        expert_forward_kernel,
        grid=(experts, 2),
        in_specs=[
            row_block,
            weight_block,
            pl.BlockSpec((width, hidden), lambda e, r: (0, experts + e)),
            pl.BlockSpec((tile, experts), lambda e, r: (r, 0)),
        ],
        out_specs=[hidden_block] * 3,
        out_shape=[jax.ShapeDtypeStruct((row_total, hidden_total), jnp.bfloat16)] * 3,
        cost_estimate=pl.CostEstimate(
            flops=4 * row_total * width * hidden_total,
            transcendentals=row_total * hidden_total,
            bytes_accessed=4 * width * hidden_total + 6 * row_total * hidden_total,
        ),
    )(rows, gate_up, gate_up, share)


def expert_backward_kernel(
    group_ref,
    grad_ref,
    down_ref,
    gate_ref,
    up_ref,
    gate_val_ref,
    up_val_ref,
    share_ref,
    grad_gate_out,
    grad_up_out,
    rows_out,
    rows_acc,
    sums_acc,
):
    expert = pl.program_id(0)
    tile, width = grad_ref.shape
    experts = pl.num_programs(0)
    window = pl.ds(pl.multiple_of(pl.program_id(1) * tile, tile), tile)
    grad_scaled = contract(grad_ref[...], down_ref[...], 1, 0)
    gate_val = gate_val_ref[...].astype(jnp.float32)
    up_val = up_val_ref[...].astype(jnp.float32)
    sigmoid_val = jax.nn.sigmoid(gate_val)
    silu_val = gate_val * sigmoid_val
    grad_sum = jnp.sum(grad_scaled * silu_val * up_val, axis=1, keepdims=True)
    grad_inner = grad_scaled * pick_column(share_ref[...], expert)
    grad_gate = (
        grad_inner * up_val * sigmoid_val * (1.0 + gate_val * (1.0 - sigmoid_val))
    ).astype(jnp.bfloat16)
    grad_up = (grad_inner * silu_val).astype(jnp.bfloat16)
    grad_gate_out[...] = grad_gate
    grad_up_out[...] = grad_up
    grad_rows = contract(grad_gate, gate_ref[...], 1, 1) + contract(
        grad_up, up_ref[...], 1, 1
    )
    lanes = lax.broadcasted_iota(jnp.int32, (tile, sums_acc.shape[1]), 1)
    sum_high = grad_sum.astype(jnp.bfloat16).astype(jnp.float32)
    column = group_ref[0] * experts + expert
    grad_sums = jnp.where(lanes == column, sum_high, 0.0) + jnp.where(
        lanes == column + group_ref[1], grad_sum - sum_high, 0.0
    )

    @pl.when(expert == 0)
    def _():
        rows_acc[window, :] = grad_rows
        sums_acc[window, :] = grad_sums

    @pl.when(expert > 0)
    def _():
        rows_acc[window, :] += grad_rows
        sums_acc[window, :] += grad_sums

    @pl.when(expert == pl.num_programs(0) - 1)
    def _():
        rows_out[:, :width] = rows_acc[window, :].astype(jnp.bfloat16)
        rows_out[:, width:] = sums_acc[window, :].astype(jnp.bfloat16)


def expert_backward(group, grad, down, gate_up, gate_val, up_val, share, extra):
    row_total, width = grad.shape
    experts = share.shape[1]
    hidden_total = gate_up.shape[1] // 2
    hidden = hidden_total // experts
    tile = row_total // 2
    row_block = pl.BlockSpec((tile, width), lambda e, r, g: (r, 0))
    weight_block = pl.BlockSpec((width, hidden), lambda e, r, g: (0, e))
    hidden_block = pl.BlockSpec((tile, hidden), lambda e, r, g: (r, e))
    hidden_shape = jax.ShapeDtypeStruct((row_total, hidden_total), jnp.bfloat16)
    return pl.pallas_call(
        expert_backward_kernel,
        grid_spec=pltpu.PrefetchScalarGridSpec(
            num_scalar_prefetch=1,
            grid=(experts, 2),
            in_specs=[
                row_block,
                weight_block,
                weight_block,
                pl.BlockSpec((width, hidden), lambda e, r, g: (0, experts + e)),
                hidden_block,
                hidden_block,
                pl.BlockSpec((tile, experts), lambda e, r, g: (r, 0)),
            ],
            out_specs=[
                hidden_block,
                hidden_block,
                pl.BlockSpec(
                    (tile, width + extra),
                    lambda e, r, g: (jnp.where(e == experts - 1, r, 0), 0),
                ),
            ],
            scratch_shapes=[
                pltpu.VMEM((row_total, width), jnp.float32),
                pltpu.VMEM((row_total, extra), jnp.float32),
            ],
        ),
        out_shape=[
            hidden_shape,
            hidden_shape,
            jax.ShapeDtypeStruct((row_total, width + extra), jnp.bfloat16),
        ],
        cost_estimate=pl.CostEstimate(
            flops=6 * row_total * width * hidden_total,
            transcendentals=row_total * hidden_total,
            bytes_accessed=6 * width * hidden_total + 8 * row_total * hidden_total,
        ),
    )(group, grad, down, gate_up, gate_up, gate_val, up_val, share)


def attention_probs(block_ref, query, key):
    scores = contract(key, query, 1, 1) * HEAD_SIZE ** (-0.5)
    key_at = lax.broadcasted_iota(jnp.int32, scores.shape, 0)
    query_at = lax.broadcasted_iota(jnp.int32, scores.shape, 1)
    offset = block_ref[0] * query.shape[0]
    masked = jnp.where(key_at <= query_at + offset, scores, -1e30)
    exp_scores = jnp.exp(masked - jnp.max(masked, axis=0, keepdims=True))
    return exp_scores / jnp.sum(exp_scores, axis=0, keepdims=True)


def head(values, index):
    return values[:, index * HEAD_SIZE : (index + 1) * HEAD_SIZE]


def attention_forward_kernel(block_ref, query_ref, key_ref, value_ref, out_ref):
    query, key, value = query_ref[...], key_ref[...], value_ref[...]
    group = QUERY_HEADS // KEY_VALUE_HEADS
    outs = []
    for index in range(2 * group):
        shared = index // group
        probs = attention_probs(block_ref, head(query, index), head(key, shared))
        outs.append(contract(head(value, shared), probs.astype(jnp.bfloat16), 0, 0))
    out_ref[...] = jnp.concatenate(outs, axis=0).T.astype(jnp.bfloat16)


def attention_specs(tokens, keys):
    pairs = KEY_VALUE_HEADS // 2
    query_block = pl.BlockSpec((tokens, QUERY_HEADS // pairs * HEAD_SIZE), lambda i, b: (0, i))
    key_block = pl.BlockSpec((keys, 2 * HEAD_SIZE), lambda i, b: (0, i))
    value_block = pl.BlockSpec((keys, 2 * HEAD_SIZE), lambda i, b: (0, i + pairs))
    return (pairs, query_block, key_block, value_block)


def attention_forward(block, query, key_value):
    tokens, width = query.shape
    keys = key_value.shape[0]
    pairs, query_block, key_block, value_block = attention_specs(tokens, keys)
    return pl.pallas_call(
        attention_forward_kernel,
        grid_spec=pltpu.PrefetchScalarGridSpec(
            num_scalar_prefetch=1,
            grid=(pairs,),
            in_specs=[query_block, key_block, value_block],
            out_specs=query_block,
        ),
        out_shape=jax.ShapeDtypeStruct((tokens, width), jnp.bfloat16),
        cost_estimate=pl.CostEstimate(
            flops=16 * tokens * width * keys,
            transcendentals=QUERY_HEADS * tokens * keys,
            bytes_accessed=4 * tokens * width + 2 * key_value.size,
        ),
    )(block, query, key_value, key_value)


def attention_backward_kernel(
    block_ref, query_ref, grad_ref, key_ref, value_ref, grad_query_out, grad_key_value_out
):
    query, grad, key, value = query_ref[...], grad_ref[...], key_ref[...], value_ref[...]
    group = QUERY_HEADS // KEY_VALUE_HEADS
    scale = HEAD_SIZE ** (-0.5)
    grad_queries, grad_keys, grad_values = [], [], []
    for shared in range(2):
        grad_key, grad_value = 0.0, 0.0
        for index in range(shared * group, (shared + 1) * group):
            query_one, grad_one = head(query, index), head(grad, index)
            probs = attention_probs(block_ref, query_one, head(key, shared))
            grad_probs = contract(head(value, shared), grad_one, 1, 1)
            centre = jnp.sum(probs * grad_probs, axis=0, keepdims=True)
            grad_scores = (probs * (grad_probs - centre)).astype(jnp.bfloat16)
            grad_queries.append(contract(head(key, shared), grad_scores, 0, 0) * scale)
            grad_key += contract(grad_scores, query_one, 1, 0)
            grad_value += contract(probs.astype(jnp.bfloat16), grad_one, 1, 0)
        grad_keys.append(grad_key * scale)
        grad_values.append(grad_value)
    grad_query_out[...] = jnp.concatenate(grad_queries, axis=0).T
    grad_key_value_out[...] = jnp.concatenate(grad_keys + grad_values, axis=1).astype(
        jnp.bfloat16
    )


def attention_backward(block, query, grad, key_value):
    tokens, width = query.shape
    keys = key_value.shape[0]
    pairs, query_block, key_block, value_block = attention_specs(tokens, keys)
    return pl.pallas_call(
        attention_backward_kernel,
        grid_spec=pltpu.PrefetchScalarGridSpec(
            num_scalar_prefetch=1,
            grid=(pairs,),
            in_specs=[query_block, query_block, key_block, value_block],
            out_specs=[
                query_block,
                pl.BlockSpec((keys, 4 * HEAD_SIZE), lambda i, b: (0, i)),
            ],
        ),
        out_shape=[
            jax.ShapeDtypeStruct((tokens, width), jnp.float32),
            jax.ShapeDtypeStruct(key_value.shape, jnp.bfloat16),
        ],
        cost_estimate=pl.CostEstimate(
            flops=40 * tokens * width * keys,
            transcendentals=QUERY_HEADS * tokens * keys,
            bytes_accessed=8 * tokens * width + 4 * key_value.size,
        ),
    )(block, query, grad, key_value, key_value)


def place_kernel(part_ref, held_ref, out_ref):
    del held_ref
    out_ref[0, 0] = part_ref[...].astype(jnp.float32)


def place_first_kernel(part_ref, out_ref):
    out_ref[0, 0] = part_ref[...].astype(jnp.float32)


def place(part, held, layer, experts):
    rows = part.shape[0]
    block = (rows, part.shape[1] // experts)
    in_specs = [pl.BlockSpec(block, lambda e: (0, e))]
    operands = [part]
    if held is not None:
        in_specs.append(pl.BlockSpec(memory_space=pl.ANY))
        operands.append(held)
    return pl.pallas_call(
        place_first_kernel if held is None else place_kernel,
        grid=(experts,),
        in_specs=in_specs,
        out_specs=pl.BlockSpec((1, 1) + block, lambda e: (layer, e, 0, 0)),
        out_shape=jax.ShapeDtypeStruct((LAYER_COUNT, experts) + block, jnp.float32),
        input_output_aliases={} if held is None else {1: 0},
    )(*operands)


def body(
    inputs,
    routes,
    cotangent,
    query_weight,
    key_projection_weight,
    value_projection_weight,
    output_weight,
    attention_gain,
    expert_gain,
    router_weight,
    gate_weight,
    up_weight,
    down_weight,
):
    sequences_per_device, block_length, model_width = inputs.shape
    token_total = sequences_per_device * block_length
    exp_dev = gate_weight.shape[1]
    groups = lax.axis_size("expert")
    expert_total = exp_dev * groups
    all_rows = token_total * groups
    query_width = query_weight.shape[2]
    key_width = key_projection_weight.shape[2]
    my_group = lax.axis_index("expert")
    positions = my_group * block_length + jnp.arange(block_length, dtype=jnp.int32)
    cosine_table, sine_table = rotary_tables(positions, HEAD_SIZE // 2)
    block_at = my_group.astype(jnp.int32).reshape(1)
    group_at = jnp.stack([my_group.astype(jnp.int32), jnp.int32(expert_total)])
    expert_ids = jnp.arange(expert_total, dtype=jnp.int32)
    small_width = -(-(expert_total + 2) // 128) * 128
    gate_width = -(-(2 * expert_total) // 128) * 128
    edges = (
        query_width,
        query_width + key_width,
        query_width + 2 * key_width,
        query_width + 2 * key_width + model_width,
        query_width + 2 * key_width + model_width + expert_total,
        query_width + 2 * key_width + model_width + expert_total + 1,
    )

    def pack_attention(query_part, key_part, value_part, output_part, router_part, one, two):
        rows = query_part.shape[0]
        fill = jnp.zeros((rows, small_width - expert_total - 2), query_part.dtype)
        return jnp.concatenate(
            [
                query_part,
                key_part,
                value_part,
                output_part,
                router_part,
                one[:, None],
                two[:, None],
                fill,
            ],
            axis=1,
        )

    chosen_hot = jnp.any(
        routes.reshape(LAYER_COUNT, token_total, -1)[:, :, :, None] == expert_ids, axis=2
    )
    chosen_all = gather_rows(
        jnp.moveaxis(chosen_hot, 0, 1).reshape(token_total, -1).astype(jnp.bfloat16)
    ).reshape(all_rows, LAYER_COUNT, expert_total)

    shards = [
        pack_attention(
            query_weight[layer],
            key_projection_weight[layer],
            value_projection_weight[layer],
            output_weight[layer].T,
            router_weight[layer],
            attention_gain[layer],
            expert_gain[layer],
        )
        for layer in range(LAYER_COUNT)
    ]
    packed = [lax.all_gather(shards[0], ("dp", "expert"), axis=0, tiled=True)]
    chip_rows = [None] + [gather_chips(shard) for shard in shards[1:]]
    inputs, chip_rows = lax.optimization_barrier((inputs, chip_rows))
    ff_width = gate_weight.shape[3]
    hidden_width = exp_dev * ff_width
    def gather_weights(*weights):
        rows = [weight.reshape(weight.shape[0], hidden_width) for weight in weights]
        return lax.all_gather(jnp.concatenate(rows, axis=1), "dp", axis=0, tiled=True)

    gathered = [
        (
            gather_weights(
                gate_weight[layer].transpose(1, 0, 2), up_weight[layer].transpose(1, 0, 2)
            ),
            gather_weights(down_weight[layer].transpose(2, 0, 1)),
        )
        for layer in range(LAYER_COUNT)
    ]

    def shares_of(rows, router_full, hot):
        logits = jnp.dot(rows, router_full, preferred_element_type=jnp.float32)
        masked = jnp.where(hot, logits, -1e30)
        exps = jnp.where(hot, jnp.exp(masked - jnp.max(masked, axis=1, keepdims=True)), 0.0)
        return exps / jnp.sum(exps, axis=1, keepdims=True)

    def expert_rows(act, down):
        return dot_f32(act, down, (1,), (1,)).astype(jnp.bfloat16)

    def layer_forward(hidden, layer):
        full = packed[layer]
        qkv_full = full[:, : edges[2]]
        output_full = full[:, edges[2] : edges[3]]
        router_full = full[:, edges[3] : edges[4]]
        gain_one = full[:, edges[4]].astype(jnp.float32)
        gain_two = full[:, edges[5]].astype(jnp.float32)
        gate_up_full, down_full = gathered[layer]
        first_normalized, inv_one = norm_forward(hidden, gain_one)
        first_normalized = first_normalized.astype(jnp.bfloat16)
        linear = jnp.dot(first_normalized, qkv_full, preferred_element_type=jnp.float32)
        query_rotated = rotate_features(
            linear[:, : edges[0]].reshape(token_total, QUERY_HEADS, HEAD_SIZE),
            cosine_table,
            sine_table,
        ).astype(jnp.bfloat16)
        query_rotated = query_rotated.reshape(token_total, query_width)
        key_rot = rotate_features(
            linear[:, edges[0] : edges[1]].reshape(token_total, KEY_VALUE_HEADS, HEAD_SIZE),
            cosine_table,
            sine_table,
        ).astype(jnp.bfloat16)
        key_value = jnp.concatenate(
            [
                key_rot.reshape(token_total, key_width),
                linear[:, edges[1] :].astype(jnp.bfloat16),
            ],
            axis=1,
        )
        key_value_all = gather_rows(key_value)
        ahead = layer + 1 < LAYER_COUNT
        attended = attention_forward(block_at, query_rotated, key_value_all)
        middle = hidden + dot_f32(attended, output_full, (1,), (1,))
        normed_two, inv_two = norm_forward(middle, gain_two)
        normed_two = normed_two.astype(jnp.bfloat16)
        arrived = gather_rows(normed_two)
        if ahead:
            arrived, next_rows = lax.optimization_barrier((arrived, chip_rows[layer + 1]))
            next_rows = gather_groups(next_rows)
        share_all = shares_of(arrived, router_full, chosen_all[:, layer] > 0)
        share_own = shares_of(normed_two, router_full, chosen_hot[layer])
        share_local = lax.dynamic_slice_in_dim(share_all, my_group * exp_dev, exp_dev, axis=1)
        gate_low, up_low, scaled_act = expert_forward(
            arrived, gate_up_full, share_local
        )
        if ahead:
            scaled_act, next_rows = lax.optimization_barrier((scaled_act, next_rows))
            packed.append(join_cores(next_rows))
        kept_state = (
            hidden,
            inv_one,
            first_normalized,
            query_rotated,
            key_value_all,
            attended,
            middle,
            inv_two,
            normed_two,
            share_own,
            share_local,
            arrived,
            gate_low,
            up_low,
            scaled_act,
            qkv_full,
            output_full,
            gain_one,
            gain_two,
            router_full,
            gate_up_full,
            down_full,
        )
        return kept_state

    hidden = inputs.astype(jnp.float32).reshape(token_total, model_width)
    kept_states = []
    for layer in range(LAYER_COUNT):
        kept_state = layer_forward(hidden, layer)
        kept_states.append(kept_state)
        last_middle, last_act, last_down = kept_state[6], kept_state[14], kept_state[-1]
        if layer + 1 < LAYER_COUNT:
            hidden = last_middle + sum_rows(expert_rows(last_act, last_down))
    output = None
    grad_hidden = cotangent.astype(jnp.float32).reshape(token_total, model_width)
    attention_list = [None] * LAYER_COUNT
    waiting = None
    group_steps = near_first("expert", 1)
    far_steps = far_first("expert", 1)
    chip_steps = near_first("dp", 2)
    for layer in range(LAYER_COUNT - 1, -1, -1):
        (
            layer_hidden,
            inv_one,
            first_normalized,
            query_rotated,
            key_value_all,
            attended,
            middle,
            inv_two,
            normed_two,
            share_own,
            share_local,
            arrived,
            gate_low,
            up_low,
            scaled_act,
            qkv_full,
            output_full,
            gain_one,
            gain_two,
            router_full,
            gate_up_full,
            down_full,
        ) = kept_states[layer]
        grad_all = gather_rows(grad_hidden.astype(jnp.bfloat16))
        if waiting is not None:
            grad_all, waiting = lax.optimization_barrier((grad_all, waiting))
            out_part, query_part, kv_part = waiting
            out_part = halve_all(out_part, group_steps[1:])
            query_part = halve_all(query_part, group_steps[:1])
            kv_part = halve_all(kv_part, group_steps[:1])
        grad_down = dot_f32(grad_all, scaled_act, (0,), (0,)).astype(jnp.bfloat16)
        grad_all, grad_down = lax.optimization_barrier((grad_all, grad_down))
        expert_parts = [lax.psum_scatter(grad_down, "dp", scatter_dimension=0, tiled=True)]
        grad_gate_val, grad_up_val, grad_rows = expert_backward(
            group_at,
            grad_all,
            down_full,
            gate_up_full,
            gate_low,
            up_low,
            share_local,
            gate_width,
        )
        grad_gate_w = dot_f32(arrived, grad_gate_val, (0,), (0,)).astype(jnp.bfloat16)
        grad_up_w = dot_f32(arrived, grad_up_val, (0,), (0,)).astype(jnp.bfloat16)
        back = sum_rows(grad_rows)
        if waiting is None:
            last_rows = expert_rows(last_act, last_down)
            back, last_rows = lax.optimization_barrier((back, last_rows))
            output = last_middle + sum_rows(last_rows)
        else:
            back, out_part, query_part, kv_part = lax.optimization_barrier(
                (back, out_part, query_part, kv_part)
            )
            late_part = jnp.concatenate([query_part, kv_part], axis=1)
            late_part = halve_all(late_part, group_steps[1:])
        back, grad_gate_w, grad_up_w = lax.optimization_barrier((back, grad_gate_w, grad_up_w))
        expert_parts += [
            lax.psum_scatter(grad_gate_w, "dp", scatter_dimension=0, tiled=True),
            lax.psum_scatter(grad_up_w, "dp", scatter_dimension=0, tiled=True),
        ]
        grad_gates_own = (
            back[:, model_width : model_width + expert_total]
            + back[:, model_width + expert_total : model_width + 2 * expert_total]
        )
        grad_logits = (
            share_own
            * (grad_gates_own - jnp.sum(share_own * grad_gates_own, axis=-1, keepdims=True))
        ).astype(jnp.bfloat16)
        grad_router = dot_f32(normed_two, grad_logits, (0,), (0,))
        grad_normed_two = back[:, :model_width] + dot_f32(grad_logits, router_full, (1,), (1,))
        grad_norm_mid, grad_gain_two = norm_backward(middle, inv_two, gain_two, grad_normed_two)
        grad_middle = grad_hidden + grad_norm_mid
        grad_branch = grad_middle.astype(jnp.bfloat16)
        grad_output_w = dot_f32(core_major(grad_branch), both_cores(attended), (0,), (0,))
        grad_output_w = halve_all(grad_output_w.astype(jnp.bfloat16), group_steps[:1])
        grad_attended = dot_f32(grad_branch, output_full, (1,), (0,)).astype(jnp.bfloat16)
        if waiting is not None:
            grad_attended, late_part = lax.optimization_barrier((grad_attended, late_part))
            chip_part = jnp.concatenate([out_part, late_part], axis=1)
            chip_part = halve_all(chip_part, chip_steps[:1])
        grad_query, grad_key_value_all = attention_backward(
            block_at, query_rotated, grad_attended, key_value_all
        )
        if waiting is None:
            grad_query, grad_key_value_all, output = lax.optimization_barrier(
                (grad_query, grad_key_value_all, output)
            )
        else:
            grad_query, grad_output_w, chip_part = lax.optimization_barrier(
                (grad_query, grad_output_w, chip_part)
            )
            grad_output_w = halve_all(grad_output_w, group_steps[1:])
            chip_part = halve_all(chip_part, chip_steps[1:])
        grad_kv = sum_rows(grad_key_value_all)
        normed_split = core_major(first_normalized)
        grad_query_lin = (
            rotate_features(
                grad_query.reshape(token_total, QUERY_HEADS, HEAD_SIZE), cosine_table, -sine_table
            )
            .astype(jnp.bfloat16)
            .reshape(token_total, query_width)
        )
        grad_query_w = dot_f32(normed_split, both_cores(grad_query_lin), (0,), (0,))
        grad_query_w = grad_query_w.astype(jnp.bfloat16)
        if layer == 0:
            grad_kv, grad_query_w = lax.optimization_barrier((grad_kv, grad_query_w))
            grad_query_w = halve_all(grad_query_w, far_steps[:1])
        grad_kv = grad_kv.reshape(token_total, -1, 2, 2 * HEAD_SIZE)
        grad_kv = grad_kv.transpose(0, 2, 1, 3).reshape(token_total, 2 * key_width)
        grad_key_lin = (
            rotate_features(
                grad_kv[:, :key_width].reshape(token_total, KEY_VALUE_HEADS, HEAD_SIZE),
                cosine_table,
                -sine_table,
            )
            .astype(jnp.bfloat16)
            .reshape(token_total, key_width)
        )
        grad_kv_lin = jnp.concatenate(
            [grad_key_lin, grad_kv[:, key_width:].astype(jnp.bfloat16)], axis=1
        )
        grad_kv_w = dot_f32(normed_split, both_cores(grad_kv_lin), (0,), (0,))
        grad_normed_one = dot_f32(grad_query_lin, qkv_full[:, : edges[0]], (1,), (1,)) + dot_f32(
            grad_kv_lin, qkv_full[:, edges[0] :], (1,), (1,)
        )
        grad_norm_in, grad_gain_one = norm_backward(
            layer_hidden, inv_one, gain_one, grad_normed_one
        )
        fill = jnp.zeros((model_width, small_width - expert_total - 2), jnp.bfloat16)
        small_part = jnp.concatenate(
            [
                grad_router.astype(jnp.bfloat16),
                grad_gain_one[:, None].astype(jnp.bfloat16),
                grad_gain_two[:, None].astype(jnp.bfloat16),
                fill,
            ],
            axis=1,
        )
        small_split = core_major(small_part.T).reshape(2, small_width, -1)
        small_half = jnp.sum(small_split.astype(jnp.float32), axis=0).T
        grad_kv_w = jnp.concatenate([grad_kv_w, small_half], axis=1).astype(jnp.bfloat16)
        if layer > 0:
            waiting = (grad_output_w, grad_query_w, grad_kv_w)
        else:
            grad_kv_w, last_parts = lax.optimization_barrier((grad_kv_w, last_parts))
            expert_held = [place(part, None, layer + 1, exp_dev) for part in last_parts]
            grad_kv_w = halve_all(grad_kv_w, group_steps[:1])
            grad_kv_w, expert_held, chip_part = lax.optimization_barrier(
                (grad_kv_w, expert_held, chip_part)
            )
            attention_list[layer + 1] = (chip_part[:, :query_width], chip_part[:, query_width:])
            late_part = jnp.concatenate(
                [
                    halve_all(grad_query_w, far_steps[1:]),
                    halve_all(grad_kv_w, group_steps[1:]),
                ],
                axis=1,
            )
            late_part = halve_all(late_part, chip_steps[:1])
            expert_held = [
                place(part, held, layer, exp_dev)
                for part, held in zip(expert_parts[:2], expert_held[:2])
            ] + expert_held[2:]
            late_part, expert_held = lax.optimization_barrier((late_part, expert_held))
            attention_list[layer] = (
                halve_all(grad_output_w, chip_steps),
                halve_all(late_part, chip_steps[1:]),
            )
        last_parts = expert_parts
        grad_hidden = grad_middle + grad_norm_in
    output_grads = jnp.stack([parts[0] for parts in attention_list]).astype(jnp.float32)
    cuts = [query_width, key_width, key_width, expert_total, 1, 1]
    cuts = [sum(cuts[:index]) for index in range(len(cuts) + 1)]
    query_grads, key_grads, value_grads, router_grads, one, two = (
        jnp.stack([parts[1][:, start:stop] for parts in attention_list]).astype(jnp.float32)
        for start, stop in zip(cuts[:-1], cuts[1:])
    )
    expert_held[2] = place(last_parts[2], expert_held[2], 0, exp_dev)
    down_grads, gate_grads, up_grads = expert_held
    return (
        output.astype(jnp.bfloat16).reshape(sequences_per_device, block_length, model_width),
        grad_hidden.reshape(sequences_per_device, block_length, model_width),
        query_grads,
        key_grads,
        value_grads,
        jnp.swapaxes(output_grads, 1, 2),
        one[:, :, 0],
        two[:, :, 0],
        router_grads,
        gate_grads,
        up_grads,
        jnp.swapaxes(down_grads, 2, 3),
    )


def solution(mesh):
    in_specs = (
        P("dp", "expert", None),
        P(None, "expert", "dp", None, None),
        P("dp", "expert", None),
        P(None, ("dp", "expert"), None),
        P(None, ("dp", "expert"), None),
        P(None, ("dp", "expert"), None),
        P(None, None, ("dp", "expert")),
        P(None, ("dp", "expert")),
        P(None, ("dp", "expert")),
        P(None, ("dp", "expert"), None),
        P(None, "expert", "dp", None),
        P(None, "expert", "dp", None),
        P(None, "expert", None, "dp"),
    )
    out_specs = (
        P("dp", "expert", None),
        P("dp", "expert", None),
        P(None, ("dp", "expert"), None),
        P(None, ("dp", "expert"), None),
        P(None, ("dp", "expert"), None),
        P(None, None, ("dp", "expert")),
        P(None, ("dp", "expert")),
        P(None, ("dp", "expert")),
        P(None, ("dp", "expert"), None),
        P(None, "expert", "dp", None),
        P(None, "expert", "dp", None),
        P(None, "expert", None, "dp"),
    )
    return jax.shard_map(body, mesh=mesh, in_specs=in_specs, out_specs=out_specs, check_vma=False)
```
